256 devices in a mesh: pole: 8 (over x, core), rows: 32 (over z, y).
Axes of the slice: x: 4, y: 4, z: 8, core: 2. Of those that a mesh axis runs over, the one named last changes fastest.
Arguments:
- subspace: float32 [2, 256, 16384], P(None, None, 'rows'), may hold values from -6 to 6
- pivots: float32 [8, 64, 2, 256, 256], P('pole', 'rows'), may hold values from -0.25 to 0.25
- lower_blocks: float32 [8, 64, 2, 256, 256], P('pole', 'rows'), may hold values from -1 to 1
- upper_blocks: float32 [8, 64, 2, 256, 256], P('pole', 'rows'), may hold values from -1 to 1
- pole_weights: float32 [8, 2], P('pole'), may hold values from -4 to 4
Outputs:
- rotated_basis: float32 [2, 256, 16384], P(None, 'pole', 'rows')
The draws below stay inside these ranges and needn't reach their ends.
All inputs are finite; a program needn't handle non-finite values.
Results may differ from the reference program's by a relative error of at most 0.00018.
Values sent between devices are 32-bit elements; how exact they have to be, the bound alone decides.
A program may use at most 128 MiB of HBM per device.

```python
import jax
import jax.numpy as jnp
from jax import lax

B = 256
M = 256
NS_ITERS = 2
CONTOUR_POLES = 8
BLOCK_ROWS = 64
N = 16384


def decaying(key):
    shape = (CONTOUR_POLES, BLOCK_ROWS, 2, B, B)
    decay_rate = 0.3 ** (1.0 / BLOCK_ROWS)
    spike_key, value_seed_key = jax.random.split(key)
    spike_events = jax.random.bernoulli(spike_key, 0.05, (CONTOUR_POLES, BLOCK_ROWS, 1, 1, 1))
    scale_factor = decay_rate * jnp.where(spike_events, 0.6, 1.0)
    values = jax.random.normal(value_seed_key, shape, jnp.float32)
    values = jnp.clip(values, -6.0, 6.0)
    return (values * scale_factor * (2.0 * B) ** (-0.5)).astype(jnp.float32)


def draw_lower_blocks(key, part):
    return decaying(jax.random.fold_in(key, 11))


def draw_upper_blocks(key, part):
    return decaying(jax.random.fold_in(key, 23))


def block_levels(key, extent, cuts, low, largest):
    gain, own = 1.0, jax.random.fold_in(key, 6)
    for position, parts in cuts:
        steps = jnp.exp(jax.random.uniform(jax.random.fold_in(own, position), (parts,), jnp.float32, low / len(cuts), largest / len(cuts)))
        gain = gain * jnp.repeat(steps, extent[position] // parts).reshape([-1 if axis == position else 1 for axis in range(len(extent))])
    return gain


def centred(key, extent, spread, limit, cuts=(), kind=jnp.bfloat16):
    array = spread * jax.random.normal(key, extent, jnp.float32)
    if cuts:
        array = array * block_levels(key, extent, cuts, -0.22, 0.18)
    return jnp.clip(array, -limit, limit).astype(kind)


def setup_inputs(seed: int = 0) -> dict:
    key_of = jax.random.split(jax.random.key(seed), 6)
    subspace = centred(key_of[0], (2, M, N), 1, 6.0, ((2, 32),), jnp.float32)
    pivots = centred(key_of[1], (CONTOUR_POLES, BLOCK_ROWS, 2, B, B), (2 * B) ** -0.5, 0.25, ((0, 8), (1, 32)), jnp.float32)
    lower_blocks = draw_lower_blocks(jax.random.fold_in(key_of[5], 71), 0)
    upper_blocks = draw_upper_blocks(jax.random.fold_in(key_of[5], 71), 0)
    pole_weights = centred(key_of[4], (CONTOUR_POLES, 2), 1, 4.0, ((0, 8),), jnp.float32)
    return dict(subspace=subspace, pivots=pivots, lower_blocks=lower_blocks, upper_blocks=upper_blocks, pole_weights=pole_weights)


HIGH = lax.Precision.HIGHEST

def real_dot(first, second, dims):
    return lax.dot_general(first, second, (dims, ((), ())), precision=HIGH, preferred_element_type=jnp.float32)

def times_trans(left, matrix):
    dims = ((1,), (1,))
    real = real_dot(left[0], matrix[0], dims) - real_dot(left[1], matrix[1], dims)
    imag = real_dot(left[0], matrix[1], dims) + real_dot(left[1], matrix[0], dims)
    return jnp.stack([real, imag])

def complex_dot(left, right):
    dims = ((1,), (0,))
    real = real_dot(left[0], right[0], dims) - real_dot(left[1], right[1], dims)
    imag = real_dot(left[0], right[1], dims) + real_dot(left[1], right[0], dims)
    return jnp.stack([real, imag])

def gram_matrix(basis):
    dims = ((1,), (1,))
    real = real_dot(basis[0], basis[0], dims) + real_dot(basis[1], basis[1], dims)
    imag = real_dot(basis[0], basis[1], dims) - real_dot(basis[1], basis[0], dims)
    return jnp.stack([real, imag])

def rotate(mixing, basis):
    dims = ((0,), (0,))
    real = real_dot(mixing[0], basis[0], dims) - real_dot(mixing[1], basis[1], dims)
    imag = real_dot(mixing[0], basis[1], dims) + real_dot(mixing[1], basis[0], dims)
    return jnp.stack([real, imag])

def newton_schulz(gram):
    size = gram.shape[1]
    unit = jnp.stack([jnp.eye(size, dtype=jnp.float32), jnp.zeros((size, size), jnp.float32)])
    frob = jnp.sqrt(jnp.sum(gram * gram))
    current = gram / frob
    inverse_root = unit
    for sweep in range(NS_ITERS):
        scale_factor = 1.5 * unit - 0.5 * complex_dot(inverse_root, current)
        current = complex_dot(current, scale_factor)
        inverse_root = complex_dot(scale_factor, inverse_root)
    return (inverse_root, frob)

def reference(subspace, pivots, lower_blocks, upper_blocks, pole_weights):
    pieces = jnp.transpose(subspace.reshape(2, M, BLOCK_ROWS, B), (2, 0, 1, 3))
    blank = jnp.zeros((2, M, B), jnp.float32)
    total = jnp.zeros((2, M, N), jnp.float32)
    for pole in range(CONTOUR_POLES):

        def forward(carry, inputs):
            pivot, lower, piece = inputs
            value = times_trans(piece, pivot) - times_trans(carry, lower)
            return (value, value)

        def backward(carry, inputs):
            value, upper = inputs
            result = value - times_trans(carry, upper)
            return (result, result)
        _, swept = lax.scan(forward, blank, (pivots[pole], lower_blocks[pole], pieces))
        _, solved = lax.scan(backward, blank, (swept, upper_blocks[pole]), reverse=True)
        solution = jnp.transpose(solved, (1, 2, 0, 3)).reshape(2, M, N)
        wreal = pole_weights[pole, 0]
        wimag = pole_weights[pole, 1]
        total = total + jnp.stack([wreal * solution[0] - wimag * solution[1], wreal * solution[1] + wimag * solution[0]])
    gram = gram_matrix(total)
    inverse_root, frob = newton_schulz(gram)
    return rotate(inverse_root, total) * jnp.sqrt(N / frob)
```

```python
import functools

import jax
import jax.numpy as jnp
from jax import lax
from jax.experimental import pallas as pl
from jax.experimental.pallas import tpu as pltpu
from jax.sharding import Mesh
from jax.sharding import PartitionSpec as P

F32 = jnp.float32
BF16 = jnp.bfloat16
MESH_ID = pl.DeviceIdType.MESH
AXES = ("x", "core", "z", "y")
SUBS = 4


def halves(value):
    high = value.astype(BF16)
    return high, (value - high.astype(F32)).astype(BF16)


def dot(left, right, trans):
    dims = (((1,), (1 if trans else 0,)), ((), ()))
    return lax.dot_general(left, right, dims, preferred_element_type=F32)


def times(rows, weights, trans):
    high, low = halves(rows)
    count = rows.shape[0]
    both = dot(jnp.concatenate([high, low], axis=0), weights[0], trans)
    return both[:count] + both[count:] + dot(high, weights[1], trans)


def prepare(weights, real, minus):
    size = real.shape[0]
    for part, (r, m) in enumerate(zip(halves(real), halves(minus))):
        weights[part, :size, :size] = r
        weights[part, :size, size:] = m
        weights[part, size:, :size] = -m
        weights[part, size:, size:] = r


def tiles(count, size, body):
    if count == size:
        body(0)
        return

    def step(i, carry):
        body(pl.multiple_of(i * size, size))
        return carry

    lax.fori_loop(0, count // size, step, 0)


def remote(src, dst, sems, slot_out, slot_in, device):
    return pltpu.make_async_remote_copy(
        src_ref=src,
        dst_ref=dst,
        send_sem=sems.at[0, slot_out],
        recv_sem=sems.at[1, slot_in],
        device_id=device,
        device_id_type=MESH_ID,
    )


def nearest_first(count):
    return sorted(range(1, count), key=lambda d: min(d, count - d))


def sweeps(
    dims, f_ref, g_ref, e_ref, u_ref, w_ref, out_ref,
    we0, we1, wf0, wf1, wg, wc, wd, wp, wq,
    c_all, d_all, b_all, e_all, qg, rg, s0, s1, y0, y1, eo, vin, win,
    vz, vo, wz, wo, vk, wk,
    sem_c, sem_b, sem_d, sem_v, sem_e, sem_w, sem_fz, sem_bz,
):
    ysize, zsize = dims
    y, z = lax.axis_index("y"), lax.axis_index("z")
    vectors, width = f_ref.shape[1], g_ref.shape[-1]
    chunk = vectors // ysize
    sub = chunk // SUBS
    tall = min(128, width)
    order = nearest_first(ysize)

    barrier = pltpu.get_barrier_semaphore()
    for d in order:
        pl.semaphore_signal(barrier, inc=1, device_id={"y": lax.rem(y + d, ysize)}, device_id_type=MESH_ID)
    for d in (1, zsize - 1):
        pl.semaphore_signal(barrier, inc=1, device_id={"z": lax.rem(z + d, zsize)}, device_id_type=MESH_ID)
    pl.semaphore_wait(barrier, ysize + 1)

    def piece(ref, j):
        return ref.at[pl.ds(pl.multiple_of(j * chunk, chunk), chunk), :]

    def to_all(store, sems):
        sent = []
        for d in order:
            copy = remote(store.at[y], store.at[y], sems, d, d, {"y": lax.rem(y + d, ysize)})
            copy.start()
            sent.append(copy)
        return sent

    def to_each(source, store, sems, d):
        peer = lax.rem(y + d, ysize)
        copy = remote(piece(source, peer), store, sems, d, d, {"y": peer})
        copy.start()
        return copy

    def arrived(store, sems, d):
        remote(store, store, sems, d, d, {"y": lax.rem(y + ysize - d, ysize)}).wait_recv()

    sent = []

    prepare(we0, e_ref[0, 0, 0], -e_ref[0, 0, 1])

    def forward_map(i):
        rows = jnp.concatenate([e_ref[0, 1, 0, pl.ds(i, tall), :], -e_ref[0, 1, 1, pl.ds(i, tall), :]], axis=1)
        c_all[y, pl.ds(i, tall), :] = times(rows, we0, False)

    tiles(width, tall, forward_map)
    sent += to_all(c_all, sem_c)

    prepare(wg.at[0], g_ref[0, 0, 0], -g_ref[0, 0, 1])
    prepare(wg.at[1], g_ref[0, 1, 0], -g_ref[0, 1, 1])
    prepare(we1, e_ref[0, 1, 0], -e_ref[0, 1, 1])

    def local(i):
        rows = pl.ds(i, tall)
        first = jnp.concatenate([f_ref[0, rows, :width], f_ref[1, rows, :width]], axis=1)
        second = jnp.concatenate([f_ref[0, rows, width:], f_ref[1, rows, width:]], axis=1)
        start = times(first, wg.at[0], True)
        s0[rows, :] = start
        s1[rows, :] = times(second, wg.at[1], True) - times(start, we1, True)

    tiles(vectors, tall, local)
    for d in order:
        sent.append(to_each(s1, b_all.at[y], sem_b, d))
    b_all[y] = piece(s1, y)[...]

    prepare(wf1, u_ref[0, 1, 0], -u_ref[0, 1, 1])

    def backward_map(i):
        rows = jnp.concatenate([u_ref[0, 0, 0, pl.ds(i, tall), :], -u_ref[0, 0, 1, pl.ds(i, tall), :]], axis=1)
        d_all[y, pl.ds(i, tall), :] = times(rows, wf1, False)

    tiles(width, tall, backward_map)
    sent += to_all(d_all, sem_d)
    prepare(wf0, u_ref[0, 0, 0], -u_ref[0, 0, 1])

    prepare(wc.at[y], c_all[y, :, :width], c_all[y, :, width:])
    for d in order:
        k = lax.rem(y + ysize - d, ysize)
        arrived(c_all.at[k], sem_c, d)
        prepare(wc.at[k], c_all[k, :, :width], c_all[k, :, width:])

    def group_forward(i):
        value = c_all[ysize - 1, pl.ds(i, tall), :]
        for k in reversed(range(ysize - 1)):
            value = times(value, wc.at[k], False)
        eo[pl.ds(i, tall), :] = value

    tiles(width, tall, group_forward)
    prepare(wp, eo[:width, :width], eo[:width, width:])
    for d in order:
        arrived(b_all.at[lax.rem(y + ysize - d, ysize)], sem_b, d)
    value = b_all[0]
    for k in range(1, ysize):
        value = times(value, wc.at[k], True) + b_all[k]
    qg[...] = value

    def group_backward():
        prepare(wd.at[y], d_all[y, :, :width], d_all[y, :, width:])
        for d in order:
            k = lax.rem(y + ysize - d, ysize)
            arrived(d_all.at[k], sem_d, d)
            prepare(wd.at[k], d_all[k, :, :width], d_all[k, :, width:])

        def compose(i):
            value = d_all[0, pl.ds(i, tall), :]
            for k in range(1, ysize):
                value = times(value, wd.at[k], False)
            win[pl.ds(i, tall), :] = value

        tiles(width, tall, compose)
        prepare(wq, win[:width, :width], win[:width, width:])

    late = z >= zsize // 2
    pl.when(late)(group_backward)

    @pl.when(z == 0)
    def _():
        vz[...] = jnp.zeros_like(vz)

    def hop(out, into, sems, s, device):
        return remote(out.at[pl.ds(s * sub, sub), :], into.at[pl.ds(s * sub, sub), :], sems, s, s, device)

    ahead, behind = {"z": lax.rem(z + 1, zsize)}, {"z": lax.rem(z + zsize - 1, zsize)}
    for s in range(SUBS):
        rows = pl.ds(s * sub, sub)

        @pl.when(z > 0)
        def _():
            hop(vz, vz, sem_fz, s, behind).wait_recv()

        @pl.when(z < zsize - 1)
        def _():
            vo[rows, :] = times(vz[rows, :], wp, True) + qg[rows, :]
            hop(vo, vz, sem_fz, s, ahead).start()

    def hand_out(k, value, staging, into, sems):
        staging[k] = value

        @pl.when(y == k)
        def _():
            piece(into, y)[...] = value

        @pl.when(y != k)
        def _():
            remote(staging.at[k], piece(into, y), sems, k, y, {"y": k}).start()

    def collect(into, sems, j):
        @pl.when(y != j)
        def _():
            remote(piece(into, j), piece(into, j), sems, j, j, {"y": j}).wait_recv()

    def handed_out(staging, into, sems):
        for k in range(ysize):
            @pl.when(y != k)
            def _():
                remote(staging.at[k], piece(into, y), sems, k, y, {"y": k}).wait_send()

    value = vz[...]
    for k in range(ysize):
        hand_out(k, value, vk, vin, sem_v)
        if k < ysize - 1:
            value = times(value, wc.at[k], True) + b_all[k]

    pl.when(jnp.logical_not(late))(group_backward)

    for j in range(ysize):
        collect(vin, sem_v, j)
        rows = pl.ds(j * chunk, chunk)
        value = vin[rows, :]
        first = s0[rows, :] - times(value, we0, True)
        second = s1[rows, :] + times(value, wc.at[y], True)
        y0[rows, :] = first
        y1[rows, :] = second
        ends = first - times(second, wf0, True)
        eo[rows, :] = ends

        @pl.when(y == j)
        def _():
            e_all[j] = ends

        @pl.when(y != j)
        def _():
            remote(eo.at[rows, :], e_all.at[y], sem_e, j, y, {"y": j}).start()

    for k in range(ysize):
        @pl.when(y != k)
        def _():
            remote(e_all.at[k], e_all.at[k], sem_e, k, k, {"y": k}).wait_recv()

    value = e_all[ysize - 1]
    for k in reversed(range(ysize - 1)):
        value = times(value, wd.at[k], True) + e_all[k]
    rg[...] = value

    @pl.when(z == zsize - 1)
    def _():
        wz[...] = jnp.zeros_like(wz)

    for s in range(SUBS):
        rows = pl.ds(s * sub, sub)

        @pl.when(z < zsize - 1)
        def _():
            hop(wz, wz, sem_bz, s, ahead).wait_recv()

        @pl.when(z > 0)
        def _():
            wo[rows, :] = times(wz[rows, :], wq, True) + rg[rows, :]
            hop(wo, wz, sem_bz, s, behind).start()

    value = wz[...]
    for k in reversed(range(ysize)):
        hand_out(k, value, wk, win, sem_w)
        if k > 0:
            value = times(value, wd.at[k], True) + e_all[k]

    wreal, wimag = w_ref[0, 0], w_ref[0, 1]
    for j in range(ysize):
        collect(win, sem_w, j)
        rows = pl.ds(j * chunk, chunk)
        second = y1[rows, :] - times(win[rows, :], wf1, True)
        first = y0[rows, :] - times(second, wf0, True)
        for n, part in enumerate((first, second)):
            real, imag = part[:, :width], part[:, width:]
            out_ref[n, rows, :width] = wreal * real - wimag * imag
            out_ref[n, rows, width:] = wreal * imag + wimag * real

    for copy in sent:
        copy.wait_send()
    handed_out(vk, vin, sem_v)
    handed_out(wk, win, sem_w)
    for j in range(ysize):
        @pl.when(y != j)
        def _():
            remote(eo.at[pl.ds(j * chunk, chunk), :], e_all.at[y], sem_e, j, y, {"y": j}).wait_send()
    for s in range(SUBS):
        @pl.when(z < zsize - 1)
        def _():
            hop(vo, vz, sem_fz, s, ahead).wait_send()

        @pl.when(z > 0)
        def _():
            hop(wo, wz, sem_bz, s, behind).wait_send()


def finish(
    dims, total_rows, x_ref, out_ref,
    other, cut, got, gram, g1, t1, g2, g3, h2, h1, wn, zs, turned, fin,
    sem_a, sem_x, sem_1, sem_2, sem_3, sem_4, sem_5, sem_6,
):
    xsize, zsize, ysize = dims
    x, core, z, y = (lax.axis_index(a) for a in AXES)
    poles = 2 * xsize
    pole = x * 2 + core
    vectors, width = x_ref.shape[1], x_ref.shape[2] // 2
    part = width // xsize
    own = vectors // poles
    line = own // ysize
    tall = min(128, vectors)

    def pole_of(d):
        p = lax.rem(pole + d, poles)
        return p, {"x": p // 2, "core": lax.rem(p, 2)}

    barrier = pltpu.get_barrier_semaphore()
    for d in range(1, poles):
        pl.semaphore_signal(barrier, inc=1, device_id=pole_of(d)[1], device_id_type=MESH_ID)
    for d in range(1, ysize):
        pl.semaphore_signal(barrier, inc=1, device_id={"y": lax.rem(y + d, ysize)}, device_id_type=MESH_ID)
    for d in range(1, zsize):
        pl.semaphore_signal(barrier, inc=1, device_id={"z": lax.rem(z + d, zsize)}, device_id_type=MESH_ID)
    pl.semaphore_wait(barrier, poles + ysize + zsize - 3)

    sent = []

    def go(src, dst, sems, d, device):
        copy = remote(src, dst, sems, d, d, device)
        copy.start()
        sent.append(copy)

    def land(dst, sems, d, device):
        remote(dst, dst, sems, d, d, device).wait_recv()

    def back(me, d, size):
        return lax.rem(me + size - d, size)

    sibling = {"core": 1 - core}
    go(x_ref.at[1 - core], other, sem_a, 0, sibling)
    land(other, sem_a, 0, sibling)
    pair = x_ref[core] + other[...]
    for j in range(xsize):
        cut[j] = jnp.concatenate(
            [pair[:, j * part : (j + 1) * part], pair[:, width + j * part : width + (j + 1) * part]], axis=1
        )
    for d in nearest_first(xsize):
        j = lax.rem(x + d, xsize)
        go(cut.at[j], got.at[x], sem_x, d, {"x": j})
    got[x] = cut[x]
    for d in nearest_first(xsize):
        j = back(x, d, xsize)
        land(got.at[j], sem_x, d, {"x": j})
    basis = got[0]
    for j in range(1, xsize):
        basis = basis + got[j]
    real, imag = basis[:, :part], basis[:, part:]
    lh, ll = halves(basis)
    rh, rl = halves(jnp.concatenate([real + imag, imag - real], axis=1))
    gram[...] = dot(lh, rh, True) + dot(ll, rh, True) + dot(lh, rl, True)

    def lines(ref, j, count):
        return ref.at[pl.ds(pl.multiple_of(j * count, count), count), :]

    for d in range(1, poles):
        p, device = pole_of(d)
        go(lines(gram, p, own), g1.at[pole], sem_1, d, device)
    g1[pole] = lines(gram, pole, own)[...]
    for d in range(1, poles):
        land(g1.at[back(pole, d, poles)], sem_1, d, pole_of(poles - d)[1])
    value = g1[0]
    for j in range(1, poles):
        value = value + g1[j]
    t1[...] = value
    for d in nearest_first(ysize):
        j = lax.rem(y + d, ysize)
        go(lines(t1, j, line), g2.at[y], sem_2, d, {"y": j})
    g2[y] = lines(t1, y, line)[...]
    for d in nearest_first(ysize):
        j = back(y, d, ysize)
        land(g2.at[j], sem_2, d, {"y": j})
    value = g2[0]
    for j in range(1, ysize):
        value = value + g2[j]
    g3[z] = value
    for d in nearest_first(zsize):
        go(g3.at[z], g3.at[z], sem_3, d, {"z": lax.rem(z + d, zsize)})
    for d in nearest_first(zsize):
        j = back(z, d, zsize)
        land(g3.at[j], sem_3, d, {"z": j})
    value = g3[0]
    for j in range(1, zsize):
        value = value + g3[j]
    lines(h2, y, line)[...] = value
    for d in nearest_first(ysize):
        go(lines(h2, y, line), lines(h2, y, line), sem_4, d, {"y": lax.rem(y + d, ysize)})
    for d in nearest_first(ysize):
        j = back(y, d, ysize)
        land(lines(h2, j, line), sem_4, d, {"y": j})
    lines(h1, pole, own)[...] = h2[...]
    for d in range(1, poles):
        go(h2, lines(h1, pole, own), sem_5, d, pole_of(d)[1])
    for d in range(1, poles):
        land(lines(h1, back(pole, d, poles), own), sem_5, d, pole_of(poles - d)[1])

    whole = h1[...]
    frob = jnp.sqrt(jnp.sum(whole * whole))
    flip = whole.T
    scale = -0.25 / frob
    eye = (
        lax.broadcasted_iota(jnp.int32, (vectors, vectors), 0)
        == lax.broadcasted_iota(jnp.int32, (vectors, vectors), 1)
    )
    first = jnp.where(eye, 1.5, 0.0) + scale * (whole + flip)
    minus = -scale * (whole - flip)
    prepare(wn.at[0], first, minus)
    zs[0, :, :vectors] = first
    zs[0, :, vectors:] = minus

    def square(i):
        rows = pl.ds(i, tall)
        zs[1, rows, :] = times(zs[0, rows, :], wn.at[0], False)

    tiles(vectors, tall, square)
    prepare(
        wn.at[1],
        zs[1, :, :vectors] - 1.5 * zs[0, :, :vectors],
        zs[1, :, vectors:] - 1.5 * zs[0, :, vectors:],
    )
    size = jnp.sqrt(total_rows / frob)
    stacked = jnp.concatenate(
        [basis, jnp.concatenate([-imag, real], axis=1)], axis=0
    )
    qh, ql = halves(stacked)
    turned[0] = qh
    turned[1] = ql

    def rotate(i):
        rows = pl.ds(i, tall)
        mix = 1.5 * zs[0, rows, :] + times(zs[1, rows, :], wn.at[1], False)
        gram_rows = times(mix, turned, False) * size
        cut[0, rows, :] = gram_rows

    for copy in sent:
        copy.wait_send()
    sent.clear()
    tiles(vectors, tall, rotate)
    for d in range(1, poles):
        p, device = pole_of(d)
        go(lines(cut.at[0], p, own), fin.at[pole], sem_6, d, device)
    fin[pole] = lines(cut.at[0], pole, own)[...]
    for d in range(1, poles):
        land(fin.at[back(pole, d, poles)], sem_6, d, pole_of(poles - d)[1])
    slots = [2 * j + n for n in range(2) for j in range(xsize)]
    out_ref[0] = jnp.concatenate([fin[k][:, :part] for k in slots], axis=1)
    out_ref[1] = jnp.concatenate([fin[k][:, part:] for k in slots], axis=1)
    for copy in sent:
        copy.wait_send()


def vmem():
    return pl.BlockSpec(memory_space=pltpu.VMEM)


def shards(sizes, subspace, pivots, lower_blocks, upper_blocks, pole_weights):
    xsize, zsize, ysize = sizes
    vectors, width = subspace.shape[1], pivots.shape[-1]
    wide = 2 * width
    chunk = vectors // ysize
    weight = (2, wide, wide)

    def dma(count):
        return pltpu.SemaphoreType.DMA((2, count))

    solved = pl.pallas_call(
        functools.partial(sweeps, (ysize, zsize)),
        out_shape=jax.ShapeDtypeStruct((2, vectors, wide), F32),
        in_specs=[vmem()] * 4 + [pl.BlockSpec(memory_space=pltpu.SMEM)],
        out_specs=vmem(),
        scratch_shapes=[pltpu.VMEM(weight, BF16)] * 4
        + [pltpu.VMEM((2, *weight), BF16)]
        + [pltpu.VMEM((ysize, *weight), BF16)] * 2
        + [pltpu.VMEM(weight, BF16)] * 2
        + [pltpu.VMEM((ysize, width, wide), F32)] * 2
        + [pltpu.VMEM((ysize, chunk, wide), F32)] * 2
        + [pltpu.VMEM((chunk, wide), F32)] * 2
        + [pltpu.VMEM((vectors, wide), F32)] * 7
        + [pltpu.VMEM((chunk, wide), F32)] * 4
        + [pltpu.VMEM((ysize, chunk, wide), F32)] * 2
        + [dma(ysize)] * 6
        + [dma(SUBS)] * 2,
        compiler_params=pltpu.CompilerParams(
            collective_id=0, has_side_effects=True, vmem_limit_bytes=56 * 2**20
        ),
        name="sweeps",
    )(subspace, pivots, lower_blocks, upper_blocks, pole_weights)

    poles = 2 * xsize
    part = width // xsize
    own = vectors // poles
    line = own // ysize
    total_rows = float(2 * width * ysize * zsize)
    return pl.pallas_call(
        functools.partial(finish, (xsize, zsize, ysize), total_rows),
        out_shape=jax.ShapeDtypeStruct((2, own, wide), F32),
        in_specs=[vmem()],
        out_specs=vmem(),
        scratch_shapes=[
            pltpu.VMEM((vectors, wide), F32),
            pltpu.VMEM((xsize, vectors, 2 * part), F32),
            pltpu.VMEM((xsize, vectors, 2 * part), F32),
            pltpu.VMEM((vectors, vectors), F32),
            pltpu.VMEM((poles, own, vectors), F32),
            pltpu.VMEM((own, vectors), F32),
            pltpu.VMEM((ysize, line, vectors), F32),
            pltpu.VMEM((zsize, line, vectors), F32),
            pltpu.VMEM((own, vectors), F32),
            pltpu.VMEM((vectors, vectors), F32),
            pltpu.VMEM((2, 2, 2 * vectors, 2 * vectors), BF16),
            pltpu.VMEM((2, vectors, 2 * vectors), F32),
            pltpu.VMEM((2, 2 * vectors, 2 * part), BF16),
            pltpu.VMEM((poles, own, 2 * part), F32),
            dma(1),
            dma(xsize),
            dma(poles),
            dma(ysize),
            dma(zsize),
            dma(ysize),
            dma(poles),
            dma(poles),
        ],
        compiler_params=pltpu.CompilerParams(
            collective_id=1, has_side_effects=True, vmem_limit_bytes=56 * 2**20
        ),
        name="finish",
    )(solved)


def build(mesh, sizes):
    xsize, zsize, ysize = sizes
    torus = Mesh(mesh.devices.reshape(xsize, 2, zsize, ysize), AXES)
    pole, rows = ("x", "core"), ("z", "y")
    return jax.shard_map(
        functools.partial(shards, sizes),
        mesh=torus,
        in_specs=(
            P(None, None, rows),
            P(pole, rows, None, None, None),
            P(pole, rows, None, None, None),
            P(pole, rows, None, None, None),
            P(pole, None),
        ),
        out_specs=P(None, pole, rows),
        check_vma=False,
    )


def solution(mesh):
    return build(mesh, (mesh.shape["pole"] // 2, mesh.shape["rows"] // 4, 4))
```

```python
import functools

import jax
import jax.numpy as jnp
from jax import lax
from jax.experimental import pallas as pl
from jax.experimental.pallas import tpu as pltpu
from jax.sharding import Mesh
from jax.sharding import PartitionSpec as P

F32 = jnp.float32
BF16 = jnp.bfloat16
MESH_ID = pl.DeviceIdType.MESH
AXES = ("x", "core", "z", "y")
SUBS = 4


def halves(value):
    high = value.astype(BF16)
    return high, (value - high.astype(F32)).astype(BF16)


def dot(left, right, trans):
    dims = (((1,), (1 if trans else 0,)), ((), ()))
    return lax.dot_general(left, right, dims, preferred_element_type=F32)


def times(rows, weights, trans):
    high, low = halves(rows)
    count = rows.shape[0]
    both = dot(jnp.concatenate([high, low], axis=0), weights[0], trans)
    return both[:count] + both[count:] + dot(high, weights[1], trans)


def prepare(weights, real, minus):
    size = real.shape[0]
    for part, (r, m) in enumerate(zip(halves(real), halves(minus))):
        weights[part, :size, :size] = r
        weights[part, :size, size:] = m
        weights[part, size:, :size] = -m
        weights[part, size:, size:] = r


def tiles(count, size, body):
    if count == size:
        body(0)
        return

    def step(i, carry):
        body(pl.multiple_of(i * size, size))
        return carry

    lax.fori_loop(0, count // size, step, 0)


def remote(src, dst, sems, slot_out, slot_in, device):
    return pltpu.make_async_remote_copy(
        src_ref=src,
        dst_ref=dst,
        send_sem=sems.at[0, slot_out],
        recv_sem=sems.at[1, slot_in],
        device_id=device,
        device_id_type=MESH_ID,
    )


def nearest_first(count):
    return sorted(range(1, count), key=lambda d: min(d, count - d))


def step_kernel(
    dims, total_rows, f_hbm, g_hbm, e_hbm, u_hbm, w_ref, out_ref,
    f_ref, g_ref, e_ref, u_ref,
    we0, we1, wf0, wf1, wg, wc, wd, wp, wq, wh,
    c_all, d_all, b_all, e_all, qg, rg, s0, s1, y0, y1, e0, eo, vin, win, tmp,
    vz, vo, wz, wo, vk, wk,
    xs, other, cut, got, gram, g1, t1, g2, g3, h2, h1, wn, zs, turned, spun, fin,
    sem_in, sem_c, sem_b, sem_d, sem_v, sem_e, sem_w, sem_fz, sem_bz,
    sem_a, sem_x, sem_1, sem_2, sem_3, sem_4, sem_5, sem_6,
):
    xsize, zsize, ysize = dims
    x, core, z, y = (lax.axis_index(a) for a in AXES)
    poles = 2 * xsize
    pole = x * 2 + core
    vectors, width = f_ref.shape[1], g_ref.shape[-1]
    chunk = vectors // ysize
    sub = chunk // SUBS
    tall = min(128, width)
    part = width // xsize
    own = vectors // poles
    line = own // ysize
    order = nearest_first(ysize)

    def pole_of(d):
        p = lax.rem(pole + d, poles)
        return p, {"x": p // 2, "core": lax.rem(p, 2)}

    def along(axis, me, d, size):
        return {axis: lax.rem(me + d, size)}

    barrier = pltpu.get_barrier_semaphore()
    for d in range(1, ysize):
        pl.semaphore_signal(barrier, inc=1, device_id=along("y", y, d, ysize), device_id_type=MESH_ID)
    for d in range(1, zsize):
        pl.semaphore_signal(barrier, inc=1, device_id=along("z", z, d, zsize), device_id_type=MESH_ID)
    for d in range(1, poles):
        pl.semaphore_signal(barrier, inc=1, device_id=pole_of(d)[1], device_id_type=MESH_ID)

    loads = [
        pltpu.make_async_copy(a, b, sem_in.at[i])
        for i, (a, b) in enumerate(((e_hbm, e_ref), (u_hbm, u_ref), (g_hbm, g_ref), (f_hbm, f_ref)))
    ]
    for load in loads:
        load.start()

    sent = []

    def go(src, dst, sems, d, device):
        copy = remote(src, dst, sems, d, d, device)
        copy.start()
        sent.append(copy)

    def land(dst, sems, d, device):
        remote(dst, dst, sems, d, d, device).wait_recv()

    def back(me, d, size):
        return lax.rem(me + size - d, size)

    def lines(ref, j, count):
        return ref.at[pl.ds(pl.multiple_of(j * count, count), count), :]

    def piece(ref, j):
        return lines(ref, j, chunk)

    loads[0].wait()
    prepare(we0, e_ref[0, 0, 0], -e_ref[0, 0, 1])

    def forward_map(i):
        rows = jnp.concatenate([e_ref[0, 1, 0, pl.ds(i, tall), :], -e_ref[0, 1, 1, pl.ds(i, tall), :]], axis=1)
        c_all[y, pl.ds(i, tall), :] = times(rows, we0, False)

    tiles(width, tall, forward_map)
    pl.semaphore_wait(barrier, ysize + zsize + poles - 3)

    half = width // 2
    right, left = along("y", y, 1, ysize), along("y", y, ysize - 1, ysize)
    after, ahead_y = back(y, 1, ysize), lax.rem(y + 1, ysize)

    def half_of(k, h):
        return c_all.at[k, pl.ds(h * half, half), :]

    go(half_of(y, 0), half_of(y, 0), sem_c, 0, right)
    if ysize > 2:
        go(half_of(y, 1), half_of(y, 1), sem_c, 2, left)
    go(half_of(y, 1), half_of(y, 1), sem_c, 1, right)
    if ysize > 2:
        go(half_of(y, 0), half_of(y, 0), sem_c, 3, left)

    loads[2].wait()
    prepare(wg.at[0], g_ref[0, 0, 0], -g_ref[0, 0, 1])
    prepare(wg.at[1], g_ref[0, 1, 0], -g_ref[0, 1, 1])
    prepare(we1, e_ref[0, 1, 0], -e_ref[0, 1, 1])
    loads[3].wait()

    def local(i):
        rows = pl.ds(i, tall)
        first = jnp.concatenate([f_ref[0, rows, :width], f_ref[1, rows, :width]], axis=1)
        second = jnp.concatenate([f_ref[0, rows, width:], f_ref[1, rows, width:]], axis=1)
        start = times(first, wg.at[0], True)
        s0[rows, :] = start
        s1[rows, :] = times(second, wg.at[1], True) - times(start, we1, True)

    tiles(vectors, tall, local)
    for d in order:
        go(piece(s1, lax.rem(y + d, ysize)), b_all.at[y], sem_b, d, along("y", y, d, ysize))
    b_all[y] = piece(s1, y)[...]

    def pass_on():
        land(half_of(after, 0), sem_c, 0, left)
        if ysize > 2:
            go(half_of(after, 0), half_of(after, 0), sem_c, 4, right)
            land(half_of(ahead_y, 1), sem_c, 2, right)
            go(half_of(ahead_y, 1), half_of(ahead_y, 1), sem_c, 5, left)

    loads[1].wait()
    prepare(wf1, u_ref[0, 1, 0], -u_ref[0, 1, 1])
    prepare(wf0, u_ref[0, 0, 0], -u_ref[0, 0, 1])
    prepare(wc.at[y], c_all[y, :, :width], c_all[y, :, width:])

    def backward_map(i):
        rows = pl.ds(i, tall)
        upper = jnp.concatenate([u_ref[0, 0, 0, rows, :], -u_ref[0, 0, 1, rows, :]], axis=1)
        d_all[y, rows, :] = times(upper, wf1, False)
        lower = jnp.concatenate([e_ref[0, 0, 0, rows, :], -e_ref[0, 0, 1, rows, :]], axis=1)
        tmp[rows, :] = -lower - times(upper, wc.at[y], False)

    tiles(width, tall, backward_map)
    pass_on()
    prepare(wh, tmp[:width, :width], tmp[:width, width:])

    def local_ends(i):
        rows = pl.ds(i, tall)
        e0[rows, :] = s0[rows, :] - times(s1[rows, :], wf0, True)

    tiles(vectors, tall, local_ends)

    land(half_of(after, 1), sem_c, 1, left)
    prepare(wc.at[after], c_all[after, :, :width], c_all[after, :, width:])
    if ysize > 2:
        land(half_of(ahead_y, 0), sem_c, 3, right)
        prepare(wc.at[ahead_y], c_all[ahead_y, :, :width], c_all[ahead_y, :, width:])
        far = lax.rem(y + 2, ysize)
        land(half_of(far, 0), sem_c, 4, left)
        land(half_of(far, 1), sem_c, 5, right)
        prepare(wc.at[far], c_all[far, :, :width], c_all[far, :, width:])
    for d in order:
        land(b_all.at[back(y, d, ysize)], sem_b, d, along("y", y, ysize - d, ysize))
    for d in order:
        go(d_all.at[y], d_all.at[y], sem_d, d, along("y", y, d, ysize))

    value = b_all[0]
    for k in range(1, ysize):
        value = times(value, wc.at[k], True) + b_all[k]
    qg[...] = value

    def hop(out, into, sems, s, device):
        return remote(out.at[pl.ds(s * sub, sub), :], into.at[pl.ds(s * sub, sub), :], sems, s, s, device)

    ahead, behind = along("z", z, 1, zsize), along("z", z, zsize - 1, zsize)

    @pl.when(z == 0)
    def _():
        for s in range(SUBS):
            hop(qg, vz, sem_fz, s, ahead).start()
        vz[...] = jnp.zeros_like(vz)

    @pl.when(jnp.logical_and(z > 0, z < zsize - 1))
    def _():
        def group_forward(i):
            value = c_all[ysize - 1, pl.ds(i, tall), :]
            for k in reversed(range(ysize - 1)):
                value = times(value, wc.at[k], False)
            tmp[pl.ds(i, tall), :] = value

        tiles(width, tall, group_forward)
        prepare(wp, tmp[:width, :width], tmp[:width, width:])

    for s in range(SUBS):
        rows = pl.ds(s * sub, sub)

        @pl.when(z > 0)
        def _():
            hop(vz, vz, sem_fz, s, behind).wait_recv()

        @pl.when(jnp.logical_and(z > 0, z < zsize - 1))
        def _():
            vo[rows, :] = times(vz[rows, :], wp, True) + qg[rows, :]
            hop(vo, vz, sem_fz, s, ahead).start()

    def hand_out(k, value, staging, into, sems):
        staging[k] = value

        @pl.when(y == k)
        def _():
            piece(into, y)[...] = value

        @pl.when(y != k)
        def _():
            remote(staging.at[k], piece(into, y), sems, k, y, {"y": k}).start()

    def handed_out(staging, into, sems):
        for k in range(ysize):
            @pl.when(y != k)
            def _():
                remote(staging.at[k], piece(into, y), sems, k, y, {"y": k}).wait_send()

    value = vz[...]
    for k in range(ysize):
        hand_out(k, value, vk, vin, sem_v)
        if k < ysize - 1:
            value = times(value, wc.at[k], True) + b_all[k]

    prepare(wd.at[y], d_all[y, :, :width], d_all[y, :, width:])
    for d in order:
        k = back(y, d, ysize)
        land(d_all.at[k], sem_d, d, along("y", y, ysize - d, ysize))
        prepare(wd.at[k], d_all[k, :, :width], d_all[k, :, width:])

    for d in [0] + order:
        j = lax.rem(y + d, ysize)
        rows = pl.ds(pl.multiple_of(j * chunk, chunk), chunk)
        if d:
            remote(vin.at[rows, :], vin.at[rows, :], sem_v, j, j, {"y": j}).wait_recv()
        ends = e0[rows, :] + times(vin[rows, :], wh, True)
        if d:
            eo[rows, :] = ends
            remote(eo.at[rows, :], e_all.at[y], sem_e, j, y, {"y": j}).start()
        else:
            e_all[y] = ends

    def swept(i):
        rows = pl.ds(i, tall)
        value = vin[rows, :]
        y0[rows, :] = s0[rows, :] - times(value, we0, True)
        y1[rows, :] = s1[rows, :] + times(value, wc.at[y], True)

    tiles(vectors, tall, swept)

    @pl.when(jnp.logical_and(z > 0, z < zsize - 1))
    def _():
        def compose(i):
            value = d_all[0, pl.ds(i, tall), :]
            for k in range(1, ysize):
                value = times(value, wd.at[k], False)
            tmp[pl.ds(i, tall), :] = value

        tiles(width, tall, compose)
        prepare(wq, tmp[:width, :width], tmp[:width, width:])

    for d in order:
        j = lax.rem(y + d, ysize)
        remote(e_all.at[j], e_all.at[j], sem_e, j, j, {"y": j}).wait_recv()
    value = e_all[ysize - 1]
    for k in reversed(range(ysize - 1)):
        value = times(value, wd.at[k], True) + e_all[k]
    rg[...] = value

    @pl.when(z == zsize - 1)
    def _():
        for s in range(SUBS):
            hop(rg, wz, sem_bz, s, behind).start()
        wz[...] = jnp.zeros_like(wz)

    for s in range(SUBS):
        rows = pl.ds(s * sub, sub)

        @pl.when(z < zsize - 1)
        def _():
            hop(wz, wz, sem_bz, s, ahead).wait_recv()

        @pl.when(jnp.logical_and(z > 0, z < zsize - 1))
        def _():
            wo[rows, :] = times(wz[rows, :], wq, True) + rg[rows, :]
            hop(wo, wz, sem_bz, s, behind).start()

    value = wz[...]
    for k in reversed(range(ysize)):
        hand_out(k, value, wk, win, sem_w)
        if k > 0:
            value = times(value, wd.at[k], True) + e_all[k]

    sibling = {"core": 1 - core}
    wreal, wimag = w_ref[0, 0], w_ref[0, 1]

    def rows_of(d):
        j = lax.rem(y + d, ysize)
        return j, pl.ds(pl.multiple_of(j * chunk, chunk), chunk)

    def over_x(turn, d):
        _, rows = rows_of(d)
        land(other.at[rows, :], sem_a, turn, sibling)
        pair = xs[core, rows, :] + other[rows, :]
        for j in range(xsize):
            cut[j, rows, :] = jnp.concatenate(
                [pair[:, j * part : (j + 1) * part], pair[:, width + j * part : width + (j + 1) * part]], axis=1
            )
        for step in nearest_first(xsize):
            go(
                cut.at[lax.rem(x + step, xsize), rows, :],
                got.at[x, rows, :],
                sem_x,
                turn * xsize + step,
                along("x", x, step, xsize),
            )
        got[x, rows, :] = cut[x, rows, :]

    turns = [0] + order
    for turn, d in enumerate(turns):
        j, rows = rows_of(d)
        if d:
            remote(win.at[rows, :], win.at[rows, :], sem_w, j, j, {"y": j}).wait_recv()
        second = y1[rows, :] - times(win[rows, :], wf1, True)
        first = y0[rows, :] - times(second, wf0, True)
        for n, solved in enumerate((first, second)):
            real, imag = solved[:, :width], solved[:, width:]
            xs[n, rows, :width] = wreal * real - wimag * imag
            xs[n, rows, width:] = wreal * imag + wimag * real
        go(xs.at[1 - core, rows, :], other.at[rows, :], sem_a, turn, sibling)
        if turn:
            over_x(turn - 1, turns[turn - 1])
    over_x(len(turns) - 1, turns[-1])
    for turn, d in enumerate(turns):
        _, rows = rows_of(d)
        for step in nearest_first(xsize):
            j = back(x, step, xsize)
            land(got.at[j, rows, :], sem_x, turn * xsize + step, {"x": j})
    basis = got[0]
    for j in range(1, xsize):
        basis = basis + got[j]
    real, imag = basis[:, :part], basis[:, part:]
    lh, ll = halves(basis)
    rh, rl = halves(jnp.concatenate([real + imag, imag - real], axis=1))
    gram[...] = dot(lh, rh, True) + dot(ll, rh, True) + dot(lh, rl, True)

    for d in range(1, poles):
        p, device = pole_of(d)
        go(lines(gram, p, own), g1.at[pole], sem_1, d, device)
    g1[pole] = lines(gram, pole, own)[...]
    for d in range(1, poles):
        land(g1.at[back(pole, d, poles)], sem_1, d, pole_of(poles - d)[1])
    value = g1[0]
    for j in range(1, poles):
        value = value + g1[j]
    t1[...] = value
    for d in nearest_first(ysize):
        j = lax.rem(y + d, ysize)
        go(lines(t1, j, line), g2.at[y], sem_2, d, {"y": j})
    g2[y] = lines(t1, y, line)[...]
    for d in nearest_first(ysize):
        j = back(y, d, ysize)
        land(g2.at[j], sem_2, d, {"y": j})
    value = g2[0]
    for j in range(1, ysize):
        value = value + g2[j]
    g3[z] = value
    for d in nearest_first(zsize):
        go(g3.at[z], g3.at[z], sem_3, d, {"z": lax.rem(z + d, zsize)})
    for d in nearest_first(zsize):
        j = back(z, d, zsize)
        land(g3.at[j], sem_3, d, {"z": j})
    value = g3[0]
    for j in range(1, zsize):
        value = value + g3[j]
    lines(h2, y, line)[...] = value
    for d in nearest_first(ysize):
        go(lines(h2, y, line), lines(h2, y, line), sem_4, d, {"y": lax.rem(y + d, ysize)})
    for d in nearest_first(ysize):
        j = back(y, d, ysize)
        land(lines(h2, j, line), sem_4, d, {"y": j})
    lines(h1, pole, own)[...] = h2[...]
    for d in range(1, poles):
        go(h2, lines(h1, pole, own), sem_5, d, pole_of(d)[1])
    for d in range(1, poles):
        land(lines(h1, back(pole, d, poles), own), sem_5, d, pole_of(poles - d)[1])

    whole = h1[...]
    frob = jnp.sqrt(jnp.sum(whole * whole))
    flip = whole.T
    scale = -0.25 / frob
    eye = (
        lax.broadcasted_iota(jnp.int32, (vectors, vectors), 0)
        == lax.broadcasted_iota(jnp.int32, (vectors, vectors), 1)
    )
    first = jnp.where(eye, 1.5, 0.0) + scale * (whole + flip)
    minus = -scale * (whole - flip)
    prepare(wn.at[0], first, minus)
    zs[0, :, :vectors] = first
    zs[0, :, vectors:] = minus

    def square(i):
        rows = pl.ds(i, tall)
        zs[1, rows, :] = times(zs[0, rows, :], wn.at[0], False)

    tiles(vectors, tall, square)
    prepare(
        wn.at[1],
        zs[1, :, :vectors] - 1.5 * zs[0, :, :vectors],
        zs[1, :, vectors:] - 1.5 * zs[0, :, vectors:],
    )
    size = jnp.sqrt(total_rows / frob)
    stacked = jnp.concatenate(
        [basis, jnp.concatenate([-imag, real], axis=1)], axis=0
    )
    qh, ql = halves(stacked)
    turned[0] = qh
    turned[1] = ql

    def rotate(i):
        rows = pl.ds(i, tall)
        mix = 1.5 * zs[0, rows, :] + times(zs[1, rows, :], wn.at[1], False)
        spun[rows, :] = times(mix, turned, False) * size

    tiles(vectors, tall, rotate)
    for d in range(1, poles):
        p, device = pole_of(d)
        go(lines(spun, p, own), fin.at[pole], sem_6, d, device)
    fin[pole] = lines(spun, pole, own)[...]
    for d in range(1, poles):
        land(fin.at[back(pole, d, poles)], sem_6, d, pole_of(poles - d)[1])
    slots = [2 * j + n for n in range(2) for j in range(xsize)]
    out_ref[0] = jnp.concatenate([fin[k][:, :part] for k in slots], axis=1)
    out_ref[1] = jnp.concatenate([fin[k][:, part:] for k in slots], axis=1)
    for copy in sent:
        copy.wait_send()
    handed_out(vk, vin, sem_v)
    handed_out(wk, win, sem_w)
    for d in order:
        j, rows = rows_of(d)
        remote(eo.at[rows, :], e_all.at[y], sem_e, j, y, {"y": j}).wait_send()
    for s in range(SUBS):
        @pl.when(z < zsize - 1)
        def _():
            hop(vo, vz, sem_fz, s, ahead).wait_send()

        @pl.when(z > 0)
        def _():
            hop(wo, wz, sem_bz, s, behind).wait_send()


def shards(sizes, subspace, pivots, lower_blocks, upper_blocks, pole_weights):
    xsize, zsize, ysize = sizes
    vectors, width = subspace.shape[1], pivots.shape[-1]
    wide = 2 * width
    chunk = vectors // ysize
    poles = 2 * xsize
    part = width // xsize
    own = vectors // poles
    line = own // ysize
    total_rows = float(2 * width * ysize * zsize)

    def dma(count):
        return pltpu.SemaphoreType.DMA((2, count))

    def f32(*shape):
        return pltpu.VMEM(shape, F32)

    def prepared(*counts):
        return pltpu.VMEM((*counts, 2, wide, wide), BF16)

    anywhere = pl.BlockSpec(memory_space=pl.ANY)
    return pl.pallas_call(
        functools.partial(step_kernel, (xsize, zsize, ysize), total_rows),
        out_shape=jax.ShapeDtypeStruct((2, own, wide), F32),
        in_specs=[anywhere] * 4 + [pl.BlockSpec(memory_space=pltpu.SMEM)],
        out_specs=pl.BlockSpec(memory_space=pltpu.VMEM),
        scratch_shapes=[f32(*a.shape) for a in (subspace, pivots, lower_blocks, upper_blocks)]
        + [prepared()] * 4
        + [prepared(2)]
        + [prepared(ysize)] * 2
        + [prepared()] * 3
        + [f32(ysize, width, wide)] * 2
        + [f32(ysize, chunk, wide)] * 2
        + [f32(chunk, wide)] * 2
        + [f32(vectors, wide)] * 9
        + [f32(chunk, wide)] * 4
        + [f32(ysize, chunk, wide)] * 2
        + [
            f32(2, vectors, wide),
            f32(vectors, wide),
            f32(xsize, vectors, 2 * part),
            f32(xsize, vectors, 2 * part),
            f32(vectors, vectors),
            f32(poles, own, vectors),
            f32(own, vectors),
            f32(ysize, line, vectors),
            f32(zsize, line, vectors),
            f32(own, vectors),
            f32(vectors, vectors),
            pltpu.VMEM((2, 2, 2 * vectors, 2 * vectors), BF16),
            f32(2, vectors, 2 * vectors),
            pltpu.VMEM((2, 2 * vectors, 2 * part), BF16),
            f32(vectors, 2 * part),
            f32(poles, own, 2 * part),
            pltpu.SemaphoreType.DMA((4,)),
            dma(6),
        ]
        + [dma(ysize)] * 5
        + [dma(SUBS)] * 2
        + [
            dma(ysize),
            dma(ysize * xsize),
            dma(poles),
            dma(ysize),
            dma(zsize),
            dma(ysize),
            dma(poles),
            dma(poles),
        ],
        compiler_params=pltpu.CompilerParams(
            collective_id=0, has_side_effects=True, vmem_limit_bytes=60 * 2**20
        ),
        name="step",
    )(subspace, pivots, lower_blocks, upper_blocks, pole_weights)


def build(mesh, sizes):
    xsize, zsize, ysize = sizes
    torus = Mesh(mesh.devices.reshape(xsize, 2, zsize, ysize), AXES)
    pole, rows = ("x", "core"), ("z", "y")
    return jax.shard_map(
        functools.partial(shards, sizes),
        mesh=torus,
        in_specs=(
            P(None, None, rows),
            P(pole, rows, None, None, None),
            P(pole, rows, None, None, None),
            P(pole, rows, None, None, None),
            P(pole, None),
        ),
        out_specs=P(None, pole, rows),
        check_vma=False,
    )


def solution(mesh):
    return build(mesh, (mesh.shape["pole"] // 2, mesh.shape["rows"] // 4, 4))
```

```python
import functools

import jax
import jax.numpy as jnp
from jax import lax
from jax.experimental import pallas as pl
from jax.experimental.pallas import tpu as pltpu
from jax.sharding import Mesh
from jax.sharding import PartitionSpec as P

F32 = jnp.float32
BF16 = jnp.bfloat16
MESH_ID = pl.DeviceIdType.MESH
AXES = ("x", "core", "z", "y")
SUBS = 4


def halves(value):
    high = value.astype(BF16)
    return high, (value - high.astype(F32)).astype(BF16)


def dot(left, right, trans):
    dims = (((1,), (1 if trans else 0,)), ((), ()))
    return lax.dot_general(left, right, dims, preferred_element_type=F32)


def times(rows, weights, trans):
    high, low = halves(rows)
    count = rows.shape[0]
    both = dot(jnp.concatenate([high, low], axis=0), weights[0], trans)
    return both[:count] + both[count:] + dot(high, weights[1], trans)


def prepare(weights, real, minus):
    size = real.shape[0]
    for part, (r, m) in enumerate(zip(halves(real), halves(minus))):
        weights[part, :size, :size] = r
        weights[part, :size, size:] = m
        weights[part, size:, :size] = -m
        weights[part, size:, size:] = r


def tiles(count, size, body):
    if count == size:
        body(0)
        return

    def step(i, carry):
        body(pl.multiple_of(i * size, size))
        return carry

    lax.fori_loop(0, count // size, step, 0)


def remote(src, dst, sems, slot_out, slot_in, device):
    return pltpu.make_async_remote_copy(
        src_ref=src,
        dst_ref=dst,
        send_sem=sems.at[0, slot_out],
        recv_sem=sems.at[1, slot_in],
        device_id=device,
        device_id_type=MESH_ID,
    )


def nearest_first(count):
    return sorted(range(1, count), key=lambda d: min(d, count - d))


def step_kernel(
    dims, total_rows, f_hbm, g_hbm, e_hbm, u_hbm, w_ref, out_ref,
    f_ref, g_ref, e_ref, u_ref,
    we0, we1, wf0, wf1, wg, wc, wd, wp, wq, wh, wj, wz1, wa0, wa1,
    c_all, d_all, b_all, e_all, qg, rg, rj, rz, s0, s1, y0, y1, e0, eo, vin, win, tmp, wb, dg, dz, am,
    vz, vo, wz, wo, vk, wk,
    xs, other, cut, got, gram, g1, t1, g2, g3, h2, h1, wn, zs, turned, spun, fin,
    sem_in, sem_c, sem_b, sem_d, sem_v, sem_e, sem_r, sem_w, sem_fz, sem_bz, sem_one, sem_far,
    sem_a, sem_x, sem_1, sem_2, sem_3, sem_4, sem_5, sem_6,
):
    xsize, zsize, ysize = dims
    x, core, z, y = (lax.axis_index(a) for a in AXES)
    poles = 2 * xsize
    pole = x * 2 + core
    vectors, width = f_ref.shape[1], g_ref.shape[-1]
    chunk = vectors // ysize
    sub = chunk // SUBS
    tall = min(128, width)
    part = width // xsize
    own = vectors // poles
    line = own // ysize
    order = nearest_first(ysize)

    def pole_of(d):
        p = lax.rem(pole + d, poles)
        return p, {"x": p // 2, "core": lax.rem(p, 2)}

    def along(axis, me, d, size):
        return {axis: lax.rem(me + d, size)}

    barrier = pltpu.get_barrier_semaphore()
    for d in range(1, ysize):
        pl.semaphore_signal(barrier, inc=1, device_id=along("y", y, d, ysize), device_id_type=MESH_ID)
    for d in range(1, zsize):
        pl.semaphore_signal(barrier, inc=1, device_id=along("z", z, d, zsize), device_id_type=MESH_ID)
    for d in range(1, poles):
        pl.semaphore_signal(barrier, inc=1, device_id=pole_of(d)[1], device_id_type=MESH_ID)

    loads = [
        pltpu.make_async_copy(a, b, sem_in.at[i])
        for i, (a, b) in enumerate(((e_hbm, e_ref), (u_hbm, u_ref), (g_hbm, g_ref), (f_hbm, f_ref)))
    ]
    for load in loads:
        load.start()

    sent = []

    def go(src, dst, sems, d, device):
        copy = remote(src, dst, sems, d, d, device)
        copy.start()
        sent.append(copy)

    def land(dst, sems, d, device):
        remote(dst, dst, sems, d, d, device).wait_recv()

    def back(me, d, size):
        return lax.rem(me + size - d, size)

    def lines(ref, j, count):
        return ref.at[pl.ds(pl.multiple_of(j * count, count), count), :]

    def piece(ref, j):
        return lines(ref, j, chunk)

    loads[0].wait()
    prepare(we0, e_ref[0, 0, 0], -e_ref[0, 0, 1])

    def forward_map(i):
        rows = jnp.concatenate([e_ref[0, 1, 0, pl.ds(i, tall), :], -e_ref[0, 1, 1, pl.ds(i, tall), :]], axis=1)
        c_all[y, pl.ds(i, tall), :] = times(rows, we0, False)

    tiles(width, tall, forward_map)
    pl.semaphore_wait(barrier, ysize + zsize + poles - 3)

    half = width // 2
    right, left = along("y", y, 1, ysize), along("y", y, ysize - 1, ysize)
    before, beyond, far = back(y, 1, ysize), lax.rem(y + 1, ysize), lax.rem(y + 2, ysize)

    def half_of(store, k, h):
        return store.at[k, pl.ds(h * half, half), :]

    def share(store, sems):
        for slot, h, device in ((0, 0, right), (2, 1, left), (1, 1, right), (3, 0, left)):
            if ysize > 2 or slot < 2:
                go(half_of(store, y, h), half_of(store, y, h), sems, slot, device)

    def onward(store, sems):
        first, second = half_of(store, before, 0), half_of(store, beyond, 1)
        return remote(first, first, sems, 4, 4, right), remote(second, second, sems, 5, 5, left)

    def pass_on(store, sems):
        land(half_of(store, before, 0), sems, 0, left)
        if ysize > 2:
            to_right, to_left = onward(store, sems)
            to_right.start()
            land(half_of(store, beyond, 1), sems, 2, right)
            to_left.start()

    def take(store, sems, weights):
        land(half_of(store, before, 1), sems, 1, left)
        prepare(weights.at[before], store[before, :, :width], store[before, :, width:])
        if ysize > 2:
            land(half_of(store, beyond, 0), sems, 3, right)
            prepare(weights.at[beyond], store[beyond, :, :width], store[beyond, :, width:])
            land(half_of(store, far, 0), sems, 4, left)
            land(half_of(store, far, 1), sems, 5, right)
            prepare(weights.at[far], store[far, :, :width], store[far, :, width:])

    share(c_all, sem_c)

    loads[2].wait()
    prepare(wg.at[0], g_ref[0, 0, 0], -g_ref[0, 0, 1])
    prepare(wg.at[1], g_ref[0, 1, 0], -g_ref[0, 1, 1])
    prepare(we1, e_ref[0, 1, 0], -e_ref[0, 1, 1])
    loads[3].wait()

    def local(i):
        rows = pl.ds(i, tall)
        first = jnp.concatenate([f_ref[0, rows, :width], f_ref[1, rows, :width]], axis=1)
        second = jnp.concatenate([f_ref[0, rows, width:], f_ref[1, rows, width:]], axis=1)
        start = times(first, wg.at[0], True)
        s0[rows, :] = start
        s1[rows, :] = times(second, wg.at[1], True) - times(start, we1, True)

    tiles(vectors, tall, local)
    for d in order:
        go(piece(s1, lax.rem(y + d, ysize)), b_all.at[y], sem_b, d, along("y", y, d, ysize))
    b_all[y] = piece(s1, y)[...]

    loads[1].wait()
    prepare(wf1, u_ref[0, 1, 0], -u_ref[0, 1, 1])
    prepare(wf0, u_ref[0, 0, 0], -u_ref[0, 0, 1])
    prepare(wc.at[y], c_all[y, :, :width], c_all[y, :, width:])

    def backward_map(i):
        rows = pl.ds(i, tall)
        upper = jnp.concatenate([u_ref[0, 0, 0, rows, :], -u_ref[0, 0, 1, rows, :]], axis=1)
        d_all[y, rows, :] = times(upper, wf1, False)
        lower = jnp.concatenate([e_ref[0, 0, 0, rows, :], -e_ref[0, 0, 1, rows, :]], axis=1)
        tmp[rows, :] = -lower - times(upper, wc.at[y], False)

    tiles(width, tall, backward_map)
    pass_on(c_all, sem_c)
    prepare(wh, tmp[:width, :width], tmp[:width, width:])

    def local_ends(i):
        rows = pl.ds(i, tall)
        e0[rows, :] = s0[rows, :] - times(s1[rows, :], wf0, True)

    tiles(vectors, tall, local_ends)

    take(c_all, sem_c, wc)
    for d in order:
        land(b_all.at[back(y, d, ysize)], sem_b, d, along("y", y, ysize - d, ysize))
    share(d_all, sem_d)

    value = b_all[0]
    for k in range(1, ysize):
        value = times(value, wc.at[k], True) + b_all[k]
    qg[...] = value

    def hop(out, into, sems, s, device):
        return remote(out.at[pl.ds(s * sub, sub), :], into.at[pl.ds(s * sub, sub), :], sems, s, s, device)

    ahead, behind = along("z", z, 1, zsize), along("z", z, zsize - 1, zsize)

    @pl.when(z == 0)
    def _():
        for s in range(SUBS):
            hop(qg, vz, sem_fz, s, ahead).start()
        vz[...] = jnp.zeros_like(vz)

    @pl.when(jnp.logical_and(z > 0, z < zsize - 1))
    def _():
        def group_forward(i):
            value = c_all[ysize - 1, pl.ds(i, tall), :]
            for k in reversed(range(ysize - 1)):
                value = times(value, wc.at[k], False)
            tmp[pl.ds(i, tall), :] = value

        tiles(width, tall, group_forward)
        prepare(wp, tmp[:width, :width], tmp[:width, width:])

    early = z < 3
    pl.when(jnp.logical_not(early))(lambda: pass_on(d_all, sem_d))

    for s in range(SUBS):
        rows = pl.ds(s * sub, sub)

        @pl.when(z > 0)
        def _():
            hop(vz, vz, sem_fz, s, behind).wait_recv()

        @pl.when(jnp.logical_and(z > 0, z < zsize - 1))
        def _():
            vo[rows, :] = times(vz[rows, :], wp, True) + qg[rows, :]
            hop(vo, vz, sem_fz, s, ahead).start()

    def hand_out(k, value, staging, into, sems):
        staging[k] = value

        @pl.when(y == k)
        def _():
            piece(into, y)[...] = value

        @pl.when(y != k)
        def _():
            remote(staging.at[k], piece(into, y), sems, k, y, {"y": k}).start()

    def handed_out(staging, into, sems, count):
        for k in range(count):
            @pl.when(y != k)
            def _():
                remote(staging.at[k], piece(into, y), sems, k, y, {"y": k}).wait_send()

    value = vz[...]
    for k in range(ysize):
        hand_out(k, value, vk, vin, sem_v)
        if k < ysize - 1:
            value = times(value, wc.at[k], True) + b_all[k]

    pl.when(early)(lambda: pass_on(d_all, sem_d))

    for d in [0] + order:
        j = lax.rem(y + d, ysize)
        rows = pl.ds(pl.multiple_of(j * chunk, chunk), chunk)
        if d:
            remote(vin.at[rows, :], vin.at[rows, :], sem_v, j, j, {"y": j}).wait_recv()
        ends = e0[rows, :] + times(vin[rows, :], wh, True)
        if d:
            eo[rows, :] = ends
            remote(eo.at[rows, :], e_all.at[y], sem_e, j, y, {"y": j}).start()
        else:
            e_all[y] = ends

    prepare(wd.at[y], d_all[y, :, :width], d_all[y, :, width:])
    take(d_all, sem_d, wd)
    even = lax.rem(z, 2) == 0
    jumps = jnp.logical_and(even, jnp.logical_and(z >= 2, z <= zsize - 4))
    feeds = jnp.logical_and(jnp.logical_not(even), z <= zsize - 5)
    leaps = jnp.logical_and(even, z <= zsize - 6)
    last = z == zsize - 1
    inner = jnp.logical_and(z > 0, z < zsize - 1)
    steps = jnp.logical_and(inner, z >= zsize - 3)

    @pl.when(inner)
    def _():
        def compose(i):
            value = d_all[0, pl.ds(i, tall), :]
            for k in range(1, ysize):
                value = times(value, wd.at[k], False)
            dg[pl.ds(i, tall), :] = value

        tiles(width, tall, compose)

    @pl.when(feeds)
    def _():
        remote(dg, dz, sem_one, 0, 0, ahead).start()

    pl.when(inner)(lambda: prepare(wq, dg[:, :width], dg[:, width:]))

    def swept(i):
        rows = pl.ds(i, tall)
        value = vin[rows, :]
        y0[rows, :] = s0[rows, :] - times(value, we0, True)
        y1[rows, :] = s1[rows, :] + times(value, wc.at[y], True)

    tiles(vectors, tall, swept)

    for d in order:
        j = lax.rem(y + d, ysize)
        remote(e_all.at[j], e_all.at[j], sem_e, j, j, {"y": j}).wait_recv()
    values = [e_all[ysize - 1]]
    for k in reversed(range(ysize - 1)):
        values.append(times(values[-1], wd.at[k], True) + e_all[k])
    rg[...] = values[-1]

    @pl.when(last)
    def _():
        for s in range(SUBS):
            hop(rg, wz, sem_bz, s, behind).start()
        wz[...] = jnp.zeros_like(wz)

    @pl.when(feeds)
    def _():
        remote(rg, rz, sem_one, 1, 1, ahead).start()

    for k in range(ysize - 1):
        hand_out(k, values[ysize - 2 - k], wk, win, sem_r)

    @pl.when(jumps)
    def _():
        remote(dz, dz, sem_one, 0, 0, behind).wait_recv()
        prepare(wz1, dz[:, :width], dz[:, width:])

        def joint(i):
            tmp[pl.ds(i, tall), :] = times(dz[pl.ds(i, tall), :], wq, False)

        tiles(width, tall, joint)
        prepare(wj, tmp[:width, :width], tmp[:width, width:])
        remote(rz, rz, sem_one, 1, 1, behind).wait_recv()
        rj[...] = times(rg[...], wz1, True) + rz[...]

    def settle():
        @pl.when(y < ysize - 1)
        def _():
            for d in order:
                j = lax.rem(y + d, ysize)
                remote(piece(win, j), piece(win, j), sem_r, j, j, {"y": j}).wait_recv()

            def inner_part(i):
                rows = pl.ds(i, tall)
                y1[rows, :] = y1[rows, :] - times(win[rows, :], wf1, True)

            tiles(vectors, tall, inner_part)

        def first_part(i):
            rows = pl.ds(i, tall)
            y0[rows, :] = y0[rows, :] - times(y1[rows, :], wf0, True)

        tiles(vectors, tall, first_part)

        @pl.when(z < zsize - 1)
        def _():
            am[:, :width] = u_ref[0, 1, 0]
            am[:, width:] = -u_ref[0, 1, 1]
            for k in range(1, ysize):
                @pl.when(k > y)
                def _():
                    def longer(i):
                        am[pl.ds(i, tall), :] = times(am[pl.ds(i, tall), :], wd.at[k], False)

                    tiles(width, tall, longer)
            prepare(wa1, am[:, :width], am[:, width:])

            def both(i):
                rows = pl.ds(i, tall)
                upper = jnp.concatenate([u_ref[0, 0, 0, rows, :], -u_ref[0, 0, 1, rows, :]], axis=1)
                am[rows, :] = times(upper, wa1, False)

            tiles(width, tall, both)
            prepare(wa0, am[:, :width], am[:, width:])

    soon = z >= zsize // 2
    pl.when(jnp.logical_not(soon))(settle)

    two_on, two_back = along("z", z, 2, zsize), along("z", z, zsize - 2, zsize)

    def spread(s, k):
        rows = pl.ds(pl.multiple_of(y * chunk + s * sub, sub), sub)
        return remote(
            wz.at[pl.ds(s * sub, sub), :], wb.at[rows, :], sem_w, k * SUBS + s, y * SUBS + s, {"y": k}
        )

    for s in range(SUBS):
        rows = pl.ds(s * sub, sub)

        @pl.when(leaps)
        def _():
            hop(wz, wz, sem_far, s, two_on).wait_recv()

        @pl.when(jnp.logical_and(z < zsize - 1, jnp.logical_not(leaps)))
        def _():
            hop(wz, wz, sem_bz, s, ahead).wait_recv()

        @pl.when(steps)
        def _():
            wo[rows, :] = times(wz[rows, :], wq, True) + rg[rows, :]
            hop(wo, wz, sem_bz, s, behind).start()

        @pl.when(jumps)
        def _():
            rj[rows, :] = times(wz[rows, :], wj, True) + rj[rows, :]
            hop(rj, wz, sem_far, s, two_back).start()

        @pl.when(z < zsize - 1)
        def _():
            for d in order:
                spread(s, lax.rem(y + d, ysize)).start()

    @pl.when(jumps)
    def _():
        wo[...] = times(wz[...], wq, True) + rg[...]
        for s in range(SUBS):
            hop(wo, wz, sem_bz, s, behind).start()

    pl.when(soon)(settle)

    sibling = {"core": 1 - core}
    wreal, wimag = w_ref[0, 0], w_ref[0, 1]

    def rows_of(d):
        j = lax.rem(y + d, ysize)
        return j, pl.ds(pl.multiple_of(j * chunk, chunk), chunk)

    def over_x(turn, d):
        _, rows = rows_of(d)
        land(other.at[rows, :], sem_a, turn, sibling)
        pair = xs[core, rows, :] + other[rows, :]
        for j in range(xsize):
            cut[j, rows, :] = jnp.concatenate(
                [pair[:, j * part : (j + 1) * part], pair[:, width + j * part : width + (j + 1) * part]], axis=1
            )
        for step in nearest_first(xsize):
            go(
                cut.at[lax.rem(x + step, xsize), rows, :],
                got.at[x, rows, :],
                sem_x,
                turn * xsize + step,
                along("x", x, step, xsize),
            )
        got[x, rows, :] = cut[x, rows, :]

    turns = [0] + order
    for turn, d in enumerate(turns):
        j, rows = rows_of(d)

        @pl.when(z < zsize - 1)
        def _():
            if d:
                for s in range(SUBS):
                    part_rows = pl.ds(pl.multiple_of(j * chunk + s * sub, sub), sub)
                    remote(
                        wb.at[part_rows, :], wb.at[part_rows, :], sem_w, j * SUBS + s, j * SUBS + s, {"y": j}
                    ).wait_recv()
                inflow = wb[rows, :]
            else:
                inflow = wz[...]
            y1[rows, :] = y1[rows, :] - times(inflow, wa1, True)
            y0[rows, :] = y0[rows, :] + times(inflow, wa0, True)

        for n, solved in enumerate((y0, y1)):
            real, imag = solved[rows, :width], solved[rows, width:]
            xs[n, rows, :width] = wreal * real - wimag * imag
            xs[n, rows, width:] = wreal * imag + wimag * real
        go(xs.at[1 - core, rows, :], other.at[rows, :], sem_a, turn, sibling)
        if turn:
            over_x(turn - 1, turns[turn - 1])
    over_x(len(turns) - 1, turns[-1])
    for turn, d in enumerate(turns):
        _, rows = rows_of(d)
        for step in nearest_first(xsize):
            j = back(x, step, xsize)
            land(got.at[j, rows, :], sem_x, turn * xsize + step, {"x": j})
    basis = got[0]
    for j in range(1, xsize):
        basis = basis + got[j]
    real, imag = basis[:, :part], basis[:, part:]
    lh, ll = halves(basis)
    rh, rl = halves(jnp.concatenate([real + imag, imag - real], axis=1))
    gram[...] = dot(lh, rh, True) + dot(ll, rh, True) + dot(lh, rl, True)

    for d in range(1, poles):
        p, device = pole_of(d)
        go(lines(gram, p, own), g1.at[pole], sem_1, d, device)
    g1[pole] = lines(gram, pole, own)[...]
    for d in range(1, poles):
        land(g1.at[back(pole, d, poles)], sem_1, d, pole_of(poles - d)[1])
    value = g1[0]
    for j in range(1, poles):
        value = value + g1[j]
    t1[...] = value
    for d in nearest_first(ysize):
        j = lax.rem(y + d, ysize)
        go(lines(t1, j, line), g2.at[y], sem_2, d, {"y": j})
    g2[y] = lines(t1, y, line)[...]
    for d in nearest_first(ysize):
        j = back(y, d, ysize)
        land(g2.at[j], sem_2, d, {"y": j})
    value = g2[0]
    for j in range(1, ysize):
        value = value + g2[j]
    g3[z] = value
    for d in nearest_first(zsize):
        go(g3.at[z], g3.at[z], sem_3, d, {"z": lax.rem(z + d, zsize)})
    for d in nearest_first(zsize):
        j = back(z, d, zsize)
        land(g3.at[j], sem_3, d, {"z": j})
    value = g3[0]
    for j in range(1, zsize):
        value = value + g3[j]
    lines(h2, y, line)[...] = value
    for d in nearest_first(ysize):
        go(lines(h2, y, line), lines(h2, y, line), sem_4, d, {"y": lax.rem(y + d, ysize)})
    for d in nearest_first(ysize):
        j = back(y, d, ysize)
        land(lines(h2, j, line), sem_4, d, {"y": j})
    lines(h1, pole, own)[...] = h2[...]
    for d in range(1, poles):
        go(h2, lines(h1, pole, own), sem_5, d, pole_of(d)[1])
    for d in range(1, poles):
        land(lines(h1, back(pole, d, poles), own), sem_5, d, pole_of(poles - d)[1])

    whole = h1[...]
    frob = jnp.sqrt(jnp.sum(whole * whole))
    flip = whole.T
    scale = -0.25 / frob
    eye = (
        lax.broadcasted_iota(jnp.int32, (vectors, vectors), 0)
        == lax.broadcasted_iota(jnp.int32, (vectors, vectors), 1)
    )
    first = jnp.where(eye, 1.5, 0.0) + scale * (whole + flip)
    minus = -scale * (whole - flip)
    prepare(wn.at[0], first, minus)
    zs[0, :, :vectors] = first
    zs[0, :, vectors:] = minus

    def square(i):
        rows = pl.ds(i, tall)
        zs[1, rows, :] = times(zs[0, rows, :], wn.at[0], False)

    tiles(vectors, tall, square)
    prepare(
        wn.at[1],
        zs[1, :, :vectors] - 1.5 * zs[0, :, :vectors],
        zs[1, :, vectors:] - 1.5 * zs[0, :, vectors:],
    )
    size = jnp.sqrt(total_rows / frob)
    stacked = jnp.concatenate(
        [basis, jnp.concatenate([-imag, real], axis=1)], axis=0
    )
    qh, ql = halves(stacked)
    turned[0] = qh
    turned[1] = ql

    def rotate(i):
        rows = pl.ds(i, tall)
        mix = 1.5 * zs[0, rows, :] + times(zs[1, rows, :], wn.at[1], False)
        spun[rows, :] = times(mix, turned, False) * size

    tiles(vectors, tall, rotate)
    for d in range(1, poles):
        p, device = pole_of(d)
        go(lines(spun, p, own), fin.at[pole], sem_6, d, device)
    fin[pole] = lines(spun, pole, own)[...]
    for d in range(1, poles):
        land(fin.at[back(pole, d, poles)], sem_6, d, pole_of(poles - d)[1])
    slots = [2 * j + n for n in range(2) for j in range(xsize)]
    out_ref[0] = jnp.concatenate([fin[k][:, :part] for k in slots], axis=1)
    out_ref[1] = jnp.concatenate([fin[k][:, part:] for k in slots], axis=1)
    for copy in sent:
        copy.wait_send()
    if ysize > 2:
        for copy in (*onward(c_all, sem_c), *onward(d_all, sem_d)):
            copy.wait_send()
    handed_out(vk, vin, sem_v, ysize)
    handed_out(wk, win, sem_r, ysize - 1)
    for d in order:
        j, rows = rows_of(d)
        remote(eo.at[rows, :], e_all.at[y], sem_e, j, y, {"y": j}).wait_send()
    for s in range(SUBS):
        @pl.when(z < zsize - 1)
        def _():
            hop(vo, vz, sem_fz, s, ahead).wait_send()

        @pl.when(jnp.logical_or(last, jnp.logical_or(steps, jumps)))
        def _():
            hop(wo, wz, sem_bz, s, behind).wait_send()

        @pl.when(jumps)
        def _():
            hop(rj, wz, sem_far, s, two_back).wait_send()

        @pl.when(z < zsize - 1)
        def _():
            for d in order:
                spread(s, lax.rem(y + d, ysize)).wait_send()

    @pl.when(feeds)
    def _():
        remote(dg, dz, sem_one, 0, 0, ahead).wait_send()
        remote(rg, rz, sem_one, 1, 1, ahead).wait_send()


def shards(sizes, subspace, pivots, lower_blocks, upper_blocks, pole_weights):
    xsize, zsize, ysize = sizes
    vectors, width = subspace.shape[1], pivots.shape[-1]
    wide = 2 * width
    chunk = vectors // ysize
    poles = 2 * xsize
    part = width // xsize
    own = vectors // poles
    line = own // ysize
    total_rows = float(2 * width * ysize * zsize)

    def dma(count):
        return pltpu.SemaphoreType.DMA((2, count))

    def f32(*shape):
        return pltpu.VMEM(shape, F32)

    def prepared(*counts):
        return pltpu.VMEM((*counts, 2, wide, wide), BF16)

    anywhere = pl.BlockSpec(memory_space=pl.ANY)
    return pl.pallas_call(
        functools.partial(step_kernel, (xsize, zsize, ysize), total_rows),
        out_shape=jax.ShapeDtypeStruct((2, own, wide), F32),
        in_specs=[anywhere] * 4 + [pl.BlockSpec(memory_space=pltpu.SMEM)],
        out_specs=pl.BlockSpec(memory_space=pltpu.VMEM),
        scratch_shapes=[f32(*a.shape) for a in (subspace, pivots, lower_blocks, upper_blocks)]
        + [prepared()] * 4
        + [prepared(2)]
        + [prepared(ysize)] * 2
        + [prepared()] * 7
        + [f32(ysize, width, wide)] * 2
        + [f32(ysize, chunk, wide)] * 2
        + [f32(chunk, wide)] * 4
        + [f32(vectors, wide)] * 10
        + [f32(width, wide)] * 3
        + [f32(chunk, wide)] * 4
        + [f32(ysize, chunk, wide)] * 2
        + [
            f32(2, vectors, wide),
            f32(vectors, wide),
            f32(xsize, vectors, 2 * part),
            f32(xsize, vectors, 2 * part),
            f32(vectors, vectors),
            f32(poles, own, vectors),
            f32(own, vectors),
            f32(ysize, line, vectors),
            f32(zsize, line, vectors),
            f32(own, vectors),
            f32(vectors, vectors),
            pltpu.VMEM((2, 2, 2 * vectors, 2 * vectors), BF16),
            f32(2, vectors, 2 * vectors),
            pltpu.VMEM((2, 2 * vectors, 2 * part), BF16),
            f32(vectors, 2 * part),
            f32(poles, own, 2 * part),
            pltpu.SemaphoreType.DMA((4,)),
            dma(6),
        ]
        + [dma(ysize), dma(6)]
        + [dma(ysize)] * 3
        + [dma(ysize * SUBS)]
        + [dma(SUBS)] * 2
        + [dma(2), dma(SUBS)]
        + [
            dma(ysize),
            dma(ysize * xsize),
            dma(poles),
            dma(ysize),
            dma(zsize),
            dma(ysize),
            dma(poles),
            dma(poles),
        ],
        compiler_params=pltpu.CompilerParams(
            collective_id=0, has_side_effects=True, vmem_limit_bytes=60 * 2**20
        ),
        name="step",
    )(subspace, pivots, lower_blocks, upper_blocks, pole_weights)


def build(mesh, sizes):
    xsize, zsize, ysize = sizes
    torus = Mesh(mesh.devices.reshape(xsize, 2, zsize, ysize), AXES)
    pole, rows = ("x", "core"), ("z", "y")
    return jax.shard_map(
        functools.partial(shards, sizes),
        mesh=torus,
        in_specs=(
            P(None, None, rows),
            P(pole, rows, None, None, None),
            P(pole, rows, None, None, None),
            P(pole, rows, None, None, None),
            P(pole, None),
        ),
        out_specs=P(None, pole, rows),
        check_vma=False,
    )


def solution(mesh):
    return build(mesh, (mesh.shape["pole"] // 2, mesh.shape["rows"] // 4, 4))
```

```python
import functools

import jax
import jax.numpy as jnp
from jax import lax
from jax.experimental import pallas as pl
from jax.experimental.pallas import tpu as pltpu
from jax.sharding import Mesh
from jax.sharding import PartitionSpec as P

F32 = jnp.float32
BF16 = jnp.bfloat16
MESH_ID = pl.DeviceIdType.MESH
AXES = ("x", "core", "z", "y")
SUBS = 4


def halves(value):
    high = value.astype(BF16)
    return high, (value - high.astype(F32)).astype(BF16)


def dot(left, right, trans):
    dims = (((1,), (1 if trans else 0,)), ((), ()))
    return lax.dot_general(left, right, dims, preferred_element_type=F32)


def times(rows, weights, trans):
    high, low = halves(rows)
    count = rows.shape[0]
    both = dot(jnp.concatenate([high, low], axis=0), weights[0], trans)
    return both[:count] + both[count:] + dot(high, weights[1], trans)


def prepare(weights, real, minus):
    height, width = real.shape
    for part, (r, m) in enumerate(zip(halves(real), halves(minus))):
        weights[part, :height, :width] = r
        weights[part, :height, width:] = m
        weights[part, height:, :width] = -m
        weights[part, height:, width:] = r


def tiles(count, size, body):
    if count == size:
        body(0)
        return

    def step(i, carry):
        body(pl.multiple_of(i * size, size))
        return carry

    lax.fori_loop(0, count // size, step, 0)


def remote(src, dst, sems, slot_out, slot_in, device):
    return pltpu.make_async_remote_copy(
        src_ref=src,
        dst_ref=dst,
        send_sem=sems.at[0, slot_out],
        recv_sem=sems.at[1, slot_in],
        device_id=device,
        device_id_type=MESH_ID,
    )


def nearest_first(count):
    return sorted(range(1, count), key=lambda d: min(d, count - d))


def step_kernel(
    dims, total_rows, f_hbm, g_hbm, e_hbm, u_hbm, w_ref, out_ref,
    f_ref, g_ref, e_ref, u_ref,
    we0, we1, wf0, wf1, wg, wc, wd, wp, wq, wh, wj, wz1, wa0, wa1,
    c_all, d_all, b_all, e_all, qg, rg, rj, rz, s0, s1, y0, y1, e0, eo, vin, win, tmp, wb, dg, dz, am,
    vz, vo, wz, wo, vk, wk,
    xs, other, cut, got, gram, g1, t1, g2, g3, h2, h1, wn, zs, turned, qall,
    sem_in, sem_c, sem_b, sem_d, sem_v, sem_e, sem_r, sem_w, sem_fz, sem_bz, sem_one, sem_far,
    sem_a, sem_x, sem_1, sem_2, sem_3, sem_4, sem_5, sem_q,
):
    xsize, zsize, ysize = dims
    x, core, z, y = (lax.axis_index(a) for a in AXES)
    poles = 2 * xsize
    pole = x * 2 + core
    vectors, width = f_ref.shape[1], g_ref.shape[-1]
    chunk = vectors // ysize
    sub = chunk // SUBS
    tall = min(128, width)
    part = width // xsize
    own = vectors // poles
    line = own // ysize
    order = nearest_first(ysize)

    def pole_of(d):
        p = lax.rem(pole + d, poles)
        return p, {"x": p // 2, "core": lax.rem(p, 2)}

    def along(axis, me, d, size):
        return {axis: lax.rem(me + d, size)}

    barrier = pltpu.get_barrier_semaphore()
    for d in range(1, ysize):
        pl.semaphore_signal(barrier, inc=1, device_id=along("y", y, d, ysize), device_id_type=MESH_ID)
    for d in range(1, zsize):
        pl.semaphore_signal(barrier, inc=1, device_id=along("z", z, d, zsize), device_id_type=MESH_ID)
    for d in range(1, poles):
        pl.semaphore_signal(barrier, inc=1, device_id=pole_of(d)[1], device_id_type=MESH_ID)

    loads = [
        pltpu.make_async_copy(a, b, sem_in.at[i])
        for i, (a, b) in enumerate(((e_hbm, e_ref), (u_hbm, u_ref), (g_hbm, g_ref), (f_hbm, f_ref)))
    ]
    for load in loads:
        load.start()

    sent = []

    def go(src, dst, sems, d, device):
        copy = remote(src, dst, sems, d, d, device)
        copy.start()
        sent.append(copy)

    def land(dst, sems, d, device):
        remote(dst, dst, sems, d, d, device).wait_recv()

    def back(me, d, size):
        return lax.rem(me + size - d, size)

    def lines(ref, j, count):
        return ref.at[pl.ds(pl.multiple_of(j * count, count), count), :]

    def piece(ref, j):
        return lines(ref, j, chunk)

    loads[0].wait()
    prepare(we0, e_ref[0, 0, 0], -e_ref[0, 0, 1])

    def forward_map(i):
        rows = jnp.concatenate([e_ref[0, 1, 0, pl.ds(i, tall), :], -e_ref[0, 1, 1, pl.ds(i, tall), :]], axis=1)
        c_all[y, pl.ds(i, tall), :] = times(rows, we0, False)

    tiles(width, tall, forward_map)
    pl.semaphore_wait(barrier, ysize + zsize + poles - 3)

    half = width // 2
    right, left = along("y", y, 1, ysize), along("y", y, ysize - 1, ysize)
    before, beyond, far = back(y, 1, ysize), lax.rem(y + 1, ysize), lax.rem(y + 2, ysize)

    def half_of(store, k, h):
        return store.at[k, pl.ds(h * half, half), :]

    def share(store, sems):
        for slot, h, device in ((0, 0, right), (2, 1, left), (1, 1, right), (3, 0, left)):
            if ysize > 2 or slot < 2:
                go(half_of(store, y, h), half_of(store, y, h), sems, slot, device)

    def onward(store, sems):
        first, second = half_of(store, before, 0), half_of(store, beyond, 1)
        return remote(first, first, sems, 4, 4, right), remote(second, second, sems, 5, 5, left)

    def pass_on(store, sems):
        land(half_of(store, before, 0), sems, 0, left)
        if ysize > 2:
            to_right, to_left = onward(store, sems)
            to_right.start()
            land(half_of(store, beyond, 1), sems, 2, right)
            to_left.start()

    def take(store, sems, weights):
        land(half_of(store, before, 1), sems, 1, left)
        prepare(weights.at[before], store[before, :, :width], store[before, :, width:])
        if ysize > 2:
            land(half_of(store, beyond, 0), sems, 3, right)
            prepare(weights.at[beyond], store[beyond, :, :width], store[beyond, :, width:])
            land(half_of(store, far, 0), sems, 4, left)
            land(half_of(store, far, 1), sems, 5, right)
            prepare(weights.at[far], store[far, :, :width], store[far, :, width:])

    share(c_all, sem_c)

    loads[2].wait()
    prepare(wg.at[0], g_ref[0, 0, 0], -g_ref[0, 0, 1])
    prepare(wg.at[1], g_ref[0, 1, 0], -g_ref[0, 1, 1])
    prepare(we1, e_ref[0, 1, 0], -e_ref[0, 1, 1])
    loads[3].wait()

    def local(i):
        rows = pl.ds(i, tall)
        first = jnp.concatenate([f_ref[0, rows, :width], f_ref[1, rows, :width]], axis=1)
        second = jnp.concatenate([f_ref[0, rows, width:], f_ref[1, rows, width:]], axis=1)
        start = times(first, wg.at[0], True)
        s0[rows, :] = start
        s1[rows, :] = times(second, wg.at[1], True) - times(start, we1, True)

    tiles(vectors, tall, local)
    for d in order:
        go(piece(s1, lax.rem(y + d, ysize)), b_all.at[y], sem_b, d, along("y", y, d, ysize))
    b_all[y] = piece(s1, y)[...]

    loads[1].wait()
    prepare(wf1, u_ref[0, 1, 0], -u_ref[0, 1, 1])
    prepare(wf0, u_ref[0, 0, 0], -u_ref[0, 0, 1])
    prepare(wc.at[y], c_all[y, :, :width], c_all[y, :, width:])

    def backward_map(i):
        rows = pl.ds(i, tall)
        upper = jnp.concatenate([u_ref[0, 0, 0, rows, :], -u_ref[0, 0, 1, rows, :]], axis=1)
        d_all[y, rows, :] = times(upper, wf1, False)
        lower = jnp.concatenate([e_ref[0, 0, 0, rows, :], -e_ref[0, 0, 1, rows, :]], axis=1)
        tmp[rows, :] = -lower - times(upper, wc.at[y], False)

    tiles(width, tall, backward_map)
    pass_on(c_all, sem_c)
    prepare(wh, tmp[:width, :width], tmp[:width, width:])

    def local_ends(i):
        rows = pl.ds(i, tall)
        e0[rows, :] = s0[rows, :] - times(s1[rows, :], wf0, True)

    tiles(vectors, tall, local_ends)

    take(c_all, sem_c, wc)
    for d in order:
        land(b_all.at[back(y, d, ysize)], sem_b, d, along("y", y, ysize - d, ysize))
    share(d_all, sem_d)

    value = b_all[0]
    for k in range(1, ysize):
        value = times(value, wc.at[k], True) + b_all[k]
    qg[...] = value

    def hop(out, into, sems, s, device):
        return remote(out.at[pl.ds(s * sub, sub), :], into.at[pl.ds(s * sub, sub), :], sems, s, s, device)

    ahead, behind = along("z", z, 1, zsize), along("z", z, zsize - 1, zsize)

    @pl.when(z == 0)
    def _():
        for s in range(SUBS):
            hop(qg, vz, sem_fz, s, ahead).start()
        vz[...] = jnp.zeros_like(vz)

    @pl.when(jnp.logical_and(z > 0, z < zsize - 1))
    def _():
        def group_forward(i):
            value = c_all[ysize - 1, pl.ds(i, tall), :]
            for k in reversed(range(ysize - 1)):
                value = times(value, wc.at[k], False)
            tmp[pl.ds(i, tall), :] = value

        tiles(width, tall, group_forward)
        prepare(wp, tmp[:width, :width].T, -tmp[:width, width:].T)

    early = z < 3
    pl.when(jnp.logical_not(early))(lambda: pass_on(d_all, sem_d))

    for s in range(SUBS):
        rows = pl.ds(s * sub, sub)

        @pl.when(z > 0)
        def _():
            hop(vz, vz, sem_fz, s, behind).wait_recv()

        @pl.when(jnp.logical_and(z > 0, z < zsize - 1))
        def _():
            vo[rows, :] = times(vz[rows, :], wp, False) + qg[rows, :]
            hop(vo, vz, sem_fz, s, ahead).start()

    def hand_out(k, value, staging, into, sems):
        staging[k] = value

        @pl.when(y == k)
        def _():
            piece(into, y)[...] = value

        @pl.when(y != k)
        def _():
            remote(staging.at[k], piece(into, y), sems, k, y, {"y": k}).start()

    def handed_out(staging, into, sems, count):
        for k in range(count):
            @pl.when(y != k)
            def _():
                remote(staging.at[k], piece(into, y), sems, k, y, {"y": k}).wait_send()

    value = vz[...]
    for k in range(ysize):
        hand_out(k, value, vk, vin, sem_v)
        if k < ysize - 1:
            value = times(value, wc.at[k], True) + b_all[k]

    pl.when(early)(lambda: pass_on(d_all, sem_d))

    for d in [0] + order:
        j = lax.rem(y + d, ysize)
        rows = pl.ds(pl.multiple_of(j * chunk, chunk), chunk)
        if d:
            remote(vin.at[rows, :], vin.at[rows, :], sem_v, j, j, {"y": j}).wait_recv()
        ends = e0[rows, :] + times(vin[rows, :], wh, True)
        if d:
            eo[rows, :] = ends
            remote(eo.at[rows, :], e_all.at[y], sem_e, j, y, {"y": j}).start()
        else:
            e_all[y] = ends

    prepare(wd.at[y], d_all[y, :, :width], d_all[y, :, width:])
    take(d_all, sem_d, wd)
    even = lax.rem(z, 2) == 0
    jumps = jnp.logical_and(even, jnp.logical_and(z >= 2, z <= zsize - 4))
    feeds = jnp.logical_and(jnp.logical_not(even), z <= zsize - 5)
    leaps = jnp.logical_and(even, z <= zsize - 6)
    last = z == zsize - 1
    inner = jnp.logical_and(z > 0, z < zsize - 1)
    steps = jnp.logical_and(inner, z >= zsize - 3)

    @pl.when(inner)
    def _():
        def compose(i):
            value = d_all[0, pl.ds(i, tall), :]
            for k in range(1, ysize):
                value = times(value, wd.at[k], False)
            dg[pl.ds(i, tall), :] = value

        tiles(width, tall, compose)

    @pl.when(feeds)
    def _():
        remote(dg, dz, sem_one, 0, 0, ahead).start()

    pl.when(jumps)(lambda: prepare(wq, dg[:, :width], dg[:, width:]))
    pl.when(steps)(lambda: prepare(wq, dg[:, :width].T, -dg[:, width:].T))

    def swept(i):
        rows = pl.ds(i, tall)
        value = vin[rows, :]
        y0[rows, :] = s0[rows, :] - times(value, we0, True)
        y1[rows, :] = s1[rows, :] + times(value, wc.at[y], True)

    tiles(vectors, tall, swept)

    for d in order:
        j = lax.rem(y + d, ysize)
        remote(e_all.at[j], e_all.at[j], sem_e, j, j, {"y": j}).wait_recv()
    values = [e_all[ysize - 1]]
    for k in reversed(range(ysize - 1)):
        values.append(times(values[-1], wd.at[k], True) + e_all[k])
    rg[...] = values[-1]

    @pl.when(last)
    def _():
        for s in range(SUBS):
            hop(rg, wz, sem_bz, s, behind).start()
        wz[...] = jnp.zeros_like(wz)

    @pl.when(feeds)
    def _():
        remote(rg, rz, sem_one, 1, 1, ahead).start()

    for k in range(ysize - 1):
        hand_out(k, values[ysize - 2 - k], wk, win, sem_r)

    @pl.when(jumps)
    def _():
        remote(dz, dz, sem_one, 0, 0, behind).wait_recv()
        prepare(wz1, dz[:, :width], dz[:, width:])

        def joint(i):
            tmp[pl.ds(i, tall), :] = times(dz[pl.ds(i, tall), :], wq, False)

        tiles(width, tall, joint)
        prepare(wj, tmp[:width, :width].T, -tmp[:width, width:].T)
        remote(rz, rz, sem_one, 1, 1, behind).wait_recv()
        rj[...] = times(rg[...], wz1, True) + rz[...]

    def settle():
        @pl.when(y < ysize - 1)
        def _():
            for d in order:
                j = lax.rem(y + d, ysize)
                remote(piece(win, j), piece(win, j), sem_r, j, j, {"y": j}).wait_recv()

            def inner_part(i):
                rows = pl.ds(i, tall)
                y1[rows, :] = y1[rows, :] - times(win[rows, :], wf1, True)

            tiles(vectors, tall, inner_part)

        def first_part(i):
            rows = pl.ds(i, tall)
            y0[rows, :] = y0[rows, :] - times(y1[rows, :], wf0, True)

        tiles(vectors, tall, first_part)

        @pl.when(z < zsize - 1)
        def _():
            am[:, :width] = u_ref[0, 1, 0]
            am[:, width:] = -u_ref[0, 1, 1]
            for k in range(1, ysize):
                @pl.when(k > y)
                def _():
                    def longer(i):
                        am[pl.ds(i, tall), :] = times(am[pl.ds(i, tall), :], wd.at[k], False)

                    tiles(width, tall, longer)
            prepare(wa1, am[:, :width], am[:, width:])

            def both(i):
                rows = pl.ds(i, tall)
                upper = jnp.concatenate([u_ref[0, 0, 0, rows, :], -u_ref[0, 0, 1, rows, :]], axis=1)
                am[rows, :] = times(upper, wa1, False)

            tiles(width, tall, both)
            prepare(wa0, am[:, :width], am[:, width:])

    soon = z >= zsize // 2
    pl.when(jnp.logical_not(soon))(settle)

    two_on, two_back = along("z", z, 2, zsize), along("z", z, zsize - 2, zsize)

    def spread(s, k):
        rows = pl.ds(pl.multiple_of(y * chunk + s * sub, sub), sub)
        return remote(
            wz.at[pl.ds(s * sub, sub), :], wb.at[rows, :], sem_w, k * SUBS + s, y * SUBS + s, {"y": k}
        )

    for s in range(SUBS):
        rows = pl.ds(s * sub, sub)

        @pl.when(leaps)
        def _():
            hop(wz, wz, sem_far, s, two_on).wait_recv()

        @pl.when(jnp.logical_and(z < zsize - 1, jnp.logical_not(leaps)))
        def _():
            hop(wz, wz, sem_bz, s, ahead).wait_recv()

        @pl.when(steps)
        def _():
            wo[rows, :] = times(wz[rows, :], wq, False) + rg[rows, :]
            hop(wo, wz, sem_bz, s, behind).start()

        @pl.when(jumps)
        def _():
            rj[rows, :] = times(wz[rows, :], wj, False) + rj[rows, :]
            hop(rj, wz, sem_far, s, two_back).start()

        @pl.when(z < zsize - 1)
        def _():
            for d in order:
                spread(s, lax.rem(y + d, ysize)).start()

    @pl.when(jumps)
    def _():
        wo[...] = times(wz[...], wq, True) + rg[...]
        for s in range(SUBS):
            hop(wo, wz, sem_bz, s, behind).start()

    pl.when(soon)(settle)

    sibling = {"core": 1 - core}
    wreal, wimag = w_ref[0, 0], w_ref[0, 1]

    def rows_of(d):
        j = lax.rem(y + d, ysize)
        return j, pl.ds(pl.multiple_of(j * chunk, chunk), chunk)

    def over_x(turn, d):
        _, rows = rows_of(d)
        land(other.at[rows, :], sem_a, turn, sibling)
        pair = xs[core, rows, :] + other[rows, :]
        for j in range(xsize):
            cut[j, rows, :] = jnp.concatenate(
                [pair[:, j * part : (j + 1) * part], pair[:, width + j * part : width + (j + 1) * part]], axis=1
            )
        for step in nearest_first(xsize):
            go(
                cut.at[lax.rem(x + step, xsize), rows, :],
                got.at[x, rows, :],
                sem_x,
                turn * xsize + step,
                along("x", x, step, xsize),
            )
        got[x, rows, :] = cut[x, rows, :]

    turns = [0] + order
    for turn, d in enumerate(turns):
        j, rows = rows_of(d)

        @pl.when(z < zsize - 1)
        def _():
            if d:
                for s in range(SUBS):
                    part_rows = pl.ds(pl.multiple_of(j * chunk + s * sub, sub), sub)
                    remote(
                        wb.at[part_rows, :], wb.at[part_rows, :], sem_w, j * SUBS + s, j * SUBS + s, {"y": j}
                    ).wait_recv()
                inflow = wb[rows, :]
            else:
                inflow = wz[...]
            y1[rows, :] = y1[rows, :] - times(inflow, wa1, True)
            y0[rows, :] = y0[rows, :] + times(inflow, wa0, True)

        for n, solved in enumerate((y0, y1)):
            real, imag = solved[rows, :width], solved[rows, width:]
            xs[n, rows, :width] = wreal * real - wimag * imag
            xs[n, rows, width:] = wreal * imag + wimag * real
        go(xs.at[1 - core, rows, :], other.at[rows, :], sem_a, turn, sibling)
        if turn:
            over_x(turn - 1, turns[turn - 1])
    over_x(len(turns) - 1, turns[-1])
    for turn, d in enumerate(turns):
        _, rows = rows_of(d)
        for step in nearest_first(xsize):
            j = back(x, step, xsize)
            land(got.at[j, rows, :], sem_x, turn * xsize + step, {"x": j})
    basis = got[0]
    for j in range(1, xsize):
        basis = basis + got[j]
    qall[core, x] = basis
    go(qall.at[core, x], qall.at[core, x], sem_q, 0, sibling)
    land(qall.at[1 - core, x], sem_q, 0, sibling)
    low_rows = pl.ds(pl.multiple_of(core * (vectors // 2), vectors // 2), vectors // 2)
    left_side = jnp.concatenate([qall[n, x, low_rows, :] for n in range(2)], axis=1)
    right_side = []
    for n in range(2):
        real, imag = qall[n, x, :, :part], qall[n, x, :, part:]
        right_side += [real + imag, imag - real]
    lh, ll = halves(left_side)
    rh, rl = halves(jnp.concatenate(right_side, axis=1))
    gram[...] = dot(lh, rh, True) + dot(ll, rh, True) + dot(lh, rl, True)
    for step in nearest_first(xsize):
        j = lax.rem(x + step, xsize)
        go(lines(gram, j, own), g1.at[x], sem_1, step, {"x": j})
    g1[x] = lines(gram, x, own)[...]
    for step in nearest_first(xsize):
        go(qall.at[core, x], qall.at[core, x], sem_q, step, along("x", x, step, xsize))
    for step in nearest_first(xsize):
        j = back(x, step, xsize)
        land(g1.at[j], sem_1, step, {"x": j})
    value = g1[0]
    for j in range(1, xsize):
        value = value + g1[j]
    t1[...] = value
    for d in nearest_first(ysize):
        j = lax.rem(y + d, ysize)
        go(lines(t1, j, line), g2.at[y], sem_2, d, {"y": j})
    g2[y] = lines(t1, y, line)[...]
    for d in nearest_first(ysize):
        j = back(y, d, ysize)
        land(g2.at[j], sem_2, d, {"y": j})
    value = g2[0]
    for j in range(1, ysize):
        value = value + g2[j]
    g3[z] = value
    for d in nearest_first(zsize):
        go(g3.at[z], g3.at[z], sem_3, d, {"z": lax.rem(z + d, zsize)})
    for d in nearest_first(zsize):
        j = back(z, d, zsize)
        land(g3.at[j], sem_3, d, {"z": j})
    value = g3[0]
    for j in range(1, zsize):
        value = value + g3[j]
    lines(h2, y, line)[...] = value
    for d in nearest_first(ysize):
        go(lines(h2, y, line), lines(h2, y, line), sem_4, d, {"y": lax.rem(y + d, ysize)})
    for d in nearest_first(ysize):
        j = back(y, d, ysize)
        land(lines(h2, j, line), sem_4, d, {"y": j})
    place = core * xsize + x
    lines(h1, place, own)[...] = h2[...]
    for d in range(1, poles):
        go(h2, lines(h1, place, own), sem_5, d, pole_of(d)[1])
    for step in nearest_first(xsize):
        j = back(x, step, xsize)
        land(qall.at[core, j], sem_q, step, {"x": j})
        go(qall.at[core, j], qall.at[core, j], sem_q, xsize + step, sibling)
    for step in nearest_first(xsize):
        land(qall.at[1 - core, back(x, step, xsize)], sem_q, xsize + step, sibling)
    prepare(
        turned,
        jnp.concatenate([qall[n, j, :, :part] for n in range(2) for j in range(xsize)], axis=1),
        jnp.concatenate([qall[n, j, :, part:] for n in range(2) for j in range(xsize)], axis=1),
    )
    for d in range(1, poles):
        p, device = pole_of(poles - d)
        land(lines(h1, lax.rem(p, 2) * xsize + p // 2, own), sem_5, d, device)

    whole = h1[...]
    frob = jnp.sqrt(jnp.sum(whole * whole))
    flip = whole.T
    scale = -0.25 / frob
    eye = (
        lax.broadcasted_iota(jnp.int32, (vectors, vectors), 0)
        == lax.broadcasted_iota(jnp.int32, (vectors, vectors), 1)
    )
    first = jnp.where(eye, 1.5, 0.0) + scale * (whole + flip)
    minus = -scale * (whole - flip)
    prepare(wn.at[0], first, minus)
    zs[0, :, :vectors] = first
    zs[0, :, vectors:] = minus

    def square(i):
        rows = pl.ds(i, tall)
        zs[1, rows, :] = times(zs[0, rows, :], wn.at[0], False)

    tiles(vectors, tall, square)
    prepare(
        wn.at[1],
        zs[1, :, :vectors] - 1.5 * zs[0, :, :vectors],
        zs[1, :, vectors:] - 1.5 * zs[0, :, vectors:],
    )
    size = jnp.sqrt(total_rows / frob)
    rows = pl.ds(pl.multiple_of(pole * own, own), own)
    mix = 1.5 * zs[0, rows, :] + times(zs[1, rows, :], wn.at[1], False)
    turned_rows = times(mix, turned, False) * size
    out_ref[0] = turned_rows[:, : 2 * width]
    out_ref[1] = turned_rows[:, 2 * width :]
    for copy in sent:
        copy.wait_send()
    if ysize > 2:
        for copy in (*onward(c_all, sem_c), *onward(d_all, sem_d)):
            copy.wait_send()
    handed_out(vk, vin, sem_v, ysize)
    handed_out(wk, win, sem_r, ysize - 1)
    for d in order:
        j, rows = rows_of(d)
        remote(eo.at[rows, :], e_all.at[y], sem_e, j, y, {"y": j}).wait_send()
    for s in range(SUBS):
        @pl.when(z < zsize - 1)
        def _():
            hop(vo, vz, sem_fz, s, ahead).wait_send()

        @pl.when(jnp.logical_or(last, jnp.logical_or(steps, jumps)))
        def _():
            hop(wo, wz, sem_bz, s, behind).wait_send()

        @pl.when(jumps)
        def _():
            hop(rj, wz, sem_far, s, two_back).wait_send()

        @pl.when(z < zsize - 1)
        def _():
            for d in order:
                spread(s, lax.rem(y + d, ysize)).wait_send()

    @pl.when(feeds)
    def _():
        remote(dg, dz, sem_one, 0, 0, ahead).wait_send()
        remote(rg, rz, sem_one, 1, 1, ahead).wait_send()


def shards(sizes, subspace, pivots, lower_blocks, upper_blocks, pole_weights):
    xsize, zsize, ysize = sizes
    vectors, width = subspace.shape[1], pivots.shape[-1]
    wide = 2 * width
    chunk = vectors // ysize
    poles = 2 * xsize
    part = width // xsize
    own = vectors // poles
    line = own // ysize
    total_rows = float(2 * width * ysize * zsize)

    def dma(count):
        return pltpu.SemaphoreType.DMA((2, count))

    def f32(*shape):
        return pltpu.VMEM(shape, F32)

    def prepared(*counts):
        return pltpu.VMEM((*counts, 2, wide, wide), BF16)

    anywhere = pl.BlockSpec(memory_space=pl.ANY)
    return pl.pallas_call(
        functools.partial(step_kernel, (xsize, zsize, ysize), total_rows),
        out_shape=jax.ShapeDtypeStruct((2, own, wide), F32),
        in_specs=[anywhere] * 4 + [pl.BlockSpec(memory_space=pltpu.SMEM)],
        out_specs=pl.BlockSpec(memory_space=pltpu.VMEM),
        scratch_shapes=[f32(*a.shape) for a in (subspace, pivots, lower_blocks, upper_blocks)]
        + [prepared()] * 4
        + [prepared(2)]
        + [prepared(ysize)] * 2
        + [prepared()] * 7
        + [f32(ysize, width, wide)] * 2
        + [f32(ysize, chunk, wide)] * 2
        + [f32(chunk, wide)] * 4
        + [f32(vectors, wide)] * 10
        + [f32(width, wide)] * 3
        + [f32(chunk, wide)] * 4
        + [f32(ysize, chunk, wide)] * 2
        + [
            f32(2, vectors, wide),
            f32(vectors, wide),
            f32(xsize, vectors, 2 * part),
            f32(xsize, vectors, 2 * part),
            f32(vectors // 2, vectors),
            f32(xsize, own, vectors),
            f32(own, vectors),
            f32(ysize, line, vectors),
            f32(zsize, line, vectors),
            f32(own, vectors),
            f32(vectors, vectors),
            pltpu.VMEM((2, 2, 2 * vectors, 2 * vectors), BF16),
            f32(2, vectors, 2 * vectors),
            pltpu.VMEM((2, 2 * vectors, 2 * wide), BF16),
            f32(2, xsize, vectors, 2 * part),
            pltpu.SemaphoreType.DMA((4,)),
            dma(6),
        ]
        + [dma(ysize), dma(6)]
        + [dma(ysize)] * 3
        + [dma(ysize * SUBS)]
        + [dma(SUBS)] * 2
        + [dma(2), dma(SUBS)]
        + [
            dma(ysize),
            dma(ysize * xsize),
            dma(xsize),
            dma(ysize),
            dma(zsize),
            dma(ysize),
            dma(poles),
            dma(2 * xsize),
        ],
        compiler_params=pltpu.CompilerParams(
            collective_id=0, has_side_effects=True, vmem_limit_bytes=60 * 2**20
        ),
        name="step",
    )(subspace, pivots, lower_blocks, upper_blocks, pole_weights)


def build(mesh, sizes):
    xsize, zsize, ysize = sizes
    torus = Mesh(mesh.devices.reshape(xsize, 2, zsize, ysize), AXES)
    pole, rows = ("x", "core"), ("z", "y")
    return jax.shard_map(
        functools.partial(shards, sizes),
        mesh=torus,
        in_specs=(
            P(None, None, rows),
            P(pole, rows, None, None, None),
            P(pole, rows, None, None, None),
            P(pole, rows, None, None, None),
            P(pole, None),
        ),
        out_specs=P(None, pole, rows),
        check_vma=False,
    )


def solution(mesh):
    return build(mesh, (mesh.shape["pole"] // 2, mesh.shape["rows"] // 4, 4))
```

```python
import functools

import jax
import jax.numpy as jnp
from jax import lax
from jax.experimental import pallas as pl
from jax.experimental.pallas import tpu as pltpu
from jax.sharding import Mesh
from jax.sharding import PartitionSpec as P

F32 = jnp.float32
BF16 = jnp.bfloat16
MESH_ID = pl.DeviceIdType.MESH
AXES = ("x", "core", "z", "y")
SUBS = 4


def halves(value):
    high = value.astype(BF16)
    return high, (value - high.astype(F32)).astype(BF16)


def dot(left, right, trans):
    dims = (((1,), (1 if trans else 0,)), ((), ()))
    return lax.dot_general(left, right, dims, preferred_element_type=F32)


def times(rows, weights, trans):
    high, low = halves(rows)
    count = rows.shape[0]
    both = dot(jnp.concatenate([high, low], axis=0), weights[0], trans)
    return both[:count] + both[count:] + dot(high, weights[1], trans)


def prepare(weights, real, minus):
    height, width = real.shape
    for part, (r, m) in enumerate(zip(halves(real), halves(minus))):
        weights[part, :height, :width] = r
        weights[part, :height, width:] = m
        weights[part, height:, :width] = -m
        weights[part, height:, width:] = r


def tiles(count, size, body):
    if count == size:
        body(0)
        return

    def step(i, carry):
        body(pl.multiple_of(i * size, size))
        return carry

    lax.fori_loop(0, count // size, step, 0)


def remote(src, dst, sems, slot_out, slot_in, device):
    return pltpu.make_async_remote_copy(
        src_ref=src,
        dst_ref=dst,
        send_sem=sems.at[0, slot_out],
        recv_sem=sems.at[1, slot_in],
        device_id=device,
        device_id_type=MESH_ID,
    )


def nearest_first(count):
    return sorted(range(1, count), key=lambda d: min(d, count - d))


def step_kernel(
    dims, total_rows, f_hbm, g_hbm, e_hbm, u_hbm, w_ref, out_ref,
    f_ref, g_ref, e_ref, u_ref,
    we0, we1, wf0, wf1, wg, wc, wd, wp, wq, wh, wj, wz1, wa0, wa1,
    c_all, d_all, b_all, e_all, qg, rg, rj, rz, s0, s1, y0, y1, e0, eo, vin, win, tmp, wb, dg, dz, am,
    vz, vo, wz, wo, vk, wk,
    xs, other, cut, got, gram, g1, g3, h1, wn, zs, turned, qall,
    sem_in, sem_c, sem_b, sem_d, sem_v, sem_e, sem_r, sem_w, sem_fz, sem_bz, sem_one, sem_far,
    sem_a, sem_x, sem_1, sem_3, sem_5, sem_q,
):
    xsize, zsize, ysize = dims
    x, core, z, y = (lax.axis_index(a) for a in AXES)
    poles = 2 * xsize
    pole = x * 2 + core
    vectors, width = f_ref.shape[1], g_ref.shape[-1]
    chunk = vectors // ysize
    sub = chunk // SUBS
    tall = min(128, width)
    part = width // xsize
    own = vectors // poles
    line = own // ysize
    order = nearest_first(ysize)

    def pole_of(d):
        p = lax.rem(pole + d, poles)
        return p, {"x": p // 2, "core": lax.rem(p, 2)}

    def along(axis, me, d, size):
        return {axis: lax.rem(me + d, size)}

    barrier = pltpu.get_barrier_semaphore()
    for dp in range(poles):
        for dy in range(ysize):
            if dp or dy:
                device = pole_of(dp)[1] | along("y", y, dy, ysize)
                pl.semaphore_signal(barrier, inc=1, device_id=device, device_id_type=MESH_ID)
    for d in range(1, zsize):
        pl.semaphore_signal(barrier, inc=1, device_id=along("z", z, d, zsize), device_id_type=MESH_ID)

    loads = [
        pltpu.make_async_copy(a, b, sem_in.at[i])
        for i, (a, b) in enumerate(((e_hbm, e_ref), (u_hbm, u_ref), (g_hbm, g_ref), (f_hbm, f_ref)))
    ]
    for load in loads:
        load.start()

    sent = []

    def go(src, dst, sems, d, device):
        copy = remote(src, dst, sems, d, d, device)
        copy.start()
        sent.append(copy)

    def land(dst, sems, d, device):
        remote(dst, dst, sems, d, d, device).wait_recv()

    def back(me, d, size):
        return lax.rem(me + size - d, size)

    def lines(ref, j, count):
        return ref.at[pl.ds(pl.multiple_of(j * count, count), count), :]

    def piece(ref, j):
        return lines(ref, j, chunk)

    loads[0].wait()
    prepare(we0, e_ref[0, 0, 0], -e_ref[0, 0, 1])

    def forward_map(i):
        rows = jnp.concatenate([e_ref[0, 1, 0, pl.ds(i, tall), :], -e_ref[0, 1, 1, pl.ds(i, tall), :]], axis=1)
        c_all[y, pl.ds(i, tall), :] = times(rows, we0, False)

    tiles(width, tall, forward_map)
    pl.semaphore_wait(barrier, ysize * poles + zsize - 2)

    half = width // 2
    right, left = along("y", y, 1, ysize), along("y", y, ysize - 1, ysize)
    before, beyond, far = back(y, 1, ysize), lax.rem(y + 1, ysize), lax.rem(y + 2, ysize)

    def half_of(store, k, h):
        return store.at[k, pl.ds(h * half, half), :]

    def share(store, sems):
        for slot, h, device in ((0, 0, right), (2, 1, left), (1, 1, right), (3, 0, left)):
            if ysize > 2 or slot < 2:
                go(half_of(store, y, h), half_of(store, y, h), sems, slot, device)

    def onward(store, sems):
        first, second = half_of(store, before, 0), half_of(store, beyond, 1)
        return remote(first, first, sems, 4, 4, right), remote(second, second, sems, 5, 5, left)

    def pass_on(store, sems):
        land(half_of(store, before, 0), sems, 0, left)
        if ysize > 2:
            to_right, to_left = onward(store, sems)
            to_right.start()
            land(half_of(store, beyond, 1), sems, 2, right)
            to_left.start()

    def take(store, sems, weights):
        land(half_of(store, before, 1), sems, 1, left)
        prepare(weights.at[before], store[before, :, :width], store[before, :, width:])
        if ysize > 2:
            land(half_of(store, beyond, 0), sems, 3, right)
            prepare(weights.at[beyond], store[beyond, :, :width], store[beyond, :, width:])
            land(half_of(store, far, 0), sems, 4, left)
            land(half_of(store, far, 1), sems, 5, right)
            prepare(weights.at[far], store[far, :, :width], store[far, :, width:])

    share(c_all, sem_c)

    loads[2].wait()
    prepare(wg.at[0], g_ref[0, 0, 0], -g_ref[0, 0, 1])
    prepare(wg.at[1], g_ref[0, 1, 0], -g_ref[0, 1, 1])
    prepare(we1, e_ref[0, 1, 0], -e_ref[0, 1, 1])
    loads[3].wait()

    def local(i):
        rows = pl.ds(i, tall)
        first = jnp.concatenate([f_ref[0, rows, :width], f_ref[1, rows, :width]], axis=1)
        second = jnp.concatenate([f_ref[0, rows, width:], f_ref[1, rows, width:]], axis=1)
        start = times(first, wg.at[0], True)
        s0[rows, :] = start
        s1[rows, :] = times(second, wg.at[1], True) - times(start, we1, True)

    tiles(vectors, tall, local)
    for d in order:
        go(piece(s1, lax.rem(y + d, ysize)), b_all.at[y], sem_b, d, along("y", y, d, ysize))
    b_all[y] = piece(s1, y)[...]

    loads[1].wait()
    prepare(wf1, u_ref[0, 1, 0], -u_ref[0, 1, 1])
    prepare(wf0, u_ref[0, 0, 0], -u_ref[0, 0, 1])
    prepare(wc.at[y], c_all[y, :, :width], c_all[y, :, width:])

    def backward_map(i):
        rows = pl.ds(i, tall)
        upper = jnp.concatenate([u_ref[0, 0, 0, rows, :], -u_ref[0, 0, 1, rows, :]], axis=1)
        d_all[y, rows, :] = times(upper, wf1, False)
        lower = jnp.concatenate([e_ref[0, 0, 0, rows, :], -e_ref[0, 0, 1, rows, :]], axis=1)
        tmp[rows, :] = -lower - times(upper, wc.at[y], False)

    tiles(width, tall, backward_map)
    pass_on(c_all, sem_c)
    prepare(wh, tmp[:width, :width], tmp[:width, width:])

    def local_ends(i):
        rows = pl.ds(i, tall)
        e0[rows, :] = s0[rows, :] - times(s1[rows, :], wf0, True)

    tiles(vectors, tall, local_ends)

    take(c_all, sem_c, wc)
    for d in order:
        land(b_all.at[back(y, d, ysize)], sem_b, d, along("y", y, ysize - d, ysize))
    share(d_all, sem_d)

    value = b_all[0]
    for k in range(1, ysize):
        value = times(value, wc.at[k], True) + b_all[k]
    qg[...] = value

    def hop(out, into, sems, s, device):
        return remote(out.at[pl.ds(s * sub, sub), :], into.at[pl.ds(s * sub, sub), :], sems, s, s, device)

    ahead, behind = along("z", z, 1, zsize), along("z", z, zsize - 1, zsize)

    @pl.when(z == 0)
    def _():
        for s in range(SUBS):
            hop(qg, vz, sem_fz, s, ahead).start()
        vz[...] = jnp.zeros_like(vz)

    @pl.when(jnp.logical_and(z > 0, z < zsize - 1))
    def _():
        def group_forward(i):
            value = c_all[ysize - 1, pl.ds(i, tall), :]
            for k in reversed(range(ysize - 1)):
                value = times(value, wc.at[k], False)
            tmp[pl.ds(i, tall), :] = value

        tiles(width, tall, group_forward)
        prepare(wp, tmp[:width, :width].T, -tmp[:width, width:].T)

    early = z < 3
    pl.when(jnp.logical_not(early))(lambda: pass_on(d_all, sem_d))

    for s in range(SUBS):
        rows = pl.ds(s * sub, sub)

        @pl.when(z > 0)
        def _():
            hop(vz, vz, sem_fz, s, behind).wait_recv()

        @pl.when(jnp.logical_and(z > 0, z < zsize - 1))
        def _():
            vo[rows, :] = times(vz[rows, :], wp, False) + qg[rows, :]
            hop(vo, vz, sem_fz, s, ahead).start()

    def hand_out(k, value, staging, into, sems):
        staging[k] = value

        @pl.when(y == k)
        def _():
            piece(into, y)[...] = value

        @pl.when(y != k)
        def _():
            remote(staging.at[k], piece(into, y), sems, k, y, {"y": k}).start()

    def handed_out(staging, into, sems, count):
        for k in range(count):
            @pl.when(y != k)
            def _():
                remote(staging.at[k], piece(into, y), sems, k, y, {"y": k}).wait_send()

    value = vz[...]
    for k in range(ysize):
        hand_out(k, value, vk, vin, sem_v)
        if k < ysize - 1:
            value = times(value, wc.at[k], True) + b_all[k]

    pl.when(early)(lambda: pass_on(d_all, sem_d))

    for d in [0] + order:
        j = lax.rem(y + d, ysize)
        rows = pl.ds(pl.multiple_of(j * chunk, chunk), chunk)
        if d:
            remote(vin.at[rows, :], vin.at[rows, :], sem_v, j, j, {"y": j}).wait_recv()
        ends = e0[rows, :] + times(vin[rows, :], wh, True)
        if d:
            eo[rows, :] = ends
            remote(eo.at[rows, :], e_all.at[y], sem_e, j, y, {"y": j}).start()
        else:
            e_all[y] = ends

    prepare(wd.at[y], d_all[y, :, :width], d_all[y, :, width:])
    take(d_all, sem_d, wd)
    even = lax.rem(z, 2) == 0
    jumps = jnp.logical_and(even, jnp.logical_and(z >= 2, z <= zsize - 4))
    feeds = jnp.logical_and(jnp.logical_not(even), z <= zsize - 5)
    leaps = jnp.logical_and(even, z <= zsize - 6)
    last = z == zsize - 1
    inner = jnp.logical_and(z > 0, z < zsize - 1)
    steps = jnp.logical_and(inner, z >= zsize - 3)

    @pl.when(inner)
    def _():
        def compose(i):
            value = d_all[0, pl.ds(i, tall), :]
            for k in range(1, ysize):
                value = times(value, wd.at[k], False)
            dg[pl.ds(i, tall), :] = value

        tiles(width, tall, compose)

    @pl.when(feeds)
    def _():
        remote(dg, dz, sem_one, 0, 0, ahead).start()

    pl.when(jumps)(lambda: prepare(wq, dg[:, :width], dg[:, width:]))
    pl.when(steps)(lambda: prepare(wq, dg[:, :width].T, -dg[:, width:].T))

    def swept(i):
        rows = pl.ds(i, tall)
        value = vin[rows, :]
        y0[rows, :] = s0[rows, :] - times(value, we0, True)
        y1[rows, :] = s1[rows, :] + times(value, wc.at[y], True)

    tiles(vectors, tall, swept)

    for d in order:
        j = lax.rem(y + d, ysize)
        remote(e_all.at[j], e_all.at[j], sem_e, j, j, {"y": j}).wait_recv()
    values = [e_all[ysize - 1]]
    for k in reversed(range(ysize - 1)):
        values.append(times(values[-1], wd.at[k], True) + e_all[k])
    rg[...] = values[-1]

    @pl.when(last)
    def _():
        for s in range(SUBS):
            hop(rg, wz, sem_bz, s, behind).start()
        wz[...] = jnp.zeros_like(wz)

    @pl.when(feeds)
    def _():
        remote(rg, rz, sem_one, 1, 1, ahead).start()

    for k in range(ysize - 1):
        hand_out(k, values[ysize - 2 - k], wk, win, sem_r)

    @pl.when(jumps)
    def _():
        remote(dz, dz, sem_one, 0, 0, behind).wait_recv()
        prepare(wz1, dz[:, :width], dz[:, width:])

        def joint(i):
            tmp[pl.ds(i, tall), :] = times(dz[pl.ds(i, tall), :], wq, False)

        tiles(width, tall, joint)
        prepare(wj, tmp[:width, :width].T, -tmp[:width, width:].T)
        remote(rz, rz, sem_one, 1, 1, behind).wait_recv()
        rj[...] = times(rg[...], wz1, True) + rz[...]

    def settle():
        @pl.when(y < ysize - 1)
        def _():
            for d in order:
                j = lax.rem(y + d, ysize)
                remote(piece(win, j), piece(win, j), sem_r, j, j, {"y": j}).wait_recv()

            def inner_part(i):
                rows = pl.ds(i, tall)
                y1[rows, :] = y1[rows, :] - times(win[rows, :], wf1, True)

            tiles(vectors, tall, inner_part)

        def first_part(i):
            rows = pl.ds(i, tall)
            y0[rows, :] = y0[rows, :] - times(y1[rows, :], wf0, True)

        tiles(vectors, tall, first_part)

        @pl.when(z < zsize - 1)
        def _():
            am[:, :width] = u_ref[0, 1, 0]
            am[:, width:] = -u_ref[0, 1, 1]
            for k in range(1, ysize):
                @pl.when(k > y)
                def _():
                    def longer(i):
                        am[pl.ds(i, tall), :] = times(am[pl.ds(i, tall), :], wd.at[k], False)

                    tiles(width, tall, longer)
            prepare(wa1, am[:, :width], am[:, width:])

            def both(i):
                rows = pl.ds(i, tall)
                upper = jnp.concatenate([u_ref[0, 0, 0, rows, :], -u_ref[0, 0, 1, rows, :]], axis=1)
                am[rows, :] = times(upper, wa1, False)

            tiles(width, tall, both)
            prepare(wa0, am[:, :width], am[:, width:])

    soon = z >= zsize // 2
    pl.when(jnp.logical_not(soon))(settle)

    two_on, two_back = along("z", z, 2, zsize), along("z", z, zsize - 2, zsize)

    def spread(s, k):
        rows = pl.ds(pl.multiple_of(y * chunk + s * sub, sub), sub)
        return remote(
            wz.at[pl.ds(s * sub, sub), :], wb.at[rows, :], sem_w, k * SUBS + s, y * SUBS + s, {"y": k}
        )

    for s in range(SUBS):
        rows = pl.ds(s * sub, sub)

        @pl.when(leaps)
        def _():
            hop(wz, wz, sem_far, s, two_on).wait_recv()

        @pl.when(jnp.logical_and(z < zsize - 1, jnp.logical_not(leaps)))
        def _():
            hop(wz, wz, sem_bz, s, ahead).wait_recv()

        @pl.when(steps)
        def _():
            wo[rows, :] = times(wz[rows, :], wq, False) + rg[rows, :]
            hop(wo, wz, sem_bz, s, behind).start()

        @pl.when(jumps)
        def _():
            rj[rows, :] = times(wz[rows, :], wj, False) + rj[rows, :]
            hop(rj, wz, sem_far, s, two_back).start()

        @pl.when(z < zsize - 1)
        def _():
            for d in order:
                spread(s, lax.rem(y + d, ysize)).start()

    @pl.when(jumps)
    def _():
        wo[...] = times(wz[...], wq, True) + rg[...]
        for s in range(SUBS):
            hop(wo, wz, sem_bz, s, behind).start()

    pl.when(soon)(settle)

    sibling = {"core": 1 - core}
    wreal, wimag = w_ref[0, 0], w_ref[0, 1]

    def rows_of(d):
        j = lax.rem(y + d, ysize)
        return j, pl.ds(pl.multiple_of(j * chunk, chunk), chunk)

    def over_x(turn, d):
        _, rows = rows_of(d)
        land(other.at[rows, :], sem_a, turn, sibling)
        pair = xs[core, rows, :] + other[rows, :]
        for j in range(xsize):
            cut[j, rows, :] = jnp.concatenate(
                [pair[:, j * part : (j + 1) * part], pair[:, width + j * part : width + (j + 1) * part]], axis=1
            )
        for step in nearest_first(xsize):
            go(
                cut.at[lax.rem(x + step, xsize), rows, :],
                got.at[x, rows, :],
                sem_x,
                turn * xsize + step,
                along("x", x, step, xsize),
            )
        got[x, rows, :] = cut[x, rows, :]

    turns = [0] + order
    for turn, d in enumerate(turns):
        j, rows = rows_of(d)

        @pl.when(z < zsize - 1)
        def _():
            if d:
                for s in range(SUBS):
                    part_rows = pl.ds(pl.multiple_of(j * chunk + s * sub, sub), sub)
                    remote(
                        wb.at[part_rows, :], wb.at[part_rows, :], sem_w, j * SUBS + s, j * SUBS + s, {"y": j}
                    ).wait_recv()
                inflow = wb[rows, :]
            else:
                inflow = wz[...]
            y1[rows, :] = y1[rows, :] - times(inflow, wa1, True)
            y0[rows, :] = y0[rows, :] + times(inflow, wa0, True)

        for n, solved in enumerate((y0, y1)):
            real, imag = solved[rows, :width], solved[rows, width:]
            xs[n, rows, :width] = wreal * real - wimag * imag
            xs[n, rows, width:] = wreal * imag + wimag * real
        go(xs.at[1 - core, rows, :], other.at[rows, :], sem_a, turn, sibling)
        if turn:
            over_x(turn - 1, turns[turn - 1])
    over_x(len(turns) - 1, turns[-1])
    for turn, d in enumerate(turns):
        _, rows = rows_of(d)
        for step in nearest_first(xsize):
            j = back(x, step, xsize)
            land(got.at[j, rows, :], sem_x, turn * xsize + step, {"x": j})
    basis = got[0]
    for j in range(1, xsize):
        basis = basis + got[j]
    qall[core, x] = basis
    go(qall.at[core, x], qall.at[core, x], sem_q, 0, sibling)
    land(qall.at[1 - core, x], sem_q, 0, sibling)
    low_rows = pl.ds(pl.multiple_of(core * (vectors // 2), vectors // 2), vectors // 2)
    left_side = jnp.concatenate([qall[n, x, low_rows, :] for n in range(2)], axis=1)
    right_side = []
    for n in range(2):
        real, imag = qall[n, x, :, :part], qall[n, x, :, part:]
        right_side += [real + imag, imag - real]
    lh, ll = halves(left_side)
    rh, rl = halves(jnp.concatenate(right_side, axis=1))
    gram[...] = dot(lh, rh, True) + dot(ll, rh, True) + dot(lh, rl, True)
    plane = [(dx, dy) for dx in range(xsize) for dy in range(ysize) if dx or dy]
    plane.sort(key=lambda p: min(p[0], xsize - p[0]) + min(p[1], ysize - p[1]))
    here = x * ysize + y
    for dx, dy in plane:
        slot = dx * ysize + dy
        jx, jy = lax.rem(x + dx, xsize), lax.rem(y + dy, ysize)
        go(lines(gram, jx * ysize + jy, line), g1.at[here], sem_1, slot, {"x": jx, "y": jy})
    g1[here] = lines(gram, here, line)[...]
    for step in nearest_first(xsize):
        go(qall.at[core, x], qall.at[core, x], sem_q, step, along("x", x, step, xsize))
    for dx, dy in plane:
        jx, jy = back(x, dx, xsize), back(y, dy, ysize)
        land(g1.at[jx * ysize + jy], sem_1, dx * ysize + dy, {"x": jx, "y": jy})
    value = g1[0]
    for j in range(1, xsize * ysize):
        value = value + g1[j]
    g3[z] = value
    for d in nearest_first(zsize):
        go(g3.at[z], g3.at[z], sem_3, d, {"z": lax.rem(z + d, zsize)})
    for d in nearest_first(zsize):
        j = back(z, d, zsize)
        land(g3.at[j], sem_3, d, {"z": j})
    value = g3[0]
    for j in range(1, zsize):
        value = value + g3[j]
    place = (core * xsize + x) * ysize + y
    lines(h1, place, line)[...] = value
    others = [(dp, dy) for dp in range(poles) for dy in range(ysize) if dp or dy]
    for dp, dy in others:
        device = pole_of(dp)[1] | along("y", y, dy, ysize)
        go(lines(h1, place, line), lines(h1, place, line), sem_5, dp * ysize + dy, device)
    for step in nearest_first(xsize):
        j = back(x, step, xsize)
        land(qall.at[core, j], sem_q, step, {"x": j})
        go(qall.at[core, j], qall.at[core, j], sem_q, xsize + step, sibling)
    for step in nearest_first(xsize):
        land(qall.at[1 - core, back(x, step, xsize)], sem_q, xsize + step, sibling)
    prepare(
        turned,
        jnp.concatenate([qall[n, j, :, :part] for n in range(2) for j in range(xsize)], axis=1),
        jnp.concatenate([qall[n, j, :, part:] for n in range(2) for j in range(xsize)], axis=1),
    )
    for dp, dy in others:
        p, device = pole_of(poles - dp)
        jy = back(y, dy, ysize)
        source = (lax.rem(p, 2) * xsize + p // 2) * ysize + jy
        land(lines(h1, source, line), sem_5, dp * ysize + dy, device | {"y": jy})

    whole = h1[...]
    frob = jnp.sqrt(jnp.sum(whole * whole))
    flip = whole.T
    scale = -0.25 / frob
    eye = (
        lax.broadcasted_iota(jnp.int32, (vectors, vectors), 0)
        == lax.broadcasted_iota(jnp.int32, (vectors, vectors), 1)
    )
    first = jnp.where(eye, 1.5, 0.0) + scale * (whole + flip)
    minus = -scale * (whole - flip)
    prepare(wn.at[0], first, minus)
    zs[0, :, :vectors] = first
    zs[0, :, vectors:] = minus

    def square(i):
        rows = pl.ds(i, tall)
        zs[1, rows, :] = times(zs[0, rows, :], wn.at[0], False)

    tiles(vectors, tall, square)
    prepare(
        wn.at[1],
        zs[1, :, :vectors] - 1.5 * zs[0, :, :vectors],
        zs[1, :, vectors:] - 1.5 * zs[0, :, vectors:],
    )
    size = jnp.sqrt(total_rows / frob)
    rows = pl.ds(pl.multiple_of(pole * own, own), own)
    mix = 1.5 * zs[0, rows, :] + times(zs[1, rows, :], wn.at[1], False)
    turned_rows = times(mix, turned, False) * size
    out_ref[0] = turned_rows[:, : 2 * width]
    out_ref[1] = turned_rows[:, 2 * width :]
    for copy in sent:
        copy.wait_send()
    if ysize > 2:
        for copy in (*onward(c_all, sem_c), *onward(d_all, sem_d)):
            copy.wait_send()
    handed_out(vk, vin, sem_v, ysize)
    handed_out(wk, win, sem_r, ysize - 1)
    for d in order:
        j, rows = rows_of(d)
        remote(eo.at[rows, :], e_all.at[y], sem_e, j, y, {"y": j}).wait_send()
    for s in range(SUBS):
        @pl.when(z < zsize - 1)
        def _():
            hop(vo, vz, sem_fz, s, ahead).wait_send()

        @pl.when(jnp.logical_or(last, jnp.logical_or(steps, jumps)))
        def _():
            hop(wo, wz, sem_bz, s, behind).wait_send()

        @pl.when(jumps)
        def _():
            hop(rj, wz, sem_far, s, two_back).wait_send()

        @pl.when(z < zsize - 1)
        def _():
            for d in order:
                spread(s, lax.rem(y + d, ysize)).wait_send()

    @pl.when(feeds)
    def _():
        remote(dg, dz, sem_one, 0, 0, ahead).wait_send()
        remote(rg, rz, sem_one, 1, 1, ahead).wait_send()


def shards(sizes, subspace, pivots, lower_blocks, upper_blocks, pole_weights):
    xsize, zsize, ysize = sizes
    vectors, width = subspace.shape[1], pivots.shape[-1]
    wide = 2 * width
    chunk = vectors // ysize
    poles = 2 * xsize
    part = width // xsize
    own = vectors // poles
    line = own // ysize
    total_rows = float(2 * width * ysize * zsize)

    def dma(count):
        return pltpu.SemaphoreType.DMA((2, count))

    def f32(*shape):
        return pltpu.VMEM(shape, F32)

    def prepared(*counts):
        return pltpu.VMEM((*counts, 2, wide, wide), BF16)

    anywhere = pl.BlockSpec(memory_space=pl.ANY)
    return pl.pallas_call(
        functools.partial(step_kernel, (xsize, zsize, ysize), total_rows),
        out_shape=jax.ShapeDtypeStruct((2, own, wide), F32),
        in_specs=[anywhere] * 4 + [pl.BlockSpec(memory_space=pltpu.SMEM)],
        out_specs=pl.BlockSpec(memory_space=pltpu.VMEM),
        scratch_shapes=[f32(*a.shape) for a in (subspace, pivots, lower_blocks, upper_blocks)]
        + [prepared()] * 4
        + [prepared(2)]
        + [prepared(ysize)] * 2
        + [prepared()] * 7
        + [f32(ysize, width, wide)] * 2
        + [f32(ysize, chunk, wide)] * 2
        + [f32(chunk, wide)] * 4
        + [f32(vectors, wide)] * 10
        + [f32(width, wide)] * 3
        + [f32(chunk, wide)] * 4
        + [f32(ysize, chunk, wide)] * 2
        + [
            f32(2, vectors, wide),
            f32(vectors, wide),
            f32(xsize, vectors, 2 * part),
            f32(xsize, vectors, 2 * part),
            f32(vectors // 2, vectors),
            f32(xsize * ysize, line, vectors),
            f32(zsize, line, vectors),
            f32(vectors, vectors),
            pltpu.VMEM((2, 2, 2 * vectors, 2 * vectors), BF16),
            f32(2, vectors, 2 * vectors),
            pltpu.VMEM((2, 2 * vectors, 2 * wide), BF16),
            f32(2, xsize, vectors, 2 * part),
            pltpu.SemaphoreType.DMA((4,)),
            dma(6),
        ]
        + [dma(ysize), dma(6)]
        + [dma(ysize)] * 3
        + [dma(ysize * SUBS)]
        + [dma(SUBS)] * 2
        + [dma(2), dma(SUBS)]
        + [
            dma(ysize),
            dma(ysize * xsize),
            dma(xsize * ysize),
            dma(zsize),
            dma(poles * ysize),
            dma(2 * xsize),
        ],
        compiler_params=pltpu.CompilerParams(
            collective_id=0, has_side_effects=True, vmem_limit_bytes=60 * 2**20
        ),
        name="step",
    )(subspace, pivots, lower_blocks, upper_blocks, pole_weights)


def build(mesh, sizes):
    xsize, zsize, ysize = sizes
    torus = Mesh(mesh.devices.reshape(xsize, 2, zsize, ysize), AXES)
    pole, rows = ("x", "core"), ("z", "y")
    return jax.shard_map(
        functools.partial(shards, sizes),
        mesh=torus,
        in_specs=(
            P(None, None, rows),
            P(pole, rows, None, None, None),
            P(pole, rows, None, None, None),
            P(pole, rows, None, None, None),
            P(pole, None),
        ),
        out_specs=P(None, pole, rows),
        check_vma=False,
    )


def solution(mesh):
    return build(mesh, (mesh.shape["pole"] // 2, mesh.shape["rows"] // 4, 4))
```

```python
import functools

import jax
import jax.numpy as jnp
from jax import lax
from jax.experimental import pallas as pl
from jax.experimental.pallas import tpu as pltpu
from jax.sharding import Mesh
from jax.sharding import PartitionSpec as P

F32 = jnp.float32
BF16 = jnp.bfloat16
MESH_ID = pl.DeviceIdType.MESH
AXES = ("x", "core", "z", "y")
SUBS = 4


def halves(value):
    high = value.astype(BF16)
    return high, (value - high.astype(F32)).astype(BF16)


def dot(left, right, trans):
    dims = (((1,), (1 if trans else 0,)), ((), ()))
    return lax.dot_general(left, right, dims, preferred_element_type=F32)


def times(rows, weights, trans):
    high, low = halves(rows)
    count = rows.shape[0]
    both = dot(jnp.concatenate([high, low], axis=0), weights[0], trans)
    return both[:count] + both[count:] + dot(high, weights[1], trans)


def prepare(weights, real, minus):
    height, width = real.shape
    for part, (r, m) in enumerate(zip(halves(real), halves(minus))):
        weights[part, :height, :width] = r
        weights[part, :height, width:] = m
        weights[part, height:, :width] = -m
        weights[part, height:, width:] = r


def tiles(count, size, body):
    if count == size:
        body(0)
        return

    def step(i, carry):
        body(pl.multiple_of(i * size, size))
        return carry

    lax.fori_loop(0, count // size, step, 0)


def remote(src, dst, sems, slot_out, slot_in, device):
    return pltpu.make_async_remote_copy(
        src_ref=src,
        dst_ref=dst,
        send_sem=sems.at[0, slot_out],
        recv_sem=sems.at[1, slot_in],
        device_id=device,
        device_id_type=MESH_ID,
    )


def nearest_first(count):
    return sorted(range(1, count), key=lambda d: min(d, count - d))


def step_kernel(
    dims, total_rows, f_hbm, g_hbm, e_hbm, u_hbm, w_ref, out_ref,
    f_ref, g_ref, e_ref, u_ref,
    we0, we1, wf0, wf1, wg, wc, wd, wp, wq, wh, wj, wz1, wa0, wa1,
    c_all, d_all, b_all, e_all, qg, rg, rj, rz, s0, s1, y0, y1, e0, eo, vin, win, tmp, wb, dg, dz, am, cg,
    vz, vo, wz, wo, vk, wk,
    xs, other, cut, got, gram, g1, g3, h1, wn, zs, turned, qall,
    sem_in, sem_c, sem_b, sem_d, sem_v, sem_e, sem_r, sem_w, sem_fz, sem_bz, sem_one, sem_far, sem_skip,
    sem_a, sem_x, sem_1, sem_3, sem_5, sem_q,
):
    xsize, zsize, ysize = dims
    x, core, z, y = (lax.axis_index(a) for a in AXES)
    poles = 2 * xsize
    pole = x * 2 + core
    vectors, width = f_ref.shape[1], g_ref.shape[-1]
    chunk = vectors // ysize
    sub = chunk // SUBS
    tall = min(128, width)
    part = width // xsize
    own = vectors // poles
    line = own // ysize
    order = nearest_first(ysize)

    def pole_of(d):
        p = lax.rem(pole + d, poles)
        return p, {"x": p // 2, "core": lax.rem(p, 2)}

    def along(axis, me, d, size):
        return {axis: lax.rem(me + d, size)}

    barrier = pltpu.get_barrier_semaphore()
    for dp in range(poles):
        for dy in range(ysize):
            if dp or dy:
                device = pole_of(dp)[1] | along("y", y, dy, ysize)
                pl.semaphore_signal(barrier, inc=1, device_id=device, device_id_type=MESH_ID)
    for d in range(1, zsize):
        pl.semaphore_signal(barrier, inc=1, device_id=along("z", z, d, zsize), device_id_type=MESH_ID)

    loads = [
        pltpu.make_async_copy(a, b, sem_in.at[i])
        for i, (a, b) in enumerate(((e_hbm, e_ref), (u_hbm, u_ref), (g_hbm, g_ref), (f_hbm, f_ref)))
    ]
    for load in loads:
        load.start()

    sent = []

    def go(src, dst, sems, d, device):
        copy = remote(src, dst, sems, d, d, device)
        copy.start()
        sent.append(copy)

    def land(dst, sems, d, device):
        remote(dst, dst, sems, d, d, device).wait_recv()

    def back(me, d, size):
        return lax.rem(me + size - d, size)

    def lines(ref, j, count):
        return ref.at[pl.ds(pl.multiple_of(j * count, count), count), :]

    def piece(ref, j):
        return lines(ref, j, chunk)

    loads[0].wait()
    prepare(we0, e_ref[0, 0, 0], -e_ref[0, 0, 1])

    def forward_map(i):
        rows = jnp.concatenate([e_ref[0, 1, 0, pl.ds(i, tall), :], -e_ref[0, 1, 1, pl.ds(i, tall), :]], axis=1)
        c_all[y, pl.ds(i, tall), :] = times(rows, we0, False)

    tiles(width, tall, forward_map)
    pl.semaphore_wait(barrier, ysize * poles + zsize - 2)

    half = width // 2
    right, left = along("y", y, 1, ysize), along("y", y, ysize - 1, ysize)
    before, beyond, far = back(y, 1, ysize), lax.rem(y + 1, ysize), lax.rem(y + 2, ysize)

    def half_of(store, k, h):
        return store.at[k, pl.ds(h * half, half), :]

    def share(store, sems):
        for slot, h, device in ((0, 0, right), (2, 1, left), (1, 1, right), (3, 0, left)):
            if ysize > 2 or slot < 2:
                go(half_of(store, y, h), half_of(store, y, h), sems, slot, device)

    def onward(store, sems):
        first, second = half_of(store, before, 0), half_of(store, beyond, 1)
        return remote(first, first, sems, 4, 4, right), remote(second, second, sems, 5, 5, left)

    def pass_on(store, sems):
        land(half_of(store, before, 0), sems, 0, left)
        if ysize > 2:
            to_right, to_left = onward(store, sems)
            to_right.start()
            land(half_of(store, beyond, 1), sems, 2, right)
            to_left.start()

    def take(store, sems, weights):
        land(half_of(store, before, 1), sems, 1, left)
        prepare(weights.at[before], store[before, :, :width], store[before, :, width:])
        if ysize > 2:
            land(half_of(store, beyond, 0), sems, 3, right)
            prepare(weights.at[beyond], store[beyond, :, :width], store[beyond, :, width:])
            land(half_of(store, far, 0), sems, 4, left)
            land(half_of(store, far, 1), sems, 5, right)
            prepare(weights.at[far], store[far, :, :width], store[far, :, width:])

    share(c_all, sem_c)

    loads[2].wait()
    prepare(wg.at[0], g_ref[0, 0, 0], -g_ref[0, 0, 1])
    prepare(wg.at[1], g_ref[0, 1, 0], -g_ref[0, 1, 1])
    prepare(we1, e_ref[0, 1, 0], -e_ref[0, 1, 1])
    loads[3].wait()

    def local(i):
        rows = pl.ds(i, tall)
        first = jnp.concatenate([f_ref[0, rows, :width], f_ref[1, rows, :width]], axis=1)
        second = jnp.concatenate([f_ref[0, rows, width:], f_ref[1, rows, width:]], axis=1)
        start = times(first, wg.at[0], True)
        s0[rows, :] = start
        s1[rows, :] = times(second, wg.at[1], True) - times(start, we1, True)

    tiles(vectors, tall, local)
    for d in order:
        go(piece(s1, lax.rem(y + d, ysize)), b_all.at[y], sem_b, d, along("y", y, d, ysize))
    b_all[y] = piece(s1, y)[...]

    loads[1].wait()
    prepare(wf1, u_ref[0, 1, 0], -u_ref[0, 1, 1])
    prepare(wf0, u_ref[0, 0, 0], -u_ref[0, 0, 1])
    prepare(wc.at[y], c_all[y, :, :width], c_all[y, :, width:])

    def backward_map(i):
        rows = pl.ds(i, tall)
        upper = jnp.concatenate([u_ref[0, 0, 0, rows, :], -u_ref[0, 0, 1, rows, :]], axis=1)
        d_all[y, rows, :] = times(upper, wf1, False)
        lower = jnp.concatenate([e_ref[0, 0, 0, rows, :], -e_ref[0, 0, 1, rows, :]], axis=1)
        tmp[rows, :] = -lower - times(upper, wc.at[y], False)

    tiles(width, tall, backward_map)
    pass_on(c_all, sem_c)
    prepare(wh, tmp[:width, :width].T, -tmp[:width, width:].T)

    def local_ends(i):
        rows = pl.ds(i, tall)
        e0[rows, :] = s0[rows, :] - times(s1[rows, :], wf0, True)

    tiles(vectors, tall, local_ends)

    take(c_all, sem_c, wc)
    for d in order:
        land(b_all.at[back(y, d, ysize)], sem_b, d, along("y", y, ysize - d, ysize))
    share(d_all, sem_d)

    value = b_all[0]
    for k in range(1, ysize):
        value = times(value, wc.at[k], True) + b_all[k]
    qg[...] = value

    def hop(out, into, sems, s, device):
        return remote(out.at[pl.ds(s * sub, sub), :], into.at[pl.ds(s * sub, sub), :], sems, s, s, device)

    ahead, behind = along("z", z, 1, zsize), along("z", z, zsize - 1, zsize)

    skips = z == (zsize - 3 if zsize > 3 else -1)
    lends = z == (zsize - 2 if zsize > 3 else -1)
    served = z == (zsize - 1 if zsize > 3 else -1)
    two_on, two_back = along("z", z, 2, zsize), along("z", z, zsize - 2, zsize)

    @pl.when(z == 0)
    def _():
        for s in range(SUBS):
            hop(qg, vz, sem_fz, s, ahead).start()
        vz[...] = jnp.zeros_like(vz)

    @pl.when(jnp.logical_and(z > 0, z < zsize - 1))
    def _():
        def group_forward(i):
            value = c_all[ysize - 1, pl.ds(i, tall), :]
            for k in reversed(range(ysize - 1)):
                value = times(value, wc.at[k], False)
            cg[pl.ds(i, tall), :] = value

        tiles(width, tall, group_forward)

        @pl.when(lends)
        def _():
            remote(cg, dz, sem_one, 2, 2, behind).start()
            remote(qg, rz, sem_one, 3, 3, behind).start()

        @pl.when(jnp.logical_not(lends))
        def _():
            prepare(wp, cg[:, :width].T, -cg[:, width:].T)

        @pl.when(skips)
        def _():
            prepare(wz1, cg[:, :width], cg[:, width:])

    early = z < 3
    pl.when(jnp.logical_not(early))(lambda: pass_on(d_all, sem_d))

    @pl.when(skips)
    def _():
        remote(dz, dz, sem_one, 2, 2, ahead).wait_recv()

        def joint(i):
            tmp[pl.ds(i, tall), :] = times(dz[pl.ds(i, tall), :], wz1, False)

        tiles(width, tall, joint)
        prepare(wj, tmp[:width, :width].T, -tmp[:width, width:].T)
        prepare(wq, dz[:, :width], dz[:, width:])
        remote(rz, rz, sem_one, 3, 3, ahead).wait_recv()
        rj[...] = times(qg[...], wq, True) + rz[...]

    for s in range(SUBS):
        rows = pl.ds(s * sub, sub)

        @pl.when(jnp.logical_and(z > 0, jnp.logical_not(served)))
        def _():
            hop(vz, vz, sem_fz, s, behind).wait_recv()

        @pl.when(served)
        def _():
            hop(vz, vz, sem_skip, s, two_back).wait_recv()

        @pl.when(jnp.logical_and(jnp.logical_and(z > 0, z < zsize - 1), jnp.logical_not(jnp.logical_or(skips, lends))))
        def _():
            vo[rows, :] = times(vz[rows, :], wp, False) + qg[rows, :]
            hop(vo, vz, sem_fz, s, ahead).start()

        @pl.when(skips)
        def _():
            rj[rows, :] = times(vz[rows, :], wj, False) + rj[rows, :]
            hop(rj, vz, sem_skip, s, two_on).start()

    @pl.when(skips)
    def _():
        vo[...] = times(vz[...], wp, False) + qg[...]
        for s in range(SUBS):
            hop(vo, vz, sem_fz, s, ahead).start()

    def hand_out(k, value, staging, into, sems):
        staging[k] = value

        @pl.when(y == k)
        def _():
            piece(into, y)[...] = value

        @pl.when(y != k)
        def _():
            remote(staging.at[k], piece(into, y), sems, k, y, {"y": k}).start()

    def handed_out(staging, into, sems, count):
        for k in range(count):
            @pl.when(y != k)
            def _():
                remote(staging.at[k], piece(into, y), sems, k, y, {"y": k}).wait_send()

    value = vz[...]
    for k in range(ysize):
        hand_out(k, value, vk, vin, sem_v)
        if k < ysize - 1:
            value = times(value, wc.at[k], True) + b_all[k]

    pl.when(early)(lambda: pass_on(d_all, sem_d))

    for d in [0] + order:
        j = lax.rem(y + d, ysize)
        rows = pl.ds(pl.multiple_of(j * chunk, chunk), chunk)
        if d:
            remote(vin.at[rows, :], vin.at[rows, :], sem_v, j, j, {"y": j}).wait_recv()
        ends = e0[rows, :] + times(vin[rows, :], wh, False)
        if d:
            eo[rows, :] = ends
            remote(eo.at[rows, :], e_all.at[y], sem_e, j, y, {"y": j}).start()
        else:
            e_all[y] = ends

    prepare(wd.at[y], d_all[y, :, :width], d_all[y, :, width:])
    take(d_all, sem_d, wd)
    even = lax.rem(z, 2) == 0
    jumps = jnp.logical_and(even, jnp.logical_and(z >= 2, z <= zsize - 4))
    feeds = jnp.logical_and(jnp.logical_not(even), z <= zsize - 5)
    leaps = jnp.logical_and(even, z <= zsize - 6)
    last = z == zsize - 1
    inner = jnp.logical_and(z > 0, z < zsize - 1)
    steps = jnp.logical_and(inner, z >= zsize - 3)

    @pl.when(inner)
    def _():
        def compose(i):
            value = d_all[0, pl.ds(i, tall), :]
            for k in range(1, ysize):
                value = times(value, wd.at[k], False)
            dg[pl.ds(i, tall), :] = value

        tiles(width, tall, compose)

    @pl.when(feeds)
    def _():
        remote(dg, dz, sem_one, 0, 0, ahead).start()

    pl.when(jumps)(lambda: prepare(wq, dg[:, :width], dg[:, width:]))
    pl.when(steps)(lambda: prepare(wq, dg[:, :width].T, -dg[:, width:].T))

    def swept(i):
        rows = pl.ds(i, tall)
        value = vin[rows, :]
        y0[rows, :] = s0[rows, :] - times(value, we0, True)
        y1[rows, :] = s1[rows, :] + times(value, wc.at[y], True)

    tiles(vectors, tall, swept)

    for d in order:
        j = lax.rem(y + d, ysize)
        remote(e_all.at[j], e_all.at[j], sem_e, j, j, {"y": j}).wait_recv()
    values = [e_all[ysize - 1]]
    for k in reversed(range(ysize - 1)):
        values.append(times(values[-1], wd.at[k], True) + e_all[k])
    rg[...] = values[-1]

    @pl.when(last)
    def _():
        for s in range(SUBS):
            hop(rg, wz, sem_bz, s, behind).start()
        wz[...] = jnp.zeros_like(wz)

    @pl.when(feeds)
    def _():
        remote(rg, rz, sem_one, 1, 1, ahead).start()

    for k in range(ysize - 1):
        hand_out(k, values[ysize - 2 - k], wk, win, sem_r)

    @pl.when(jumps)
    def _():
        remote(dz, dz, sem_one, 0, 0, behind).wait_recv()
        prepare(wz1, dz[:, :width], dz[:, width:])

        def joint(i):
            tmp[pl.ds(i, tall), :] = times(dz[pl.ds(i, tall), :], wq, False)

        tiles(width, tall, joint)
        prepare(wj, tmp[:width, :width].T, -tmp[:width, width:].T)
        remote(rz, rz, sem_one, 1, 1, behind).wait_recv()
        rj[...] = times(rg[...], wz1, True) + rz[...]

    def settle():
        @pl.when(y < ysize - 1)
        def _():
            for d in order:
                j = lax.rem(y + d, ysize)
                remote(piece(win, j), piece(win, j), sem_r, j, j, {"y": j}).wait_recv()

            def inner_part(i):
                rows = pl.ds(i, tall)
                y1[rows, :] = y1[rows, :] - times(win[rows, :], wf1, True)

            tiles(vectors, tall, inner_part)

        def first_part(i):
            rows = pl.ds(i, tall)
            y0[rows, :] = y0[rows, :] - times(y1[rows, :], wf0, True)

        tiles(vectors, tall, first_part)

        @pl.when(z < zsize - 1)
        def _():
            am[:, :width] = u_ref[0, 1, 0]
            am[:, width:] = -u_ref[0, 1, 1]
            for k in range(1, ysize):
                @pl.when(k > y)
                def _():
                    def longer(i):
                        am[pl.ds(i, tall), :] = times(am[pl.ds(i, tall), :], wd.at[k], False)

                    tiles(width, tall, longer)
            prepare(wa1, am[:, :width], am[:, width:])

            def both(i):
                rows = pl.ds(i, tall)
                upper = jnp.concatenate([u_ref[0, 0, 0, rows, :], -u_ref[0, 0, 1, rows, :]], axis=1)
                tmp[rows, :] = times(upper, wa1, False)

            tiles(width, tall, both)
            prepare(wa1, am[:, :width].T, -am[:, width:].T)
            prepare(wa0, tmp[:width, :width].T, -tmp[:width, width:].T)

    soon = z >= zsize // 2
    pl.when(jnp.logical_not(soon))(settle)

    def spread(s, k):
        rows = pl.ds(pl.multiple_of(y * chunk + s * sub, sub), sub)
        return remote(
            wz.at[pl.ds(s * sub, sub), :], wb.at[rows, :], sem_w, k * SUBS + s, y * SUBS + s, {"y": k}
        )

    for s in range(SUBS):
        rows = pl.ds(s * sub, sub)

        @pl.when(leaps)
        def _():
            hop(wz, wz, sem_far, s, two_on).wait_recv()

        @pl.when(jnp.logical_and(z < zsize - 1, jnp.logical_not(leaps)))
        def _():
            hop(wz, wz, sem_bz, s, ahead).wait_recv()

        @pl.when(steps)
        def _():
            wo[rows, :] = times(wz[rows, :], wq, False) + rg[rows, :]
            hop(wo, wz, sem_bz, s, behind).start()

        @pl.when(jumps)
        def _():
            rj[rows, :] = times(wz[rows, :], wj, False) + rj[rows, :]
            hop(rj, wz, sem_far, s, two_back).start()

        @pl.when(z < zsize - 1)
        def _():
            for d in order:
                spread(s, lax.rem(y + d, ysize)).start()

    @pl.when(jumps)
    def _():
        wo[...] = times(wz[...], wq, True) + rg[...]
        for s in range(SUBS):
            hop(wo, wz, sem_bz, s, behind).start()

    pl.when(soon)(settle)

    sibling = {"core": 1 - core}
    wreal, wimag = w_ref[0, 0], w_ref[0, 1]

    def rows_of(d):
        j = lax.rem(y + d, ysize)
        return j, pl.ds(pl.multiple_of(j * chunk, chunk), chunk)

    def over_x(turn, d):
        _, rows = rows_of(d)
        land(other.at[rows, :], sem_a, turn, sibling)
        pair = xs[core, rows, :] + other[rows, :]
        for j in range(xsize):
            cut[j, rows, :] = jnp.concatenate(
                [pair[:, j * part : (j + 1) * part], pair[:, width + j * part : width + (j + 1) * part]], axis=1
            )
        for step in nearest_first(xsize):
            go(
                cut.at[lax.rem(x + step, xsize), rows, :],
                got.at[x, rows, :],
                sem_x,
                turn * xsize + step,
                along("x", x, step, xsize),
            )
        got[x, rows, :] = cut[x, rows, :]

    turns = [0] + order
    for turn, d in enumerate(turns):
        j, rows = rows_of(d)

        @pl.when(z < zsize - 1)
        def _():
            if d:
                for s in range(SUBS):
                    part_rows = pl.ds(pl.multiple_of(j * chunk + s * sub, sub), sub)
                    remote(
                        wb.at[part_rows, :], wb.at[part_rows, :], sem_w, j * SUBS + s, j * SUBS + s, {"y": j}
                    ).wait_recv()
                inflow = wb[rows, :]
            else:
                inflow = wz[...]
            y1[rows, :] = y1[rows, :] - times(inflow, wa1, False)
            y0[rows, :] = y0[rows, :] + times(inflow, wa0, False)

        for n, solved in enumerate((y0, y1)):
            real, imag = solved[rows, :width], solved[rows, width:]
            xs[n, rows, :width] = wreal * real - wimag * imag
            xs[n, rows, width:] = wreal * imag + wimag * real
        go(xs.at[1 - core, rows, :], other.at[rows, :], sem_a, turn, sibling)
        if turn:
            over_x(turn - 1, turns[turn - 1])
    over_x(len(turns) - 1, turns[-1])
    for turn, d in enumerate(turns):
        _, rows = rows_of(d)
        for step in nearest_first(xsize):
            j = back(x, step, xsize)
            land(got.at[j, rows, :], sem_x, turn * xsize + step, {"x": j})
    basis = got[0]
    for j in range(1, xsize):
        basis = basis + got[j]
    qall[core, x] = basis
    go(qall.at[core, x], qall.at[core, x], sem_q, 0, sibling)
    land(qall.at[1 - core, x], sem_q, 0, sibling)
    low_rows = pl.ds(pl.multiple_of(core * (vectors // 2), vectors // 2), vectors // 2)
    left_side = jnp.concatenate([qall[n, x, low_rows, :] for n in range(2)], axis=1)
    right_side = []
    for n in range(2):
        real, imag = qall[n, x, :, :part], qall[n, x, :, part:]
        right_side += [real + imag, imag - real]
    lh, ll = halves(left_side)
    rh, rl = halves(jnp.concatenate(right_side, axis=1))
    gram[...] = dot(lh, rh, True) + dot(ll, rh, True) + dot(lh, rl, True)
    plane = [(dx, dy) for dx in range(xsize) for dy in range(ysize) if dx or dy]
    plane.sort(key=lambda p: min(p[0], xsize - p[0]) + min(p[1], ysize - p[1]))
    here = x * ysize + y
    for dx, dy in plane:
        slot = dx * ysize + dy
        jx, jy = lax.rem(x + dx, xsize), lax.rem(y + dy, ysize)
        go(lines(gram, jx * ysize + jy, line), g1.at[here], sem_1, slot, {"x": jx, "y": jy})
    g1[here] = lines(gram, here, line)[...]
    for step in nearest_first(xsize):
        go(qall.at[core, x], qall.at[core, x], sem_q, step, along("x", x, step, xsize))
    for dx, dy in plane:
        jx, jy = back(x, dx, xsize), back(y, dy, ysize)
        land(g1.at[jx * ysize + jy], sem_1, dx * ysize + dy, {"x": jx, "y": jy})
    value = g1[0]
    for j in range(1, xsize * ysize):
        value = value + g1[j]
    g3[z] = value
    for d in nearest_first(zsize):
        go(g3.at[z], g3.at[z], sem_3, d, {"z": lax.rem(z + d, zsize)})
    for d in nearest_first(zsize):
        j = back(z, d, zsize)
        land(g3.at[j], sem_3, d, {"z": j})
    value = g3[0]
    for j in range(1, zsize):
        value = value + g3[j]
    place = (core * xsize + x) * ysize + y
    lines(h1, place, line)[...] = value
    others = [(dp, dy) for dp in range(poles) for dy in range(ysize) if dp or dy]
    for dp, dy in others:
        device = pole_of(dp)[1] | along("y", y, dy, ysize)
        go(lines(h1, place, line), lines(h1, place, line), sem_5, dp * ysize + dy, device)
    for step in nearest_first(xsize):
        j = back(x, step, xsize)
        land(qall.at[core, j], sem_q, step, {"x": j})
        go(qall.at[core, j], qall.at[core, j], sem_q, xsize + step, sibling)
    for step in nearest_first(xsize):
        land(qall.at[1 - core, back(x, step, xsize)], sem_q, xsize + step, sibling)
    prepare(
        turned,
        jnp.concatenate([qall[n, j, :, :part] for n in range(2) for j in range(xsize)], axis=1),
        jnp.concatenate([qall[n, j, :, part:] for n in range(2) for j in range(xsize)], axis=1),
    )
    for dp, dy in others:
        p, device = pole_of(poles - dp)
        jy = back(y, dy, ysize)
        source = (lax.rem(p, 2) * xsize + p // 2) * ysize + jy
        land(lines(h1, source, line), sem_5, dp * ysize + dy, device | {"y": jy})

    whole = h1[...]
    frob = jnp.sqrt(jnp.sum(whole * whole))
    flip = whole.T
    scale = -0.25 / frob
    eye = (
        lax.broadcasted_iota(jnp.int32, (vectors, vectors), 0)
        == lax.broadcasted_iota(jnp.int32, (vectors, vectors), 1)
    )
    first = jnp.where(eye, 1.5, 0.0) + scale * (whole + flip)
    minus = -scale * (whole - flip)
    prepare(wn.at[0], first, minus)
    zs[0, :, :vectors] = first
    zs[0, :, vectors:] = minus

    def square(i):
        rows = pl.ds(i, tall)
        zs[1, rows, :] = times(zs[0, rows, :], wn.at[0], False)

    tiles(vectors, tall, square)
    prepare(
        wn.at[1],
        zs[1, :, :vectors] - 1.5 * zs[0, :, :vectors],
        zs[1, :, vectors:] - 1.5 * zs[0, :, vectors:],
    )
    size = jnp.sqrt(total_rows / frob)
    rows = pl.ds(pl.multiple_of(pole * own, own), own)
    mix = 1.5 * zs[0, rows, :] + times(zs[1, rows, :], wn.at[1], False)
    turned_rows = times(mix, turned, False) * size
    out_ref[0] = turned_rows[:, : 2 * width]
    out_ref[1] = turned_rows[:, 2 * width :]
    for copy in sent:
        copy.wait_send()
    if ysize > 2:
        for copy in (*onward(c_all, sem_c), *onward(d_all, sem_d)):
            copy.wait_send()
    handed_out(vk, vin, sem_v, ysize)
    handed_out(wk, win, sem_r, ysize - 1)
    for d in order:
        j, rows = rows_of(d)
        remote(eo.at[rows, :], e_all.at[y], sem_e, j, y, {"y": j}).wait_send()
    for s in range(SUBS):
        @pl.when(jnp.logical_and(z < zsize - 1, jnp.logical_not(lends)))
        def _():
            hop(vo, vz, sem_fz, s, ahead).wait_send()

        @pl.when(skips)
        def _():
            hop(rj, vz, sem_skip, s, two_on).wait_send()

        @pl.when(jnp.logical_or(last, jnp.logical_or(steps, jumps)))
        def _():
            hop(wo, wz, sem_bz, s, behind).wait_send()

        @pl.when(jumps)
        def _():
            hop(rj, wz, sem_far, s, two_back).wait_send()

        @pl.when(z < zsize - 1)
        def _():
            for d in order:
                spread(s, lax.rem(y + d, ysize)).wait_send()

    @pl.when(lends)
    def _():
        remote(cg, dz, sem_one, 2, 2, behind).wait_send()
        remote(qg, rz, sem_one, 3, 3, behind).wait_send()

    @pl.when(feeds)
    def _():
        remote(dg, dz, sem_one, 0, 0, ahead).wait_send()
        remote(rg, rz, sem_one, 1, 1, ahead).wait_send()


def shards(sizes, subspace, pivots, lower_blocks, upper_blocks, pole_weights):
    xsize, zsize, ysize = sizes
    vectors, width = subspace.shape[1], pivots.shape[-1]
    wide = 2 * width
    chunk = vectors // ysize
    poles = 2 * xsize
    part = width // xsize
    own = vectors // poles
    line = own // ysize
    total_rows = float(2 * width * ysize * zsize)

    def dma(count):
        return pltpu.SemaphoreType.DMA((2, count))

    def f32(*shape):
        return pltpu.VMEM(shape, F32)

    def prepared(*counts):
        return pltpu.VMEM((*counts, 2, wide, wide), BF16)

    anywhere = pl.BlockSpec(memory_space=pl.ANY)
    return pl.pallas_call(
        functools.partial(step_kernel, (xsize, zsize, ysize), total_rows),
        out_shape=jax.ShapeDtypeStruct((2, own, wide), F32),
        in_specs=[anywhere] * 4 + [pl.BlockSpec(memory_space=pltpu.SMEM)],
        out_specs=pl.BlockSpec(memory_space=pltpu.VMEM),
        scratch_shapes=[f32(*a.shape) for a in (subspace, pivots, lower_blocks, upper_blocks)]
        + [prepared()] * 4
        + [prepared(2)]
        + [prepared(ysize)] * 2
        + [prepared()] * 7
        + [f32(ysize, width, wide)] * 2
        + [f32(ysize, chunk, wide)] * 2
        + [f32(chunk, wide)] * 4
        + [f32(vectors, wide)] * 10
        + [f32(width, wide)] * 4
        + [f32(chunk, wide)] * 4
        + [f32(ysize, chunk, wide)] * 2
        + [
            f32(2, vectors, wide),
            f32(vectors, wide),
            f32(xsize, vectors, 2 * part),
            f32(xsize, vectors, 2 * part),
            f32(vectors // 2, vectors),
            f32(xsize * ysize, line, vectors),
            f32(zsize, line, vectors),
            f32(vectors, vectors),
            pltpu.VMEM((2, 2, 2 * vectors, 2 * vectors), BF16),
            f32(2, vectors, 2 * vectors),
            pltpu.VMEM((2, 2 * vectors, 2 * wide), BF16),
            f32(2, xsize, vectors, 2 * part),
            pltpu.SemaphoreType.DMA((4,)),
            dma(6),
        ]
        + [dma(ysize), dma(6)]
        + [dma(ysize)] * 3
        + [dma(ysize * SUBS)]
        + [dma(SUBS)] * 2
        + [dma(4)] + [dma(SUBS)] * 2
        + [
            dma(ysize),
            dma(ysize * xsize),
            dma(xsize * ysize),
            dma(zsize),
            dma(poles * ysize),
            dma(2 * xsize),
        ],
        compiler_params=pltpu.CompilerParams(
            collective_id=0, has_side_effects=True, vmem_limit_bytes=60 * 2**20
        ),
        name="step",
    )(subspace, pivots, lower_blocks, upper_blocks, pole_weights)


def build(mesh, sizes):
    xsize, zsize, ysize = sizes
    torus = Mesh(mesh.devices.reshape(xsize, 2, zsize, ysize), AXES)
    pole, rows = ("x", "core"), ("z", "y")
    return jax.shard_map(
        functools.partial(shards, sizes),
        mesh=torus,
        in_specs=(
            P(None, None, rows),
            P(pole, rows, None, None, None),
            P(pole, rows, None, None, None),
            P(pole, rows, None, None, None),
            P(pole, None),
        ),
        out_specs=P(None, pole, rows),
        check_vma=False,
    )


def solution(mesh):
    return build(mesh, (mesh.shape["pole"] // 2, mesh.shape["rows"] // 4, 4))
```

```python
import functools

import jax
import jax.numpy as jnp
from jax import lax
from jax.experimental import pallas as pl
from jax.experimental.pallas import tpu as pltpu
from jax.sharding import Mesh
from jax.sharding import PartitionSpec as P

F32 = jnp.float32
BF16 = jnp.bfloat16
MESH_ID = pl.DeviceIdType.MESH
AXES = ("x", "core", "z", "y")
SUBS = 4


def halves(value):
    high = value.astype(BF16)
    return high, (value - high.astype(F32)).astype(BF16)


def dot(left, right, trans):
    dims = (((1,), (1 if trans else 0,)), ((), ()))
    return lax.dot_general(left, right, dims, preferred_element_type=F32)


def times(rows, weights, trans):
    high, low = halves(rows)
    count = rows.shape[0]
    both = dot(jnp.concatenate([high, low], axis=0), weights[0], trans)
    return both[:count] + both[count:] + dot(high, weights[1], trans)


def prepare(weights, real, minus):
    height, width = real.shape
    for part, (r, m) in enumerate(zip(halves(real), halves(minus))):
        weights[part, :height, :width] = r
        weights[part, :height, width:] = m
        weights[part, height:, :width] = -m
        weights[part, height:, width:] = r


def tiles(count, size, body):
    if count == size:
        body(0)
        return

    def step(i, carry):
        body(pl.multiple_of(i * size, size))
        return carry

    lax.fori_loop(0, count // size, step, 0)


def remote(src, dst, sems, slot_out, slot_in, device):
    return pltpu.make_async_remote_copy(
        src_ref=src,
        dst_ref=dst,
        send_sem=sems.at[0, slot_out],
        recv_sem=sems.at[1, slot_in],
        device_id=device,
        device_id_type=MESH_ID,
    )


def nearest_first(count):
    return sorted(range(1, count), key=lambda d: min(d, count - d))


def step_kernel(
    dims, total_rows, f_hbm, g_hbm, e_hbm, u_hbm, w_ref, out_ref,
    f_ref, g_ref, e_ref, u_ref,
    we0, we1, wf0, wf1, wg, wc, wd, wp, wq, wh, wj, wz1, wa0, wa1,
    c_all, d_all, b_all, e_all, qg, rg, rj, rz, s0, s1, y0, y1, e0, eo, vin, win, tmp, wb, dg, dz, am,
    vz, vo, wz, wo, vk, wk,
    xs, other, cut, got, gram, g1, g3, h1, wn, zs, turned, qall,
    sem_in, sem_c, sem_b, sem_d, sem_v, sem_e, sem_r, sem_w, sem_fz, sem_bz, sem_one, sem_far,
    sem_a, sem_x, sem_1, sem_3, sem_5, sem_q,
):
    xsize, zsize, ysize = dims
    x, core, z, y = (lax.axis_index(a) for a in AXES)
    poles = 2 * xsize
    pole = x * 2 + core
    vectors, width = f_ref.shape[1], g_ref.shape[-1]
    chunk = vectors // ysize
    sub = chunk // SUBS
    tall = min(128, width)
    part = width // xsize
    own = vectors // poles
    line = own // ysize
    order = nearest_first(ysize)

    def pole_of(d):
        p = lax.rem(pole + d, poles)
        return p, {"x": p // 2, "core": lax.rem(p, 2)}

    def along(axis, me, d, size):
        return {axis: lax.rem(me + d, size)}

    barrier = pltpu.get_barrier_semaphore()
    for dp in range(poles):
        for dy in range(ysize):
            if dp or dy:
                device = pole_of(dp)[1] | along("y", y, dy, ysize)
                pl.semaphore_signal(barrier, inc=1, device_id=device, device_id_type=MESH_ID)
    for d in range(1, zsize):
        pl.semaphore_signal(barrier, inc=1, device_id=along("z", z, d, zsize), device_id_type=MESH_ID)

    loads = [
        pltpu.make_async_copy(a, b, sem_in.at[i])
        for i, (a, b) in enumerate(((e_hbm, e_ref), (u_hbm, u_ref), (g_hbm, g_ref), (f_hbm, f_ref)))
    ]
    for load in loads:
        load.start()

    sent = []

    def go(src, dst, sems, d, device):
        copy = remote(src, dst, sems, d, d, device)
        copy.start()
        sent.append(copy)

    def land(dst, sems, d, device):
        remote(dst, dst, sems, d, d, device).wait_recv()

    def back(me, d, size):
        return lax.rem(me + size - d, size)

    def lines(ref, j, count):
        return ref.at[pl.ds(pl.multiple_of(j * count, count), count), :]

    def piece(ref, j):
        return lines(ref, j, chunk)

    loads[0].wait()
    prepare(we0, e_ref[0, 0, 0], -e_ref[0, 0, 1])

    def forward_map(i):
        rows = jnp.concatenate([e_ref[0, 1, 0, pl.ds(i, tall), :], -e_ref[0, 1, 1, pl.ds(i, tall), :]], axis=1)
        c_all[y, pl.ds(i, tall), :] = times(rows, we0, False)

    tiles(width, tall, forward_map)
    pl.semaphore_wait(barrier, ysize * poles + zsize - 2)

    half = width // 2
    right, left = along("y", y, 1, ysize), along("y", y, ysize - 1, ysize)
    before, beyond, far = back(y, 1, ysize), lax.rem(y + 1, ysize), lax.rem(y + 2, ysize)

    def half_of(store, k, h):
        return store.at[k, pl.ds(h * half, half), :]

    def share(store, sems):
        for slot, h, device in ((0, 0, right), (2, 1, left), (1, 1, right), (3, 0, left)):
            if ysize > 2 or slot < 2:
                go(half_of(store, y, h), half_of(store, y, h), sems, slot, device)

    def onward(store, sems):
        first, second = half_of(store, before, 0), half_of(store, beyond, 1)
        return remote(first, first, sems, 4, 4, right), remote(second, second, sems, 5, 5, left)

    def pass_on(store, sems):
        land(half_of(store, before, 0), sems, 0, left)
        if ysize > 2:
            to_right, to_left = onward(store, sems)
            to_right.start()
            land(half_of(store, beyond, 1), sems, 2, right)
            to_left.start()

    def take(store, sems, weights):
        land(half_of(store, before, 1), sems, 1, left)
        prepare(weights.at[before], store[before, :, :width], store[before, :, width:])
        if ysize > 2:
            land(half_of(store, beyond, 0), sems, 3, right)
            prepare(weights.at[beyond], store[beyond, :, :width], store[beyond, :, width:])
            land(half_of(store, far, 0), sems, 4, left)
            land(half_of(store, far, 1), sems, 5, right)
            prepare(weights.at[far], store[far, :, :width], store[far, :, width:])

    share(c_all, sem_c)

    loads[2].wait()
    prepare(wg.at[0], g_ref[0, 0, 0], -g_ref[0, 0, 1])
    prepare(wg.at[1], g_ref[0, 1, 0], -g_ref[0, 1, 1])
    prepare(we1, e_ref[0, 1, 0], -e_ref[0, 1, 1])
    loads[3].wait()

    def local(i):
        rows = pl.ds(i, tall)
        first = jnp.concatenate([f_ref[0, rows, :width], f_ref[1, rows, :width]], axis=1)
        second = jnp.concatenate([f_ref[0, rows, width:], f_ref[1, rows, width:]], axis=1)
        start = times(first, wg.at[0], True)
        s0[rows, :] = start
        s1[rows, :] = times(second, wg.at[1], True) - times(start, we1, True)

    tiles(vectors, tall, local)
    for d in order:
        go(piece(s1, lax.rem(y + d, ysize)), b_all.at[y], sem_b, d, along("y", y, d, ysize))
    b_all[y] = piece(s1, y)[...]

    loads[1].wait()
    prepare(wf1, u_ref[0, 1, 0], -u_ref[0, 1, 1])
    prepare(wf0, u_ref[0, 0, 0], -u_ref[0, 0, 1])
    prepare(wc.at[y], c_all[y, :, :width], c_all[y, :, width:])

    def backward_map(i):
        rows = pl.ds(i, tall)
        upper = jnp.concatenate([u_ref[0, 0, 0, rows, :], -u_ref[0, 0, 1, rows, :]], axis=1)
        d_all[y, rows, :] = times(upper, wf1, False)
        lower = jnp.concatenate([e_ref[0, 0, 0, rows, :], -e_ref[0, 0, 1, rows, :]], axis=1)
        tmp[rows, :] = -lower - times(upper, wc.at[y], False)

    tiles(width, tall, backward_map)
    pass_on(c_all, sem_c)
    prepare(wh, tmp[:width, :width].T, -tmp[:width, width:].T)

    def local_ends(i):
        rows = pl.ds(i, tall)
        e0[rows, :] = s0[rows, :] - times(s1[rows, :], wf0, True)

    tiles(vectors, tall, local_ends)

    take(c_all, sem_c, wc)
    for d in order:
        land(b_all.at[back(y, d, ysize)], sem_b, d, along("y", y, ysize - d, ysize))
    share(d_all, sem_d)

    value = b_all[0]
    for k in range(1, ysize):
        value = times(value, wc.at[k], True) + b_all[k]
    qg[...] = value

    def hop(out, into, sems, s, device):
        return remote(out.at[pl.ds(s * sub, sub), :], into.at[pl.ds(s * sub, sub), :], sems, s, s, device)

    ahead, behind = along("z", z, 1, zsize), along("z", z, zsize - 1, zsize)

    @pl.when(z == 0)
    def _():
        for s in range(SUBS):
            hop(qg, vz, sem_fz, s, ahead).start()
        vz[...] = jnp.zeros_like(vz)

    @pl.when(jnp.logical_and(z > 0, z < zsize - 1))
    def _():
        def group_forward(i):
            value = c_all[ysize - 1, pl.ds(i, tall), :]
            for k in reversed(range(ysize - 1)):
                value = times(value, wc.at[k], False)
            tmp[pl.ds(i, tall), :] = value

        tiles(width, tall, group_forward)
        prepare(wp, tmp[:width, :width].T, -tmp[:width, width:].T)

    early = z < 3
    pl.when(jnp.logical_not(early))(lambda: pass_on(d_all, sem_d))

    for s in range(SUBS):
        rows = pl.ds(s * sub, sub)

        @pl.when(z > 0)
        def _():
            hop(vz, vz, sem_fz, s, behind).wait_recv()

        @pl.when(jnp.logical_and(z > 0, z < zsize - 1))
        def _():
            vo[rows, :] = times(vz[rows, :], wp, False) + qg[rows, :]
            hop(vo, vz, sem_fz, s, ahead).start()

    def hand_out(k, value, staging, into, sems):
        staging[k] = value

        @pl.when(y == k)
        def _():
            piece(into, y)[...] = value

        @pl.when(y != k)
        def _():
            remote(staging.at[k], piece(into, y), sems, k, y, {"y": k}).start()

    def handed_out(staging, into, sems, count):
        for k in range(count):
            @pl.when(y != k)
            def _():
                remote(staging.at[k], piece(into, y), sems, k, y, {"y": k}).wait_send()

    value = vz[...]
    for k in range(ysize):
        hand_out(k, value, vk, vin, sem_v)
        if k < ysize - 1:
            value = times(value, wc.at[k], True) + b_all[k]

    pl.when(early)(lambda: pass_on(d_all, sem_d))

    for d in [0] + order:
        j = lax.rem(y + d, ysize)
        rows = pl.ds(pl.multiple_of(j * chunk, chunk), chunk)
        if d:
            remote(vin.at[rows, :], vin.at[rows, :], sem_v, j, j, {"y": j}).wait_recv()
        ends = e0[rows, :] + times(vin[rows, :], wh, False)
        if d:
            eo[rows, :] = ends
            remote(eo.at[rows, :], e_all.at[y], sem_e, j, y, {"y": j}).start()
        else:
            e_all[y] = ends

    prepare(wd.at[y], d_all[y, :, :width], d_all[y, :, width:])
    take(d_all, sem_d, wd)
    even = lax.rem(z, 2) == 0
    jumps = jnp.logical_and(even, jnp.logical_and(z >= 2, z <= zsize - 4))
    feeds = jnp.logical_and(jnp.logical_not(even), z <= zsize - 5)
    leaps = jnp.logical_and(even, z <= zsize - 6)
    last = z == zsize - 1
    inner = jnp.logical_and(z > 0, z < zsize - 1)
    steps = jnp.logical_and(inner, z >= zsize - 3)

    @pl.when(inner)
    def _():
        def compose(i):
            value = d_all[0, pl.ds(i, tall), :]
            for k in range(1, ysize):
                value = times(value, wd.at[k], False)
            dg[pl.ds(i, tall), :] = value

        tiles(width, tall, compose)

    @pl.when(feeds)
    def _():
        remote(dg, dz, sem_one, 0, 0, ahead).start()

    pl.when(jumps)(lambda: prepare(wq, dg[:, :width], dg[:, width:]))
    pl.when(steps)(lambda: prepare(wq, dg[:, :width].T, -dg[:, width:].T))

    def swept(i):
        rows = pl.ds(i, tall)
        value = vin[rows, :]
        y0[rows, :] = s0[rows, :] - times(value, we0, True)
        y1[rows, :] = s1[rows, :] + times(value, wc.at[y], True)

    tiles(vectors, tall, swept)

    for d in order:
        j = lax.rem(y + d, ysize)
        remote(e_all.at[j], e_all.at[j], sem_e, j, j, {"y": j}).wait_recv()
    values = [e_all[ysize - 1]]
    for k in reversed(range(ysize - 1)):
        values.append(times(values[-1], wd.at[k], True) + e_all[k])
    rg[...] = values[-1]

    @pl.when(last)
    def _():
        for s in range(SUBS):
            hop(rg, wz, sem_bz, s, behind).start()
        wz[...] = jnp.zeros_like(wz)

    @pl.when(feeds)
    def _():
        remote(rg, rz, sem_one, 1, 1, ahead).start()

    for k in range(ysize - 1):
        hand_out(k, values[ysize - 2 - k], wk, win, sem_r)

    @pl.when(jumps)
    def _():
        remote(dz, dz, sem_one, 0, 0, behind).wait_recv()
        prepare(wz1, dz[:, :width], dz[:, width:])

        def joint(i):
            tmp[pl.ds(i, tall), :] = times(dz[pl.ds(i, tall), :], wq, False)

        tiles(width, tall, joint)
        prepare(wj, tmp[:width, :width].T, -tmp[:width, width:].T)
        remote(rz, rz, sem_one, 1, 1, behind).wait_recv()
        rj[...] = times(rg[...], wz1, True) + rz[...]

    def settle():
        @pl.when(y < ysize - 1)
        def _():
            for d in order:
                j = lax.rem(y + d, ysize)
                remote(piece(win, j), piece(win, j), sem_r, j, j, {"y": j}).wait_recv()

            def inner_part(i):
                rows = pl.ds(i, tall)
                y1[rows, :] = y1[rows, :] - times(win[rows, :], wf1, True)

            tiles(vectors, tall, inner_part)

        def first_part(i):
            rows = pl.ds(i, tall)
            y0[rows, :] = y0[rows, :] - times(y1[rows, :], wf0, True)

        tiles(vectors, tall, first_part)

        @pl.when(z < zsize - 1)
        def _():
            am[:, :width] = u_ref[0, 1, 0]
            am[:, width:] = -u_ref[0, 1, 1]
            for k in range(1, ysize):
                @pl.when(k > y)
                def _():
                    def longer(i):
                        am[pl.ds(i, tall), :] = times(am[pl.ds(i, tall), :], wd.at[k], False)

                    tiles(width, tall, longer)
            prepare(wa1, am[:, :width], am[:, width:])

            def both(i):
                rows = pl.ds(i, tall)
                upper = jnp.concatenate([u_ref[0, 0, 0, rows, :], -u_ref[0, 0, 1, rows, :]], axis=1)
                tmp[rows, :] = times(upper, wa1, False)

            tiles(width, tall, both)
            prepare(wa1, am[:, :width].T, -am[:, width:].T)
            prepare(wa0, tmp[:width, :width].T, -tmp[:width, width:].T)

    soon = z >= zsize // 2
    pl.when(jnp.logical_not(soon))(settle)

    two_on, two_back = along("z", z, 2, zsize), along("z", z, zsize - 2, zsize)

    def spread(s, k):
        rows = pl.ds(pl.multiple_of(y * chunk + s * sub, sub), sub)
        return remote(
            wz.at[pl.ds(s * sub, sub), :], wb.at[rows, :], sem_w, k * SUBS + s, y * SUBS + s, {"y": k}
        )

    for s in range(SUBS):
        rows = pl.ds(s * sub, sub)

        @pl.when(leaps)
        def _():
            hop(wz, wz, sem_far, s, two_on).wait_recv()

        @pl.when(jnp.logical_and(z < zsize - 1, jnp.logical_not(leaps)))
        def _():
            hop(wz, wz, sem_bz, s, ahead).wait_recv()

        @pl.when(steps)
        def _():
            wo[rows, :] = times(wz[rows, :], wq, False) + rg[rows, :]
            hop(wo, wz, sem_bz, s, behind).start()

        @pl.when(jumps)
        def _():
            rj[rows, :] = times(wz[rows, :], wj, False) + rj[rows, :]
            hop(rj, wz, sem_far, s, two_back).start()

        @pl.when(z < zsize - 1)
        def _():
            for d in order:
                spread(s, lax.rem(y + d, ysize)).start()

    @pl.when(jumps)
    def _():
        wo[...] = times(wz[...], wq, True) + rg[...]
        for s in range(SUBS):
            hop(wo, wz, sem_bz, s, behind).start()

    pl.when(soon)(settle)

    sibling = {"core": 1 - core}
    wreal, wimag = w_ref[0, 0], w_ref[0, 1]

    def rows_of(d):
        j = lax.rem(y + d, ysize)
        return j, pl.ds(pl.multiple_of(j * chunk, chunk), chunk)

    def over_x(turn, d):
        _, rows = rows_of(d)
        land(other.at[rows, :], sem_a, turn, sibling)
        pair = xs[core, rows, :] + other[rows, :]
        for j in range(xsize):
            cut[j, rows, :] = jnp.concatenate(
                [pair[:, j * part : (j + 1) * part], pair[:, width + j * part : width + (j + 1) * part]], axis=1
            )
        for step in nearest_first(xsize):
            go(
                cut.at[lax.rem(x + step, xsize), rows, :],
                got.at[x, rows, :],
                sem_x,
                turn * xsize + step,
                along("x", x, step, xsize),
            )
        got[x, rows, :] = cut[x, rows, :]

    turns = [0] + order
    for turn, d in enumerate(turns):
        j, rows = rows_of(d)

        @pl.when(z < zsize - 1)
        def _():
            if d:
                for s in range(SUBS):
                    part_rows = pl.ds(pl.multiple_of(j * chunk + s * sub, sub), sub)
                    remote(
                        wb.at[part_rows, :], wb.at[part_rows, :], sem_w, j * SUBS + s, j * SUBS + s, {"y": j}
                    ).wait_recv()
                inflow = wb[rows, :]
            else:
                inflow = wz[...]
            y1[rows, :] = y1[rows, :] - times(inflow, wa1, False)
            y0[rows, :] = y0[rows, :] + times(inflow, wa0, False)

        for n, solved in enumerate((y0, y1)):
            real, imag = solved[rows, :width], solved[rows, width:]
            xs[n, rows, :width] = wreal * real - wimag * imag
            xs[n, rows, width:] = wreal * imag + wimag * real
        go(xs.at[1 - core, rows, :], other.at[rows, :], sem_a, turn, sibling)
        for done in {0: [0], 2: [1, 2]}.get(turn, [turn] if turn == len(turns) - 1 else []):
            over_x(done, turns[done])
    for turn, d in enumerate(turns):
        _, rows = rows_of(d)
        for step in nearest_first(xsize):
            j = back(x, step, xsize)
            land(got.at[j, rows, :], sem_x, turn * xsize + step, {"x": j})
    basis = got[0]
    for j in range(1, xsize):
        basis = basis + got[j]
    qall[core, x] = basis
    go(qall.at[core, x], qall.at[core, x], sem_q, 0, sibling)
    land(qall.at[1 - core, x], sem_q, 0, sibling)
    low_rows = pl.ds(pl.multiple_of(core * (vectors // 2), vectors // 2), vectors // 2)
    left_side = jnp.concatenate([qall[n, x, low_rows, :] for n in range(2)], axis=1)
    right_side = []
    for n in range(2):
        real, imag = qall[n, x, :, :part], qall[n, x, :, part:]
        right_side += [real + imag, imag - real]
    lh, ll = halves(left_side)
    rh, rl = halves(jnp.concatenate(right_side, axis=1))
    gram[...] = dot(lh, rh, True) + dot(ll, rh, True) + dot(lh, rl, True)
    plane = [(dx, dy) for dx in range(xsize) for dy in range(ysize) if dx or dy]
    plane.sort(key=lambda p: min(p[0], xsize - p[0]) + min(p[1], ysize - p[1]))
    here = x * ysize + y
    for dx, dy in plane:
        slot = dx * ysize + dy
        jx, jy = lax.rem(x + dx, xsize), lax.rem(y + dy, ysize)
        go(lines(gram, jx * ysize + jy, line), g1.at[here], sem_1, slot, {"x": jx, "y": jy})
    g1[here] = lines(gram, here, line)[...]
    for step in nearest_first(xsize):
        go(qall.at[core, x], qall.at[core, x], sem_q, step, along("x", x, step, xsize))
    for dx, dy in plane:
        jx, jy = back(x, dx, xsize), back(y, dy, ysize)
        land(g1.at[jx * ysize + jy], sem_1, dx * ysize + dy, {"x": jx, "y": jy})
    value = g1[0]
    for j in range(1, xsize * ysize):
        value = value + g1[j]
    g3[z] = value
    for d in nearest_first(zsize):
        go(g3.at[z], g3.at[z], sem_3, d, {"z": lax.rem(z + d, zsize)})
    for d in nearest_first(zsize):
        j = back(z, d, zsize)
        land(g3.at[j], sem_3, d, {"z": j})
    value = g3[0]
    for j in range(1, zsize):
        value = value + g3[j]
    place = (core * xsize + x) * ysize + y
    lines(h1, place, line)[...] = value
    others = [(dp, dy) for dp in range(poles) for dy in range(ysize) if dp or dy]
    for dp, dy in others:
        device = pole_of(dp)[1] | along("y", y, dy, ysize)
        go(lines(h1, place, line), lines(h1, place, line), sem_5, dp * ysize + dy, device)
    for step in nearest_first(xsize):
        j = back(x, step, xsize)
        land(qall.at[core, j], sem_q, step, {"x": j})
        go(qall.at[core, j], qall.at[core, j], sem_q, xsize + step, sibling)
    for step in nearest_first(xsize):
        land(qall.at[1 - core, back(x, step, xsize)], sem_q, xsize + step, sibling)
    prepare(
        turned,
        jnp.concatenate([qall[n, j, :, :part] for n in range(2) for j in range(xsize)], axis=1),
        jnp.concatenate([qall[n, j, :, part:] for n in range(2) for j in range(xsize)], axis=1),
    )
    for dp, dy in others:
        p, device = pole_of(poles - dp)
        jy = back(y, dy, ysize)
        source = (lax.rem(p, 2) * xsize + p // 2) * ysize + jy
        land(lines(h1, source, line), sem_5, dp * ysize + dy, device | {"y": jy})

    whole = h1[...]
    frob = jnp.sqrt(jnp.sum(whole * whole))
    flip = whole.T
    scale = -0.25 / frob
    eye = (
        lax.broadcasted_iota(jnp.int32, (vectors, vectors), 0)
        == lax.broadcasted_iota(jnp.int32, (vectors, vectors), 1)
    )
    first = jnp.where(eye, 1.5, 0.0) + scale * (whole + flip)
    minus = -scale * (whole - flip)
    prepare(wn.at[0], first, minus)
    zs[0, :, :vectors] = first
    zs[0, :, vectors:] = minus

    def square(i):
        rows = pl.ds(i, tall)
        zs[1, rows, :] = times(zs[0, rows, :], wn.at[0], False)

    tiles(vectors, tall, square)
    prepare(
        wn.at[1],
        zs[1, :, :vectors] - 1.5 * zs[0, :, :vectors],
        zs[1, :, vectors:] - 1.5 * zs[0, :, vectors:],
    )
    size = jnp.sqrt(total_rows / frob)
    rows = pl.ds(pl.multiple_of(pole * own, own), own)
    mix = 1.5 * zs[0, rows, :] + times(zs[1, rows, :], wn.at[1], False)
    turned_rows = times(mix, turned, False) * size
    out_ref[0] = turned_rows[:, : 2 * width]
    out_ref[1] = turned_rows[:, 2 * width :]
    for copy in sent:
        copy.wait_send()
    if ysize > 2:
        for copy in (*onward(c_all, sem_c), *onward(d_all, sem_d)):
            copy.wait_send()
    handed_out(vk, vin, sem_v, ysize)
    handed_out(wk, win, sem_r, ysize - 1)
    for d in order:
        j, rows = rows_of(d)
        remote(eo.at[rows, :], e_all.at[y], sem_e, j, y, {"y": j}).wait_send()
    for s in range(SUBS):
        @pl.when(z < zsize - 1)
        def _():
            hop(vo, vz, sem_fz, s, ahead).wait_send()

        @pl.when(jnp.logical_or(last, jnp.logical_or(steps, jumps)))
        def _():
            hop(wo, wz, sem_bz, s, behind).wait_send()

        @pl.when(jumps)
        def _():
            hop(rj, wz, sem_far, s, two_back).wait_send()

        @pl.when(z < zsize - 1)
        def _():
            for d in order:
                spread(s, lax.rem(y + d, ysize)).wait_send()

    @pl.when(feeds)
    def _():
        remote(dg, dz, sem_one, 0, 0, ahead).wait_send()
        remote(rg, rz, sem_one, 1, 1, ahead).wait_send()


def shards(sizes, subspace, pivots, lower_blocks, upper_blocks, pole_weights):
    xsize, zsize, ysize = sizes
    vectors, width = subspace.shape[1], pivots.shape[-1]
    wide = 2 * width
    chunk = vectors // ysize
    poles = 2 * xsize
    part = width // xsize
    own = vectors // poles
    line = own // ysize
    total_rows = float(2 * width * ysize * zsize)

    def dma(count):
        return pltpu.SemaphoreType.DMA((2, count))

    def f32(*shape):
        return pltpu.VMEM(shape, F32)

    def prepared(*counts):
        return pltpu.VMEM((*counts, 2, wide, wide), BF16)

    anywhere = pl.BlockSpec(memory_space=pl.ANY)
    return pl.pallas_call(
        functools.partial(step_kernel, (xsize, zsize, ysize), total_rows),
        out_shape=jax.ShapeDtypeStruct((2, own, wide), F32),
        in_specs=[anywhere] * 4 + [pl.BlockSpec(memory_space=pltpu.SMEM)],
        out_specs=pl.BlockSpec(memory_space=pltpu.VMEM),
        scratch_shapes=[f32(*a.shape) for a in (subspace, pivots, lower_blocks, upper_blocks)]
        + [prepared()] * 4
        + [prepared(2)]
        + [prepared(ysize)] * 2
        + [prepared()] * 7
        + [f32(ysize, width, wide)] * 2
        + [f32(ysize, chunk, wide)] * 2
        + [f32(chunk, wide)] * 4
        + [f32(vectors, wide)] * 10
        + [f32(width, wide)] * 3
        + [f32(chunk, wide)] * 4
        + [f32(ysize, chunk, wide)] * 2
        + [
            f32(2, vectors, wide),
            f32(vectors, wide),
            f32(xsize, vectors, 2 * part),
            f32(xsize, vectors, 2 * part),
            f32(vectors // 2, vectors),
            f32(xsize * ysize, line, vectors),
            f32(zsize, line, vectors),
            f32(vectors, vectors),
            pltpu.VMEM((2, 2, 2 * vectors, 2 * vectors), BF16),
            f32(2, vectors, 2 * vectors),
            pltpu.VMEM((2, 2 * vectors, 2 * wide), BF16),
            f32(2, xsize, vectors, 2 * part),
            pltpu.SemaphoreType.DMA((4,)),
            dma(6),
        ]
        + [dma(ysize), dma(6)]
        + [dma(ysize)] * 3
        + [dma(ysize * SUBS)]
        + [dma(SUBS)] * 2
        + [dma(2), dma(SUBS)]
        + [
            dma(ysize),
            dma(ysize * xsize),
            dma(xsize * ysize),
            dma(zsize),
            dma(poles * ysize),
            dma(2 * xsize),
        ],
        compiler_params=pltpu.CompilerParams(
            collective_id=0, has_side_effects=True, vmem_limit_bytes=60 * 2**20
        ),
        name="step",
    )(subspace, pivots, lower_blocks, upper_blocks, pole_weights)


def build(mesh, sizes):
    xsize, zsize, ysize = sizes
    torus = Mesh(mesh.devices.reshape(xsize, 2, zsize, ysize), AXES)
    pole, rows = ("x", "core"), ("z", "y")
    return jax.shard_map(
        functools.partial(shards, sizes),
        mesh=torus,
        in_specs=(
            P(None, None, rows),
            P(pole, rows, None, None, None),
            P(pole, rows, None, None, None),
            P(pole, rows, None, None, None),
            P(pole, None),
        ),
        out_specs=P(None, pole, rows),
        check_vma=False,
    )


def solution(mesh):
    return build(mesh, (mesh.shape["pole"] // 2, mesh.shape["rows"] // 4, 4))
```

```python
import functools

import jax
import jax.numpy as jnp
from jax import lax
from jax.experimental import pallas as pl
from jax.experimental.pallas import tpu as pltpu
from jax.sharding import Mesh
from jax.sharding import PartitionSpec as P

F32 = jnp.float32
BF16 = jnp.bfloat16
MESH_ID = pl.DeviceIdType.MESH
AXES = ("x", "core", "z", "y")
SUBS = 4


def halves(value):
    high = value.astype(BF16)
    return high, (value - high.astype(F32)).astype(BF16)


def dot(left, right, trans):
    dims = (((1,), (1 if trans else 0,)), ((), ()))
    return lax.dot_general(left, right, dims, preferred_element_type=F32)


def times(rows, weights, trans):
    high, low = halves(rows)
    count = rows.shape[0]
    both = dot(jnp.concatenate([high, low], axis=0), weights[0], trans)
    return both[:count] + both[count:] + dot(high, weights[1], trans)


def prepare(weights, real, minus):
    height, width = real.shape
    for part, (r, m) in enumerate(zip(halves(real), halves(minus))):
        weights[part, :height, :width] = r
        weights[part, :height, width:] = m
        weights[part, height:, :width] = -m
        weights[part, height:, width:] = r


def tiles(count, size, body):
    if count == size:
        body(0)
        return

    def step(i, carry):
        body(pl.multiple_of(i * size, size))
        return carry

    lax.fori_loop(0, count // size, step, 0)


def remote(src, dst, sems, slot_out, slot_in, device):
    return pltpu.make_async_remote_copy(
        src_ref=src,
        dst_ref=dst,
        send_sem=sems.at[0, slot_out],
        recv_sem=sems.at[1, slot_in],
        device_id=device,
        device_id_type=MESH_ID,
    )


def nearest_first(count):
    return sorted(range(1, count), key=lambda d: min(d, count - d))


def step_kernel(
    dims, total_rows, f_hbm, g_hbm, e_hbm, u_hbm, w_ref, out_ref,
    f_ref, g_ref, e_ref, u_ref,
    we0, we1, wf0, wf1, wg, wc, wd, wp, wq, wh, wj, wz1, wa0, wa1,
    c_all, d_all, b_all, e_all, qg, rg, rj, rz, s0, s1, y0, y1, e0, eo, vin, win, tmp, wb, dg, dz, am,
    vz, vo, wz, wo, vk, wk,
    xs, other, cut, got, gram, g1, g3, h1, wn, zs, turned, qall,
    sem_in, sem_c, sem_b, sem_d, sem_v, sem_e, sem_r, sem_w, sem_fz, sem_bz, sem_one, sem_far,
    sem_a, sem_x, sem_1, sem_3, sem_5, sem_q,
):
    xsize, zsize, ysize = dims
    x, core, z, y = (lax.axis_index(a) for a in AXES)
    poles = 2 * xsize
    pole = x * 2 + core
    vectors, width = f_ref.shape[1], g_ref.shape[-1]
    chunk = vectors // ysize
    sub = chunk // SUBS
    tall = min(256, width)
    part = width // xsize
    own = vectors // poles
    line = own // ysize
    order = nearest_first(ysize)

    def pole_of(d):
        p = lax.rem(pole + d, poles)
        return p, {"x": p // 2, "core": lax.rem(p, 2)}

    def along(axis, me, d, size):
        return {axis: lax.rem(me + d, size)}

    barrier = pltpu.get_barrier_semaphore()
    for dp in range(poles):
        for dy in range(ysize):
            if dp or dy:
                device = pole_of(dp)[1] | along("y", y, dy, ysize)
                pl.semaphore_signal(barrier, inc=1, device_id=device, device_id_type=MESH_ID)
    for d in range(1, zsize):
        pl.semaphore_signal(barrier, inc=1, device_id=along("z", z, d, zsize), device_id_type=MESH_ID)

    loads = [
        pltpu.make_async_copy(a, b, sem_in.at[i])
        for i, (a, b) in enumerate(((e_hbm, e_ref), (u_hbm, u_ref), (g_hbm, g_ref), (f_hbm, f_ref)))
    ]
    for load in loads:
        load.start()

    sent = []

    def go(src, dst, sems, d, device):
        copy = remote(src, dst, sems, d, d, device)
        copy.start()
        sent.append(copy)

    def land(dst, sems, d, device):
        remote(dst, dst, sems, d, d, device).wait_recv()

    def back(me, d, size):
        return lax.rem(me + size - d, size)

    def lines(ref, j, count):
        return ref.at[pl.ds(pl.multiple_of(j * count, count), count), :]

    def piece(ref, j):
        return lines(ref, j, chunk)

    loads[0].wait()
    prepare(we0, e_ref[0, 0, 0], -e_ref[0, 0, 1])

    def forward_map(i):
        rows = jnp.concatenate([e_ref[0, 1, 0, pl.ds(i, tall), :], -e_ref[0, 1, 1, pl.ds(i, tall), :]], axis=1)
        c_all[y, pl.ds(i, tall), :] = times(rows, we0, False)

    tiles(width, tall, forward_map)
    pl.semaphore_wait(barrier, ysize * poles + zsize - 2)

    half = width // 2
    right, left = along("y", y, 1, ysize), along("y", y, ysize - 1, ysize)
    before, beyond, far = back(y, 1, ysize), lax.rem(y + 1, ysize), lax.rem(y + 2, ysize)

    def half_of(store, k, h):
        return store.at[k, pl.ds(h * half, half), :]

    def share(store, sems):
        for slot, h, device in ((0, 0, right), (2, 1, left), (1, 1, right), (3, 0, left)):
            if ysize > 2 or slot < 2:
                go(half_of(store, y, h), half_of(store, y, h), sems, slot, device)

    def onward(store, sems):
        first, second = half_of(store, before, 0), half_of(store, beyond, 1)
        return remote(first, first, sems, 4, 4, right), remote(second, second, sems, 5, 5, left)

    def pass_on(store, sems):
        land(half_of(store, before, 0), sems, 0, left)
        if ysize > 2:
            to_right, to_left = onward(store, sems)
            to_right.start()
            land(half_of(store, beyond, 1), sems, 2, right)
            to_left.start()

    def take(store, sems, weights):
        land(half_of(store, before, 1), sems, 1, left)
        prepare(weights.at[before], store[before, :, :width], store[before, :, width:])
        if ysize > 2:
            land(half_of(store, beyond, 0), sems, 3, right)
            prepare(weights.at[beyond], store[beyond, :, :width], store[beyond, :, width:])
            land(half_of(store, far, 0), sems, 4, left)
            land(half_of(store, far, 1), sems, 5, right)
            prepare(weights.at[far], store[far, :, :width], store[far, :, width:])

    share(c_all, sem_c)

    loads[2].wait()
    prepare(wg.at[0], g_ref[0, 0, 0], -g_ref[0, 0, 1])
    prepare(wg.at[1], g_ref[0, 1, 0], -g_ref[0, 1, 1])
    prepare(we1, e_ref[0, 1, 0], -e_ref[0, 1, 1])
    loads[3].wait()

    def local(i):
        rows = pl.ds(i, tall)
        first = jnp.concatenate([f_ref[0, rows, :width], f_ref[1, rows, :width]], axis=1)
        second = jnp.concatenate([f_ref[0, rows, width:], f_ref[1, rows, width:]], axis=1)
        start = times(first, wg.at[0], True)
        s0[rows, :] = start
        s1[rows, :] = times(second, wg.at[1], True) - times(start, we1, True)

    tiles(vectors, tall, local)
    for d in order:
        go(piece(s1, lax.rem(y + d, ysize)), b_all.at[y], sem_b, d, along("y", y, d, ysize))
    b_all[y] = piece(s1, y)[...]

    loads[1].wait()
    prepare(wf1, u_ref[0, 1, 0], -u_ref[0, 1, 1])
    prepare(wf0, u_ref[0, 0, 0], -u_ref[0, 0, 1])
    prepare(wc.at[y], c_all[y, :, :width], c_all[y, :, width:])

    def backward_map(i):
        rows = pl.ds(i, tall)
        upper = jnp.concatenate([u_ref[0, 0, 0, rows, :], -u_ref[0, 0, 1, rows, :]], axis=1)
        d_all[y, rows, :] = times(upper, wf1, False)
        lower = jnp.concatenate([e_ref[0, 0, 0, rows, :], -e_ref[0, 0, 1, rows, :]], axis=1)
        tmp[rows, :] = -lower - times(upper, wc.at[y], False)

    tiles(width, tall, backward_map)
    pass_on(c_all, sem_c)
    prepare(wh, tmp[:width, :width].T, -tmp[:width, width:].T)

    def local_ends(i):
        rows = pl.ds(i, tall)
        e0[rows, :] = s0[rows, :] - times(s1[rows, :], wf0, True)

    tiles(vectors, tall, local_ends)

    take(c_all, sem_c, wc)
    for d in order:
        land(b_all.at[back(y, d, ysize)], sem_b, d, along("y", y, ysize - d, ysize))
    share(d_all, sem_d)

    value = b_all[0]
    for k in range(1, ysize):
        value = times(value, wc.at[k], True) + b_all[k]
    qg[...] = value

    def hop(out, into, sems, s, device):
        return remote(out.at[pl.ds(s * sub, sub), :], into.at[pl.ds(s * sub, sub), :], sems, s, s, device)

    ahead, behind = along("z", z, 1, zsize), along("z", z, zsize - 1, zsize)

    @pl.when(z == 0)
    def _():
        for s in range(SUBS):
            hop(qg, vz, sem_fz, s, ahead).start()
        vz[...] = jnp.zeros_like(vz)

    @pl.when(jnp.logical_and(z > 0, z < zsize - 1))
    def _():
        def group_forward(i):
            value = c_all[ysize - 1, pl.ds(i, tall), :]
            for k in reversed(range(ysize - 1)):
                value = times(value, wc.at[k], False)
            tmp[pl.ds(i, tall), :] = value

        tiles(width, tall, group_forward)
        prepare(wp, tmp[:width, :width].T, -tmp[:width, width:].T)

    early = z < 3
    pl.when(jnp.logical_not(early))(lambda: pass_on(d_all, sem_d))

    for s in range(SUBS):
        rows = pl.ds(s * sub, sub)

        @pl.when(z > 0)
        def _():
            hop(vz, vz, sem_fz, s, behind).wait_recv()

        @pl.when(jnp.logical_and(z > 0, z < zsize - 1))
        def _():
            vo[rows, :] = times(vz[rows, :], wp, False) + qg[rows, :]
            hop(vo, vz, sem_fz, s, ahead).start()

    def hand_out(k, value, staging, into, sems):
        staging[k] = value

        @pl.when(y == k)
        def _():
            piece(into, y)[...] = value

        @pl.when(y != k)
        def _():
            remote(staging.at[k], piece(into, y), sems, k, y, {"y": k}).start()

    def handed_out(staging, into, sems, count):
        for k in range(count):
            @pl.when(y != k)
            def _():
                remote(staging.at[k], piece(into, y), sems, k, y, {"y": k}).wait_send()

    value = vz[...]
    for k in range(ysize):
        hand_out(k, value, vk, vin, sem_v)
        if k < ysize - 1:
            value = times(value, wc.at[k], True) + b_all[k]

    pl.when(early)(lambda: pass_on(d_all, sem_d))

    for d in [0] + order:
        j = lax.rem(y + d, ysize)
        rows = pl.ds(pl.multiple_of(j * chunk, chunk), chunk)
        if d:
            remote(vin.at[rows, :], vin.at[rows, :], sem_v, j, j, {"y": j}).wait_recv()
        ends = e0[rows, :] + times(vin[rows, :], wh, False)
        if d:
            eo[rows, :] = ends
            remote(eo.at[rows, :], e_all.at[y], sem_e, j, y, {"y": j}).start()
        else:
            e_all[y] = ends

    prepare(wd.at[y], d_all[y, :, :width], d_all[y, :, width:])
    take(d_all, sem_d, wd)
    even = lax.rem(z, 2) == 0
    jumps = jnp.logical_and(even, jnp.logical_and(z >= 2, z <= zsize - 4))
    feeds = jnp.logical_and(jnp.logical_not(even), z <= zsize - 5)
    leaps = jnp.logical_and(even, z <= zsize - 6)
    last = z == zsize - 1
    inner = jnp.logical_and(z > 0, z < zsize - 1)
    steps = jnp.logical_and(inner, z >= zsize - 3)

    @pl.when(inner)
    def _():
        def compose(i):
            value = d_all[0, pl.ds(i, tall), :]
            for k in range(1, ysize):
                value = times(value, wd.at[k], False)
            dg[pl.ds(i, tall), :] = value

        tiles(width, tall, compose)

    @pl.when(feeds)
    def _():
        remote(dg, dz, sem_one, 0, 0, ahead).start()

    pl.when(jumps)(lambda: prepare(wq, dg[:, :width], dg[:, width:]))
    pl.when(steps)(lambda: prepare(wq, dg[:, :width].T, -dg[:, width:].T))

    def swept(i):
        rows = pl.ds(i, tall)
        value = vin[rows, :]
        y0[rows, :] = s0[rows, :] - times(value, we0, True)
        y1[rows, :] = s1[rows, :] + times(value, wc.at[y], True)

    tiles(vectors, tall, swept)

    for d in order:
        j = lax.rem(y + d, ysize)
        remote(e_all.at[j], e_all.at[j], sem_e, j, j, {"y": j}).wait_recv()
    values = [e_all[ysize - 1]]
    for k in reversed(range(ysize - 1)):
        values.append(times(values[-1], wd.at[k], True) + e_all[k])
    rg[...] = values[-1]

    @pl.when(last)
    def _():
        for s in range(SUBS):
            hop(rg, wz, sem_bz, s, behind).start()
        wz[...] = jnp.zeros_like(wz)

    @pl.when(feeds)
    def _():
        remote(rg, rz, sem_one, 1, 1, ahead).start()

    for k in range(ysize - 1):
        hand_out(k, values[ysize - 2 - k], wk, win, sem_r)

    @pl.when(jumps)
    def _():
        remote(dz, dz, sem_one, 0, 0, behind).wait_recv()
        prepare(wz1, dz[:, :width], dz[:, width:])

        def joint(i):
            tmp[pl.ds(i, tall), :] = times(dz[pl.ds(i, tall), :], wq, False)

        tiles(width, tall, joint)
        prepare(wj, tmp[:width, :width].T, -tmp[:width, width:].T)
        remote(rz, rz, sem_one, 1, 1, behind).wait_recv()
        rj[...] = times(rg[...], wz1, True) + rz[...]

    def settle():
        @pl.when(y < ysize - 1)
        def _():
            for d in order:
                j = lax.rem(y + d, ysize)
                remote(piece(win, j), piece(win, j), sem_r, j, j, {"y": j}).wait_recv()

            def inner_part(i):
                rows = pl.ds(i, tall)
                y1[rows, :] = y1[rows, :] - times(win[rows, :], wf1, True)

            tiles(vectors, tall, inner_part)

        def first_part(i):
            rows = pl.ds(i, tall)
            y0[rows, :] = y0[rows, :] - times(y1[rows, :], wf0, True)

        tiles(vectors, tall, first_part)

        @pl.when(z < zsize - 1)
        def _():
            am[:, :width] = u_ref[0, 1, 0]
            am[:, width:] = -u_ref[0, 1, 1]
            for k in range(1, ysize):
                @pl.when(k > y)
                def _():
                    def longer(i):
                        am[pl.ds(i, tall), :] = times(am[pl.ds(i, tall), :], wd.at[k], False)

                    tiles(width, tall, longer)
            prepare(wa1, am[:, :width], am[:, width:])

            def both(i):
                rows = pl.ds(i, tall)
                upper = jnp.concatenate([u_ref[0, 0, 0, rows, :], -u_ref[0, 0, 1, rows, :]], axis=1)
                tmp[rows, :] = times(upper, wa1, False)

            tiles(width, tall, both)
            prepare(wa1, am[:, :width].T, -am[:, width:].T)
            prepare(wa0, tmp[:width, :width].T, -tmp[:width, width:].T)

    soon = z >= zsize // 2
    pl.when(jnp.logical_not(soon))(settle)

    two_on, two_back = along("z", z, 2, zsize), along("z", z, zsize - 2, zsize)

    def spread(s, k):
        rows = pl.ds(pl.multiple_of(y * chunk + s * sub, sub), sub)
        return remote(
            wz.at[pl.ds(s * sub, sub), :], wb.at[rows, :], sem_w, k * SUBS + s, y * SUBS + s, {"y": k}
        )

    for s in range(SUBS):
        rows = pl.ds(s * sub, sub)

        @pl.when(leaps)
        def _():
            hop(wz, wz, sem_far, s, two_on).wait_recv()

        @pl.when(jnp.logical_and(z < zsize - 1, jnp.logical_not(leaps)))
        def _():
            hop(wz, wz, sem_bz, s, ahead).wait_recv()

        @pl.when(steps)
        def _():
            wo[rows, :] = times(wz[rows, :], wq, False) + rg[rows, :]
            hop(wo, wz, sem_bz, s, behind).start()

        @pl.when(jumps)
        def _():
            rj[rows, :] = times(wz[rows, :], wj, False) + rj[rows, :]
            hop(rj, wz, sem_far, s, two_back).start()

        @pl.when(z < zsize - 1)
        def _():
            for d in order:
                spread(s, lax.rem(y + d, ysize)).start()

    @pl.when(jumps)
    def _():
        wo[...] = times(wz[...], wq, True) + rg[...]
        for s in range(SUBS):
            hop(wo, wz, sem_bz, s, behind).start()

    pl.when(soon)(settle)

    sibling = {"core": 1 - core}
    wreal, wimag = w_ref[0, 0], w_ref[0, 1]

    def rows_of(d):
        j = lax.rem(y + d, ysize)
        return j, pl.ds(pl.multiple_of(j * chunk, chunk), chunk)

    def over_x(turn, d):
        _, rows = rows_of(d)
        land(other.at[rows, :], sem_a, turn, sibling)
        pair = xs[core, rows, :] + other[rows, :]
        for j in range(xsize):
            cut[j, rows, :] = jnp.concatenate(
                [pair[:, j * part : (j + 1) * part], pair[:, width + j * part : width + (j + 1) * part]], axis=1
            )
        for step in nearest_first(xsize):
            go(
                cut.at[lax.rem(x + step, xsize), rows, :],
                got.at[x, rows, :],
                sem_x,
                turn * xsize + step,
                along("x", x, step, xsize),
            )
        got[x, rows, :] = cut[x, rows, :]

    turns = [0] + order
    for turn, d in enumerate(turns):
        j, rows = rows_of(d)

        @pl.when(z < zsize - 1)
        def _():
            if d:
                for s in range(SUBS):
                    part_rows = pl.ds(pl.multiple_of(j * chunk + s * sub, sub), sub)
                    remote(
                        wb.at[part_rows, :], wb.at[part_rows, :], sem_w, j * SUBS + s, j * SUBS + s, {"y": j}
                    ).wait_recv()
                inflow = wb[rows, :]
            else:
                inflow = wz[...]
            y1[rows, :] = y1[rows, :] - times(inflow, wa1, False)
            y0[rows, :] = y0[rows, :] + times(inflow, wa0, False)

        for n, solved in enumerate((y0, y1)):
            real, imag = solved[rows, :width], solved[rows, width:]
            xs[n, rows, :width] = wreal * real - wimag * imag
            xs[n, rows, width:] = wreal * imag + wimag * real
        go(xs.at[1 - core, rows, :], other.at[rows, :], sem_a, turn, sibling)
        for done in {0: [0], 2: [1, 2]}.get(turn, [turn] if turn == len(turns) - 1 else []):
            over_x(done, turns[done])
    for turn, d in enumerate(turns):
        _, rows = rows_of(d)
        for step in nearest_first(xsize):
            j = back(x, step, xsize)
            land(got.at[j, rows, :], sem_x, turn * xsize + step, {"x": j})
    basis = got[0]
    for j in range(1, xsize):
        basis = basis + got[j]
    qall[core, x] = basis
    go(qall.at[core, x], qall.at[core, x], sem_q, 0, sibling)
    land(qall.at[1 - core, x], sem_q, 0, sibling)
    low_rows = pl.ds(pl.multiple_of(core * (vectors // 2), vectors // 2), vectors // 2)
    left_side = jnp.concatenate([qall[n, x, low_rows, :] for n in range(2)], axis=1)
    right_side = []
    for n in range(2):
        real, imag = qall[n, x, :, :part], qall[n, x, :, part:]
        right_side += [real + imag, imag - real]
    lh, ll = halves(left_side)
    rh, rl = halves(jnp.concatenate(right_side, axis=1))
    gram[...] = dot(lh, rh, True) + dot(ll, rh, True) + dot(lh, rl, True)
    plane = [(dx, dy) for dx in range(xsize) for dy in range(ysize) if dx or dy]
    plane.sort(key=lambda p: min(p[0], xsize - p[0]) + min(p[1], ysize - p[1]))
    here = x * ysize + y
    for dx, dy in plane:
        slot = dx * ysize + dy
        jx, jy = lax.rem(x + dx, xsize), lax.rem(y + dy, ysize)
        go(lines(gram, jx * ysize + jy, line), g1.at[here], sem_1, slot, {"x": jx, "y": jy})
    g1[here] = lines(gram, here, line)[...]
    for step in nearest_first(xsize):
        go(qall.at[core, x], qall.at[core, x], sem_q, step, along("x", x, step, xsize))
    for dx, dy in plane:
        jx, jy = back(x, dx, xsize), back(y, dy, ysize)
        land(g1.at[jx * ysize + jy], sem_1, dx * ysize + dy, {"x": jx, "y": jy})
    value = g1[0]
    for j in range(1, xsize * ysize):
        value = value + g1[j]
    g3[z] = value
    for d in nearest_first(zsize):
        go(g3.at[z], g3.at[z], sem_3, d, {"z": lax.rem(z + d, zsize)})
    for d in nearest_first(zsize):
        j = back(z, d, zsize)
        land(g3.at[j], sem_3, d, {"z": j})
    value = g3[0]
    for j in range(1, zsize):
        value = value + g3[j]
    place = (core * xsize + x) * ysize + y
    lines(h1, place, line)[...] = value
    others = [(dp, dy) for dp in range(poles) for dy in range(ysize) if dp or dy]
    for dp, dy in others:
        device = pole_of(dp)[1] | along("y", y, dy, ysize)
        go(lines(h1, place, line), lines(h1, place, line), sem_5, dp * ysize + dy, device)
    for step in nearest_first(xsize):
        j = back(x, step, xsize)
        land(qall.at[core, j], sem_q, step, {"x": j})
        go(qall.at[core, j], qall.at[core, j], sem_q, xsize + step, sibling)
    for step in nearest_first(xsize):
        land(qall.at[1 - core, back(x, step, xsize)], sem_q, xsize + step, sibling)
    prepare(
        turned,
        jnp.concatenate([qall[n, j, :, :part] for n in range(2) for j in range(xsize)], axis=1),
        jnp.concatenate([qall[n, j, :, part:] for n in range(2) for j in range(xsize)], axis=1),
    )
    for dp, dy in others:
        p, device = pole_of(poles - dp)
        jy = back(y, dy, ysize)
        source = (lax.rem(p, 2) * xsize + p // 2) * ysize + jy
        land(lines(h1, source, line), sem_5, dp * ysize + dy, device | {"y": jy})

    whole = h1[...]
    frob = jnp.sqrt(jnp.sum(whole * whole))
    flip = whole.T
    scale = -0.25 / frob
    eye = (
        lax.broadcasted_iota(jnp.int32, (vectors, vectors), 0)
        == lax.broadcasted_iota(jnp.int32, (vectors, vectors), 1)
    )
    first = jnp.where(eye, 1.5, 0.0) + scale * (whole + flip)
    minus = -scale * (whole - flip)
    prepare(wn.at[0], first, minus)
    zs[0, :, :vectors] = first
    zs[0, :, vectors:] = minus

    def square(i):
        rows = pl.ds(i, tall)
        zs[1, rows, :] = times(zs[0, rows, :], wn.at[0], False)

    tiles(vectors, tall, square)
    prepare(
        wn.at[1],
        zs[1, :, :vectors] - 1.5 * zs[0, :, :vectors],
        zs[1, :, vectors:] - 1.5 * zs[0, :, vectors:],
    )
    size = jnp.sqrt(total_rows / frob)
    rows = pl.ds(pl.multiple_of(pole * own, own), own)
    mix = 1.5 * zs[0, rows, :] + times(zs[1, rows, :], wn.at[1], False)
    turned_rows = times(mix, turned, False) * size
    out_ref[0] = turned_rows[:, : 2 * width]
    out_ref[1] = turned_rows[:, 2 * width :]
    for copy in sent:
        copy.wait_send()
    if ysize > 2:
        for copy in (*onward(c_all, sem_c), *onward(d_all, sem_d)):
            copy.wait_send()
    handed_out(vk, vin, sem_v, ysize)
    handed_out(wk, win, sem_r, ysize - 1)
    for d in order:
        j, rows = rows_of(d)
        remote(eo.at[rows, :], e_all.at[y], sem_e, j, y, {"y": j}).wait_send()
    for s in range(SUBS):
        @pl.when(z < zsize - 1)
        def _():
            hop(vo, vz, sem_fz, s, ahead).wait_send()

        @pl.when(jnp.logical_or(last, jnp.logical_or(steps, jumps)))
        def _():
            hop(wo, wz, sem_bz, s, behind).wait_send()

        @pl.when(jumps)
        def _():
            hop(rj, wz, sem_far, s, two_back).wait_send()

        @pl.when(z < zsize - 1)
        def _():
            for d in order:
                spread(s, lax.rem(y + d, ysize)).wait_send()

    @pl.when(feeds)
    def _():
        remote(dg, dz, sem_one, 0, 0, ahead).wait_send()
        remote(rg, rz, sem_one, 1, 1, ahead).wait_send()


def shards(sizes, subspace, pivots, lower_blocks, upper_blocks, pole_weights):
    xsize, zsize, ysize = sizes
    vectors, width = subspace.shape[1], pivots.shape[-1]
    wide = 2 * width
    chunk = vectors // ysize
    poles = 2 * xsize
    part = width // xsize
    own = vectors // poles
    line = own // ysize
    total_rows = float(2 * width * ysize * zsize)

    def dma(count):
        return pltpu.SemaphoreType.DMA((2, count))

    def f32(*shape):
        return pltpu.VMEM(shape, F32)

    def prepared(*counts):
        return pltpu.VMEM((*counts, 2, wide, wide), BF16)

    anywhere = pl.BlockSpec(memory_space=pl.ANY)
    return pl.pallas_call(
        functools.partial(step_kernel, (xsize, zsize, ysize), total_rows),
        out_shape=jax.ShapeDtypeStruct((2, own, wide), F32),
        in_specs=[anywhere] * 4 + [pl.BlockSpec(memory_space=pltpu.SMEM)],
        out_specs=pl.BlockSpec(memory_space=pltpu.VMEM),
        scratch_shapes=[f32(*a.shape) for a in (subspace, pivots, lower_blocks, upper_blocks)]
        + [prepared()] * 4
        + [prepared(2)]
        + [prepared(ysize)] * 2
        + [prepared()] * 7
        + [f32(ysize, width, wide)] * 2
        + [f32(ysize, chunk, wide)] * 2
        + [f32(chunk, wide)] * 4
        + [f32(vectors, wide)] * 10
        + [f32(width, wide)] * 3
        + [f32(chunk, wide)] * 4
        + [f32(ysize, chunk, wide)] * 2
        + [
            f32(2, vectors, wide),
            f32(vectors, wide),
            f32(xsize, vectors, 2 * part),
            f32(xsize, vectors, 2 * part),
            f32(vectors // 2, vectors),
            f32(xsize * ysize, line, vectors),
            f32(zsize, line, vectors),
            f32(vectors, vectors),
            pltpu.VMEM((2, 2, 2 * vectors, 2 * vectors), BF16),
            f32(2, vectors, 2 * vectors),
            pltpu.VMEM((2, 2 * vectors, 2 * wide), BF16),
            f32(2, xsize, vectors, 2 * part),
            pltpu.SemaphoreType.DMA((4,)),
            dma(6),
        ]
        + [dma(ysize), dma(6)]
        + [dma(ysize)] * 3
        + [dma(ysize * SUBS)]
        + [dma(SUBS)] * 2
        + [dma(2), dma(SUBS)]
        + [
            dma(ysize),
            dma(ysize * xsize),
            dma(xsize * ysize),
            dma(zsize),
            dma(poles * ysize),
            dma(2 * xsize),
        ],
        compiler_params=pltpu.CompilerParams(
            collective_id=0, has_side_effects=True, vmem_limit_bytes=60 * 2**20
        ),
        name="step",
    )(subspace, pivots, lower_blocks, upper_blocks, pole_weights)


def build(mesh, sizes):
    xsize, zsize, ysize = sizes
    torus = Mesh(mesh.devices.reshape(xsize, 2, zsize, ysize), AXES)
    pole, rows = ("x", "core"), ("z", "y")
    return jax.shard_map(
        functools.partial(shards, sizes),
        mesh=torus,
        in_specs=(
            P(None, None, rows),
            P(pole, rows, None, None, None),
            P(pole, rows, None, None, None),
            P(pole, rows, None, None, None),
            P(pole, None),
        ),
        out_specs=P(None, pole, rows),
        check_vma=False,
    )


def solution(mesh):
    return build(mesh, (mesh.shape["pole"] // 2, mesh.shape["rows"] // 4, 4))
```

```python
import functools

import jax
import jax.numpy as jnp
from jax import lax
from jax.experimental import pallas as pl
from jax.experimental.pallas import tpu as pltpu
from jax.sharding import Mesh
from jax.sharding import PartitionSpec as P

F32 = jnp.float32
BF16 = jnp.bfloat16
MESH_ID = pl.DeviceIdType.MESH
AXES = ("x", "core", "z", "y")
SUBS = 4


def halves(value):
    high = value.astype(BF16)
    return high, (value - high.astype(F32)).astype(BF16)


def dot(left, right, trans):
    dims = (((1,), (1 if trans else 0,)), ((), ()))
    return lax.dot_general(left, right, dims, preferred_element_type=F32)


def times(rows, weights, trans):
    high, low = halves(rows)
    count = rows.shape[0]
    both = dot(jnp.concatenate([high, low], axis=0), weights[0], trans)
    return both[:count] + both[count:] + dot(high, weights[1], trans)


def prepare(weights, real, minus):
    height, width = real.shape
    for part, (r, m) in enumerate(zip(halves(real), halves(minus))):
        weights[part, :height, :width] = r
        weights[part, :height, width:] = m
        weights[part, height:, :width] = -m
        weights[part, height:, width:] = r


def tiles(count, size, body):
    if count == size:
        body(0)
        return

    def step(i, carry):
        body(pl.multiple_of(i * size, size))
        return carry

    lax.fori_loop(0, count // size, step, 0)


def remote(src, dst, sems, slot_out, slot_in, device):
    return pltpu.make_async_remote_copy(
        src_ref=src,
        dst_ref=dst,
        send_sem=sems.at[0, slot_out],
        recv_sem=sems.at[1, slot_in],
        device_id=device,
        device_id_type=MESH_ID,
    )


def nearest_first(count):
    return sorted(range(1, count), key=lambda d: min(d, count - d))


def step_kernel(
    dims, total_rows, f_hbm, g_hbm, e_hbm, u_hbm, w_ref, out_ref,
    f_ref, g_ref, e_ref, u_ref,
    we0, we1, wf0, wf1, wg, wc, wd, wp, wq, wh, wj, wz1, wa0, wa1,
    c_all, d_all, b_all, e_all, qg, rg, rj, rz, s0, s1, y0, y1, e0, eo, vin, win, tmp, wb, dg, dz, am,
    vz, vo, wz, wo, vk, wk,
    xs, other, cut, got, gram, g1, g3, h1, wn, zs, turned, qall,
    sem_in, sem_c, sem_b, sem_d, sem_v, sem_e, sem_r, sem_w, sem_fz, sem_bz, sem_one, sem_far,
    sem_a, sem_x, sem_1, sem_3, sem_5, sem_q,
):
    xsize, zsize, ysize = dims
    x, core, z, y = (lax.axis_index(a) for a in AXES)
    poles = 2 * xsize
    pole = x * 2 + core
    vectors, width = f_ref.shape[1], g_ref.shape[-1]
    chunk = vectors // ysize
    sub = chunk // SUBS
    tall = min(256, width)
    part = width // xsize
    own = vectors // poles
    line = own // ysize
    order = nearest_first(ysize)

    def pole_of(d):
        p = lax.rem(pole + d, poles)
        return p, {"x": p // 2, "core": lax.rem(p, 2)}

    def along(axis, me, d, size):
        return {axis: lax.rem(me + d, size)}

    barrier = pltpu.get_barrier_semaphore()
    for dp in range(poles):
        for dy in range(ysize):
            if dp or dy:
                device = pole_of(dp)[1] | along("y", y, dy, ysize)
                pl.semaphore_signal(barrier, inc=1, device_id=device, device_id_type=MESH_ID)
    for d in range(1, zsize):
        pl.semaphore_signal(barrier, inc=1, device_id=along("z", z, d, zsize), device_id_type=MESH_ID)

    loads = [
        pltpu.make_async_copy(a, b, sem_in.at[i])
        for i, (a, b) in enumerate(((e_hbm, e_ref), (u_hbm, u_ref), (g_hbm, g_ref), (f_hbm, f_ref)))
    ]
    for load in loads:
        load.start()

    sent = []

    def go(src, dst, sems, d, device):
        copy = remote(src, dst, sems, d, d, device)
        copy.start()
        sent.append(copy)

    def land(dst, sems, d, device):
        remote(dst, dst, sems, d, d, device).wait_recv()

    def back(me, d, size):
        return lax.rem(me + size - d, size)

    def lines(ref, j, count):
        return ref.at[pl.ds(pl.multiple_of(j * count, count), count), :]

    def piece(ref, j):
        return lines(ref, j, chunk)

    loads[0].wait()
    prepare(we0, e_ref[0, 0, 0], -e_ref[0, 0, 1])

    def forward_map(i):
        rows = jnp.concatenate([e_ref[0, 1, 0, pl.ds(i, tall), :], -e_ref[0, 1, 1, pl.ds(i, tall), :]], axis=1)
        c_all[y, pl.ds(i, tall), :] = times(rows, we0, False)

    tiles(width, tall, forward_map)
    pl.semaphore_wait(barrier, ysize * poles + zsize - 2)

    half = width // 2
    right, left = along("y", y, 1, ysize), along("y", y, ysize - 1, ysize)
    before, beyond, far = back(y, 1, ysize), lax.rem(y + 1, ysize), lax.rem(y + 2, ysize)

    def half_of(store, k, h):
        return store.at[k, pl.ds(h * half, half), :]

    def share(store, sems):
        for slot, h, device in ((0, 0, right), (2, 1, left), (1, 1, right), (3, 0, left)):
            if ysize > 2 or slot < 2:
                go(half_of(store, y, h), half_of(store, y, h), sems, slot, device)

    def onward(store, sems):
        first, second = half_of(store, before, 0), half_of(store, beyond, 1)
        return remote(first, first, sems, 4, 4, right), remote(second, second, sems, 5, 5, left)

    def pass_on(store, sems):
        land(half_of(store, before, 0), sems, 0, left)
        if ysize > 2:
            to_right, to_left = onward(store, sems)
            to_right.start()
            land(half_of(store, beyond, 1), sems, 2, right)
            to_left.start()

    def take(store, sems, weights):
        land(half_of(store, before, 1), sems, 1, left)
        prepare(weights.at[before], store[before, :, :width], store[before, :, width:])
        if ysize > 2:
            land(half_of(store, beyond, 0), sems, 3, right)
            prepare(weights.at[beyond], store[beyond, :, :width], store[beyond, :, width:])
            land(half_of(store, far, 0), sems, 4, left)
            land(half_of(store, far, 1), sems, 5, right)
            prepare(weights.at[far], store[far, :, :width], store[far, :, width:])

    share(c_all, sem_c)

    loads[2].wait()
    prepare(wg.at[0], g_ref[0, 0, 0], -g_ref[0, 0, 1])
    prepare(wg.at[1], g_ref[0, 1, 0], -g_ref[0, 1, 1])
    prepare(we1, e_ref[0, 1, 0], -e_ref[0, 1, 1])
    loads[3].wait()

    def local(i):
        rows = pl.ds(i, tall)
        first = jnp.concatenate([f_ref[0, rows, :width], f_ref[1, rows, :width]], axis=1)
        second = jnp.concatenate([f_ref[0, rows, width:], f_ref[1, rows, width:]], axis=1)
        start = times(first, wg.at[0], True)
        s0[rows, :] = start
        s1[rows, :] = times(second, wg.at[1], True) - times(start, we1, True)

    tiles(vectors, tall, local)
    for d in order:
        go(piece(s1, lax.rem(y + d, ysize)), b_all.at[y], sem_b, d, along("y", y, d, ysize))
    b_all[y] = piece(s1, y)[...]

    loads[1].wait()
    prepare(wf1, u_ref[0, 1, 0], -u_ref[0, 1, 1])
    prepare(wf0, u_ref[0, 0, 0], -u_ref[0, 0, 1])
    prepare(wc.at[y], c_all[y, :, :width], c_all[y, :, width:])

    def backward_map(i):
        rows = pl.ds(i, tall)
        upper = jnp.concatenate([u_ref[0, 0, 0, rows, :], -u_ref[0, 0, 1, rows, :]], axis=1)
        d_all[y, rows, :] = times(upper, wf1, False)
        lower = jnp.concatenate([e_ref[0, 0, 0, rows, :], -e_ref[0, 0, 1, rows, :]], axis=1)
        tmp[rows, :] = -lower - times(upper, wc.at[y], False)

    tiles(width, tall, backward_map)
    pass_on(c_all, sem_c)
    prepare(wh, tmp[:width, :width].T, -tmp[:width, width:].T)

    def local_ends(i):
        rows = pl.ds(i, tall)
        e0[rows, :] = s0[rows, :] - times(s1[rows, :], wf0, True)

    tiles(vectors, tall, local_ends)

    take(c_all, sem_c, wc)
    for d in order:
        land(b_all.at[back(y, d, ysize)], sem_b, d, along("y", y, ysize - d, ysize))
    share(d_all, sem_d)

    value = b_all[0]
    for k in range(1, ysize):
        value = times(value, wc.at[k], True) + b_all[k]
    qg[...] = value

    def hop(out, into, sems, s, device):
        return remote(out.at[pl.ds(s * sub, sub), :], into.at[pl.ds(s * sub, sub), :], sems, s, s, device)

    ahead, behind = along("z", z, 1, zsize), along("z", z, zsize - 1, zsize)

    @pl.when(z == 0)
    def _():
        for s in range(SUBS):
            hop(qg, vz, sem_fz, s, ahead).start()
        vz[...] = jnp.zeros_like(vz)

    @pl.when(jnp.logical_and(z > 0, z < zsize - 1))
    def _():
        def group_forward(i):
            value = c_all[ysize - 1, pl.ds(i, tall), :]
            for k in reversed(range(ysize - 1)):
                value = times(value, wc.at[k], False)
            tmp[pl.ds(i, tall), :] = value

        tiles(width, tall, group_forward)
        prepare(wp, tmp[:width, :width].T, -tmp[:width, width:].T)

    early = z < 3
    pl.when(jnp.logical_not(early))(lambda: pass_on(d_all, sem_d))

    for s in range(SUBS):
        rows = pl.ds(s * sub, sub)

        @pl.when(z > 0)
        def _():
            hop(vz, vz, sem_fz, s, behind).wait_recv()

        @pl.when(jnp.logical_and(z > 0, z < zsize - 1))
        def _():
            vo[rows, :] = times(vz[rows, :], wp, False) + qg[rows, :]
            hop(vo, vz, sem_fz, s, ahead).start()

    def hand_out(k, value, staging, into, sems):
        staging[k] = value

        @pl.when(y == k)
        def _():
            piece(into, y)[...] = value

        @pl.when(y != k)
        def _():
            remote(staging.at[k], piece(into, y), sems, k, y, {"y": k}).start()

    def handed_out(staging, into, sems, count):
        for k in range(count):
            @pl.when(y != k)
            def _():
                remote(staging.at[k], piece(into, y), sems, k, y, {"y": k}).wait_send()

    value = vz[...]
    for k in range(ysize):
        hand_out(k, value, vk, vin, sem_v)
        if k < ysize - 1:
            value = times(value, wc.at[k], True) + b_all[k]

    pl.when(early)(lambda: pass_on(d_all, sem_d))

    for d in [0] + order:
        j = lax.rem(y + d, ysize)
        rows = pl.ds(pl.multiple_of(j * chunk, chunk), chunk)
        if d:
            remote(vin.at[rows, :], vin.at[rows, :], sem_v, j, j, {"y": j}).wait_recv()
        ends = e0[rows, :] + times(vin[rows, :], wh, False)
        if d:
            eo[rows, :] = ends
            remote(eo.at[rows, :], e_all.at[y], sem_e, j, y, {"y": j}).start()
        else:
            e_all[y] = ends

    prepare(wd.at[y], d_all[y, :, :width], d_all[y, :, width:])
    take(d_all, sem_d, wd)
    even = lax.rem(z, 2) == 0
    jumps = jnp.logical_and(even, jnp.logical_and(z >= 2, z <= zsize - 4))
    feeds = jnp.logical_and(jnp.logical_not(even), z <= zsize - 5)
    leaps = jnp.logical_and(even, z <= zsize - 6)
    last = z == zsize - 1
    inner = jnp.logical_and(z > 0, z < zsize - 1)
    steps = jnp.logical_and(inner, z >= zsize - 3)

    @pl.when(inner)
    def _():
        def compose(i):
            value = d_all[0, pl.ds(i, tall), :]
            for k in range(1, ysize):
                value = times(value, wd.at[k], False)
            dg[pl.ds(i, tall), :] = value

        tiles(width, tall, compose)

    @pl.when(feeds)
    def _():
        remote(dg, dz, sem_one, 0, 0, ahead).start()

    pl.when(jumps)(lambda: prepare(wq, dg[:, :width], dg[:, width:]))
    pl.when(steps)(lambda: prepare(wq, dg[:, :width].T, -dg[:, width:].T))

    def swept(i):
        rows = pl.ds(i, tall)
        value = vin[rows, :]
        y0[rows, :] = s0[rows, :] - times(value, we0, True)
        y1[rows, :] = s1[rows, :] + times(value, wc.at[y], True)

    tiles(vectors, tall, swept)

    for d in order:
        j = lax.rem(y + d, ysize)
        remote(e_all.at[j], e_all.at[j], sem_e, j, j, {"y": j}).wait_recv()
    values = [e_all[ysize - 1]]
    for k in reversed(range(ysize - 1)):
        values.append(times(values[-1], wd.at[k], True) + e_all[k])
    rg[...] = values[-1]

    @pl.when(last)
    def _():
        for s in range(SUBS):
            hop(rg, wz, sem_bz, s, behind).start()
        wz[...] = jnp.zeros_like(wz)

    @pl.when(feeds)
    def _():
        remote(rg, rz, sem_one, 1, 1, ahead).start()

    for k in range(ysize - 1):
        hand_out(k, values[ysize - 2 - k], wk, win, sem_r)

    @pl.when(jumps)
    def _():
        remote(dz, dz, sem_one, 0, 0, behind).wait_recv()
        prepare(wz1, dz[:, :width], dz[:, width:])

        def joint(i):
            tmp[pl.ds(i, tall), :] = times(dz[pl.ds(i, tall), :], wq, False)

        tiles(width, tall, joint)
        prepare(wj, tmp[:width, :width].T, -tmp[:width, width:].T)
        remote(rz, rz, sem_one, 1, 1, behind).wait_recv()
        rj[...] = times(rg[...], wz1, True) + rz[...]

    def settle():
        @pl.when(y < ysize - 1)
        def _():
            for d in order:
                j = lax.rem(y + d, ysize)
                remote(piece(win, j), piece(win, j), sem_r, j, j, {"y": j}).wait_recv()

            def inner_part(i):
                rows = pl.ds(i, tall)
                y1[rows, :] = y1[rows, :] - times(win[rows, :], wf1, True)

            tiles(vectors, tall, inner_part)

        def first_part(i):
            rows = pl.ds(i, tall)
            y0[rows, :] = y0[rows, :] - times(y1[rows, :], wf0, True)

        tiles(vectors, tall, first_part)

        @pl.when(z < zsize - 1)
        def _():
            am[:, :width] = u_ref[0, 1, 0]
            am[:, width:] = -u_ref[0, 1, 1]
            for k in range(1, ysize):
                @pl.when(k > y)
                def _():
                    def longer(i):
                        am[pl.ds(i, tall), :] = times(am[pl.ds(i, tall), :], wd.at[k], False)

                    tiles(width, tall, longer)
            prepare(wa1, am[:, :width], am[:, width:])

            def both(i):
                rows = pl.ds(i, tall)
                upper = jnp.concatenate([u_ref[0, 0, 0, rows, :], -u_ref[0, 0, 1, rows, :]], axis=1)
                tmp[rows, :] = times(upper, wa1, False)

            tiles(width, tall, both)
            prepare(wa1, am[:, :width].T, -am[:, width:].T)
            prepare(wa0, tmp[:width, :width].T, -tmp[:width, width:].T)

    soon = z >= zsize // 2
    pl.when(jnp.logical_not(soon))(settle)

    two_on, two_back = along("z", z, 2, zsize), along("z", z, zsize - 2, zsize)

    def spread(s, k):
        rows = pl.ds(pl.multiple_of(y * chunk + s * sub, sub), sub)
        return remote(
            wz.at[pl.ds(s * sub, sub), :], wb.at[rows, :], sem_w, k * SUBS + s, y * SUBS + s, {"y": k}
        )

    for s in range(SUBS):
        rows = pl.ds(s * sub, sub)

        @pl.when(leaps)
        def _():
            hop(wz, wz, sem_far, s, two_on).wait_recv()

        @pl.when(jnp.logical_and(z < zsize - 1, jnp.logical_not(leaps)))
        def _():
            hop(wz, wz, sem_bz, s, ahead).wait_recv()

        @pl.when(steps)
        def _():
            wo[rows, :] = times(wz[rows, :], wq, False) + rg[rows, :]
            hop(wo, wz, sem_bz, s, behind).start()

        @pl.when(jumps)
        def _():
            rj[rows, :] = times(wz[rows, :], wj, False) + rj[rows, :]
            hop(rj, wz, sem_far, s, two_back).start()

        @pl.when(z < zsize - 1)
        def _():
            for d in order:
                spread(s, lax.rem(y + d, ysize)).start()

    @pl.when(jumps)
    def _():
        wo[...] = times(wz[...], wq, True) + rg[...]
        for s in range(SUBS):
            hop(wo, wz, sem_bz, s, behind).start()

    pl.when(soon)(settle)

    sibling = {"core": 1 - core}
    wreal, wimag = w_ref[0, 0], w_ref[0, 1]

    def rows_of(d):
        j = lax.rem(y + d, ysize)
        return j, pl.ds(pl.multiple_of(j * chunk, chunk), chunk)

    def over_x(turn, d):
        _, rows = rows_of(d)
        land(other.at[rows, :], sem_a, turn, sibling)
        pair = xs[core, rows, :] + other[rows, :]
        for j in range(xsize):
            cut[j, rows, :] = jnp.concatenate(
                [pair[:, j * part : (j + 1) * part], pair[:, width + j * part : width + (j + 1) * part]], axis=1
            )
        for step in nearest_first(xsize):
            go(
                cut.at[lax.rem(x + step, xsize), rows, :],
                got.at[x, rows, :],
                sem_x,
                turn * xsize + step,
                along("x", x, step, xsize),
            )
        got[x, rows, :] = cut[x, rows, :]

    turns = [0] + order
    for turn, d in enumerate(turns):
        j, rows = rows_of(d)

        @pl.when(z < zsize - 1)
        def _():
            if d:
                for s in range(SUBS):
                    part_rows = pl.ds(pl.multiple_of(j * chunk + s * sub, sub), sub)
                    remote(
                        wb.at[part_rows, :], wb.at[part_rows, :], sem_w, j * SUBS + s, j * SUBS + s, {"y": j}
                    ).wait_recv()
                inflow = wb[rows, :]
            else:
                inflow = wz[...]
            y1[rows, :] = y1[rows, :] - times(inflow, wa1, False)
            y0[rows, :] = y0[rows, :] + times(inflow, wa0, False)

        for n, solved in enumerate((y0, y1)):
            real, imag = solved[rows, :width], solved[rows, width:]
            xs[n, rows, :width] = wreal * real - wimag * imag
            xs[n, rows, width:] = wreal * imag + wimag * real
        go(xs.at[1 - core, rows, :], other.at[rows, :], sem_a, turn, sibling)
        for done in {0: [0], 2: [1, 2]}.get(turn, [turn] if turn == len(turns) - 1 else []):
            over_x(done, turns[done])
    for turn, d in enumerate(turns):
        _, rows = rows_of(d)
        for step in nearest_first(xsize):
            j = back(x, step, xsize)
            land(got.at[j, rows, :], sem_x, turn * xsize + step, {"x": j})
    basis = got[0]
    for j in range(1, xsize):
        basis = basis + got[j]
    qall[core, x] = basis
    go(qall.at[core, x], qall.at[core, x], sem_q, 0, sibling)
    land(qall.at[1 - core, x], sem_q, 0, sibling)
    low_rows = pl.ds(pl.multiple_of(core * (vectors // 2), vectors // 2), vectors // 2)
    left_side = jnp.concatenate([qall[n, x, low_rows, :] for n in range(2)], axis=1)
    right_side = []
    for n in range(2):
        real, imag = qall[n, x, :, :part], qall[n, x, :, part:]
        right_side += [real + imag, imag - real]
    lh, ll = halves(left_side)
    rh, rl = halves(jnp.concatenate(right_side, axis=1))
    gram[...] = dot(lh, rh, True) + dot(ll, rh, True) + dot(lh, rl, True)
    plane = [(dx, dy) for dx in range(xsize) for dy in range(ysize) if dx or dy]
    plane.sort(key=lambda p: -min(p[0], xsize - p[0]) - min(p[1], ysize - p[1]))
    here = x * ysize + y
    for dx, dy in plane:
        slot = dx * ysize + dy
        jx, jy = lax.rem(x + dx, xsize), lax.rem(y + dy, ysize)
        go(lines(gram, jx * ysize + jy, line), g1.at[here], sem_1, slot, {"x": jx, "y": jy})
    g1[here] = lines(gram, here, line)[...]
    for step in nearest_first(xsize):
        go(qall.at[core, x], qall.at[core, x], sem_q, step, along("x", x, step, xsize))
    for dx, dy in plane:
        jx, jy = back(x, dx, xsize), back(y, dy, ysize)
        land(g1.at[jx * ysize + jy], sem_1, dx * ysize + dy, {"x": jx, "y": jy})
    value = g1[0]
    for j in range(1, xsize * ysize):
        value = value + g1[j]
    g3[z] = value
    for d in reversed(nearest_first(zsize)):
        go(g3.at[z], g3.at[z], sem_3, d, {"z": lax.rem(z + d, zsize)})
    for d in nearest_first(zsize):
        j = back(z, d, zsize)
        land(g3.at[j], sem_3, d, {"z": j})
    value = g3[0]
    for j in range(1, zsize):
        value = value + g3[j]
    place = (core * xsize + x) * ysize + y
    lines(h1, place, line)[...] = value
    others = [(dp, dy) for dp in range(poles) for dy in range(ysize) if dp or dy]
    others.sort(key=lambda p: -min(p[0], poles - p[0]) // 2 - min(p[1], ysize - p[1]))
    for dp, dy in others:
        device = pole_of(dp)[1] | along("y", y, dy, ysize)
        go(lines(h1, place, line), lines(h1, place, line), sem_5, dp * ysize + dy, device)
    for step in nearest_first(xsize):
        j = back(x, step, xsize)
        land(qall.at[core, j], sem_q, step, {"x": j})
        go(qall.at[core, j], qall.at[core, j], sem_q, xsize + step, sibling)
    for step in nearest_first(xsize):
        land(qall.at[1 - core, back(x, step, xsize)], sem_q, xsize + step, sibling)
    prepare(
        turned,
        jnp.concatenate([qall[n, j, :, :part] for n in range(2) for j in range(xsize)], axis=1),
        jnp.concatenate([qall[n, j, :, part:] for n in range(2) for j in range(xsize)], axis=1),
    )
    for dp, dy in others:
        p, device = pole_of(poles - dp)
        jy = back(y, dy, ysize)
        source = (lax.rem(p, 2) * xsize + p // 2) * ysize + jy
        land(lines(h1, source, line), sem_5, dp * ysize + dy, device | {"y": jy})

    whole = h1[...]
    frob = jnp.sqrt(jnp.sum(whole * whole))
    flip = whole.T
    scale = -0.25 / frob
    eye = (
        lax.broadcasted_iota(jnp.int32, (vectors, vectors), 0)
        == lax.broadcasted_iota(jnp.int32, (vectors, vectors), 1)
    )
    first = jnp.where(eye, 1.5, 0.0) + scale * (whole + flip)
    minus = -scale * (whole - flip)
    prepare(wn.at[0], first, minus)
    zs[0, :, :vectors] = first
    zs[0, :, vectors:] = minus

    def square(i):
        rows = pl.ds(i, tall)
        zs[1, rows, :] = times(zs[0, rows, :], wn.at[0], False)

    tiles(vectors, tall, square)
    prepare(
        wn.at[1],
        zs[1, :, :vectors] - 1.5 * zs[0, :, :vectors],
        zs[1, :, vectors:] - 1.5 * zs[0, :, vectors:],
    )
    size = jnp.sqrt(total_rows / frob)
    rows = pl.ds(pl.multiple_of(pole * own, own), own)
    mix = 1.5 * zs[0, rows, :] + times(zs[1, rows, :], wn.at[1], False)
    turned_rows = times(mix, turned, False) * size
    out_ref[0] = turned_rows[:, : 2 * width]
    out_ref[1] = turned_rows[:, 2 * width :]
    for copy in sent:
        copy.wait_send()
    if ysize > 2:
        for copy in (*onward(c_all, sem_c), *onward(d_all, sem_d)):
            copy.wait_send()
    handed_out(vk, vin, sem_v, ysize)
    handed_out(wk, win, sem_r, ysize - 1)
    for d in order:
        j, rows = rows_of(d)
        remote(eo.at[rows, :], e_all.at[y], sem_e, j, y, {"y": j}).wait_send()
    for s in range(SUBS):
        @pl.when(z < zsize - 1)
        def _():
            hop(vo, vz, sem_fz, s, ahead).wait_send()

        @pl.when(jnp.logical_or(last, jnp.logical_or(steps, jumps)))
        def _():
            hop(wo, wz, sem_bz, s, behind).wait_send()

        @pl.when(jumps)
        def _():
            hop(rj, wz, sem_far, s, two_back).wait_send()

        @pl.when(z < zsize - 1)
        def _():
            for d in order:
                spread(s, lax.rem(y + d, ysize)).wait_send()

    @pl.when(feeds)
    def _():
        remote(dg, dz, sem_one, 0, 0, ahead).wait_send()
        remote(rg, rz, sem_one, 1, 1, ahead).wait_send()


def shards(sizes, subspace, pivots, lower_blocks, upper_blocks, pole_weights):
    xsize, zsize, ysize = sizes
    vectors, width = subspace.shape[1], pivots.shape[-1]
    wide = 2 * width
    chunk = vectors // ysize
    poles = 2 * xsize
    part = width // xsize
    own = vectors // poles
    line = own // ysize
    total_rows = float(2 * width * ysize * zsize)

    def dma(count):
        return pltpu.SemaphoreType.DMA((2, count))

    def f32(*shape):
        return pltpu.VMEM(shape, F32)

    def prepared(*counts):
        return pltpu.VMEM((*counts, 2, wide, wide), BF16)

    anywhere = pl.BlockSpec(memory_space=pl.ANY)
    return pl.pallas_call(
        functools.partial(step_kernel, (xsize, zsize, ysize), total_rows),
        out_shape=jax.ShapeDtypeStruct((2, own, wide), F32),
        in_specs=[anywhere] * 4 + [pl.BlockSpec(memory_space=pltpu.SMEM)],
        out_specs=pl.BlockSpec(memory_space=pltpu.VMEM),
        scratch_shapes=[f32(*a.shape) for a in (subspace, pivots, lower_blocks, upper_blocks)]
        + [prepared()] * 4
        + [prepared(2)]
        + [prepared(ysize)] * 2
        + [prepared()] * 7
        + [f32(ysize, width, wide)] * 2
        + [f32(ysize, chunk, wide)] * 2
        + [f32(chunk, wide)] * 4
        + [f32(vectors, wide)] * 10
        + [f32(width, wide)] * 3
        + [f32(chunk, wide)] * 4
        + [f32(ysize, chunk, wide)] * 2
        + [
            f32(2, vectors, wide),
            f32(vectors, wide),
            f32(xsize, vectors, 2 * part),
            f32(xsize, vectors, 2 * part),
            f32(vectors // 2, vectors),
            f32(xsize * ysize, line, vectors),
            f32(zsize, line, vectors),
            f32(vectors, vectors),
            pltpu.VMEM((2, 2, 2 * vectors, 2 * vectors), BF16),
            f32(2, vectors, 2 * vectors),
            pltpu.VMEM((2, 2 * vectors, 2 * wide), BF16),
            f32(2, xsize, vectors, 2 * part),
            pltpu.SemaphoreType.DMA((4,)),
            dma(6),
        ]
        + [dma(ysize), dma(6)]
        + [dma(ysize)] * 3
        + [dma(ysize * SUBS)]
        + [dma(SUBS)] * 2
        + [dma(2), dma(SUBS)]
        + [
            dma(ysize),
            dma(ysize * xsize),
            dma(xsize * ysize),
            dma(zsize),
            dma(poles * ysize),
            dma(2 * xsize),
        ],
        compiler_params=pltpu.CompilerParams(
            collective_id=0, has_side_effects=True, vmem_limit_bytes=60 * 2**20
        ),
        name="step",
    )(subspace, pivots, lower_blocks, upper_blocks, pole_weights)


def build(mesh, sizes):
    xsize, zsize, ysize = sizes
    torus = Mesh(mesh.devices.reshape(xsize, 2, zsize, ysize), AXES)
    pole, rows = ("x", "core"), ("z", "y")
    return jax.shard_map(
        functools.partial(shards, sizes),
        mesh=torus,
        in_specs=(
            P(None, None, rows),
            P(pole, rows, None, None, None),
            P(pole, rows, None, None, None),
            P(pole, rows, None, None, None),
            P(pole, None),
        ),
        out_specs=P(None, pole, rows),
        check_vma=False,
    )


def solution(mesh):
    return build(mesh, (mesh.shape["pole"] // 2, mesh.shape["rows"] // 4, 4))
```
